32 devices in a mesh: groups: 2 (over x), ctx: 16 (over z, y, core).
Axes of the slice: x: 2, y: 2, z: 4, core: 2. Of those that a mesh axis runs over, the one named last changes fastest.
Arguments:
- features: bfloat16 [32768, 1024], P(('groups', 'ctx')), parts along dimension 0, may hold values from -6 to 6
- write_map: bfloat16 [32768, 128], P(('groups', 'ctx')), parts along dimension 0, may hold values from -6 to 6
- read_map: bfloat16 [32768, 128], P(('groups', 'ctx')), parts along dimension 0, may hold values from -3 to 3
- step_raw: float32 [32768, 16], P(('groups', 'ctx')), parts along dimension 0, may hold values from -3 to 3
- tokens: int32 [32768], P(('groups', 'ctx')), parts along dimension 0, may hold values from 0 to 4
- base_shift: float32 [5, 16], replicated, may hold values from -8 to -2
- decay_rate: float32 [16], replicated, may hold values from 0 to 2, as said below
- skip_gain: float32 [16], replicated, may hold values from 0.5 to 1.5
- cotangent: bfloat16 [32768, 1024], P(('groups', 'ctx')), parts along dimension 0, may hold values from -20 to 20
Outputs:
- layer_out: bfloat16 [32768, 1024], P(('groups', 'ctx')), parts along dimension 0
- grad_feature: bfloat16 [32768, 1024], P(('groups', 'ctx')), parts along dimension 0
- grad_write: bfloat16 [32768, 128], P(('groups', 'ctx')), parts along dimension 0
- grad_read: bfloat16 [32768, 128], P(('groups', 'ctx')), parts along dimension 0
- grad_step: float32 [32768, 16], P(('groups', 'ctx')), parts along dimension 0
- grad_skip: float32 [32], P('groups'), parts along dimension 0
The draws below stay inside these ranges and needn't reach their ends.
There are 2 independent parts, one for each index of `groups`. The reference program is written for one: setup_inputs(seed, part) draws one part's arguments, and reference() takes and returns one part's arrays. A program takes and returns all parts, laid end to end along the dimension named above; an argument that names none is the same for every part. Nothing has to cross between parts.
Inputs may be any that keep to these rules, and one draw needn't show every extreme that they name: `tokens`: 0, 1, 2, 3 stand for the bases A, C, G, T and 4 for an unknown base N. `decay_rate`: positive.
All inputs are finite; a program needn't handle non-finite values.
Results may differ from the reference program's by a relative error of at most 0.0015.
Values sent between devices are 32-bit elements; how exact they have to be, the bound alone decides.
A program may use at most 704 MiB of HBM per device.

```python
import math
import jax
import jax.numpy as jnp
from jax import lax

HEADS = 16
HEAD_DIM = 64
STATE_DIM = 128
SPAN = 256
ROWS = 1024
LENGTH = 16384


def head_kinds(key):
    key_count, key_order, key_slow, key_fast = jax.random.split(jax.random.fold_in(key, 11), 4)
    slow_count = jax.random.randint(key_count, (), max(1, HEADS // 4), HEADS - max(1, HEADS // 4) + 1)
    order = jax.random.permutation(key_order, HEADS)
    slow_heads = jnp.zeros((HEADS,), jnp.bool_).at[order].set(jnp.arange(HEADS) < slow_count)
    return (slow_heads, key_slow, key_fast)


def draw_decay_rate(key, part):
    slow_heads, key_slow, key_fast = head_kinds(key)
    slow_rate = 2.0 * jnp.exp(jax.random.uniform(key_slow, (HEADS,), jnp.float32, math.log(0.4), math.log(1.2))) / math.sqrt(LENGTH)
    fast_rate = jnp.exp(jax.random.uniform(key_fast, (HEADS,), jnp.float32, math.log(0.5), math.log(2.0)))
    return jnp.where(slow_heads, slow_rate, fast_rate).astype(jnp.float32)


def draw_base_shift(key, part):
    slow_heads, unused_slow, unused_fast = head_kinds(key)
    head_level = jnp.where(slow_heads, math.log(0.5 / math.sqrt(LENGTH)), math.log(0.03))
    jitter = jax.random.uniform(jax.random.fold_in(key, 23), (5, HEADS), jnp.float32, -0.5, 0.5)
    return (head_level[None, :] + jitter).astype(jnp.float32)


def draw_step_raw(key, part):
    key_noise, key_level = jax.random.split(jax.random.fold_in(key, 31))
    noise = jnp.clip(0.4 * jax.random.normal(key_noise, (LENGTH, HEADS), jnp.float32), -1.6, 1.6)
    offsets = jax.random.uniform(key_level, (LENGTH // ROWS, 1, HEADS), jnp.float32, -0.7, 0.7)
    spread_out = jnp.broadcast_to(offsets, (LENGTH // ROWS, ROWS, HEADS)).reshape(LENGTH, HEADS)
    return (noise + spread_out).astype(jnp.float32)


def draw_cotangent(key, part):
    rising = 1.0 + 2.0 * jnp.arange(LENGTH, dtype=jnp.float32) / (LENGTH - 1)
    raw_draw = jnp.clip(jax.random.normal(key, (LENGTH, HEADS * HEAD_DIM), jnp.float32), -4.0, 4.0)
    scaled = raw_draw * rising[:, None]
    return scaled.astype(jnp.bfloat16)


def touch_ends(values, key, least, high):
    dims = values.shape
    place = [jax.random.randint(jax.random.fold_in(key, axis), (), 0, dims[axis]) for axis in range(len(dims))]
    values = values.at[tuple(place)].set(least)
    longest = dims.index(max(dims))
    place[longest] = (place[longest] + 1) % dims[longest]
    return values.at[tuple(place)].set(high)


def steps_of(own_key, dims, cuts, low, largest):
    level, own = 1.0, jax.random.fold_in(own_key, 6)
    for position, parts in cuts:
        draws = jnp.exp(jax.random.uniform(jax.random.fold_in(own, position), (parts,), jnp.float32, low / len(cuts), largest / len(cuts)))
        level = level * jnp.repeat(draws, dims[position] // parts).reshape([-1 if axis == position else 1 for axis in range(len(dims))])
    return level


def scatter_about(rng, extent, scale, reach, cuts=(), kind=jnp.bfloat16):
    gain = steps_of(rng, extent, cuts, -0.22, 0.18) if cuts else 1.0
    values = jax.random.normal(rng, extent, jnp.float32) * scale * gain
    return jnp.minimum(jnp.maximum(values, -reach), reach).astype(kind)


def setup_inputs(seed: int = 0, part: int = 0) -> dict:
    keys = jax.random.split(jax.random.key(seed), 10)
    own_keys = jax.random.split(jax.random.fold_in(keys[9], part), 10)
    features = scatter_about(own_keys[0], (LENGTH, HEADS * HEAD_DIM), 1.0, 6.0, ((0, 16),))
    write_map = scatter_about(own_keys[1], (LENGTH, STATE_DIM), 1.0, 6.0, ((0, 16),))
    read_map = scatter_about(own_keys[2], (LENGTH, STATE_DIM), 0.5, 3.0, ((0, 16),))
    step_raw = draw_step_raw(jax.random.fold_in(jax.random.fold_in(keys[9], part), 71), part)
    tokens = touch_ends(jax.random.randint(own_keys[4], (LENGTH,), 0, 5), jax.random.fold_in(own_keys[4], 1), 0, 4).astype(jnp.int32)
    base_shift = draw_base_shift(jax.random.fold_in(keys[9], 71), part)
    decay_rate = draw_decay_rate(jax.random.fold_in(keys[9], 71), part)
    skip_gain = jnp.clip(jax.random.uniform(keys[7], (HEADS,), jnp.float32, 0.5, 1.5), 0.5, 1.5)
    cotangent = draw_cotangent(jax.random.fold_in(jax.random.fold_in(keys[9], part), 71), part)
    return dict(features=features, write_map=write_map, read_map=read_map, step_raw=step_raw, tokens=tokens, base_shift=base_shift, decay_rate=decay_rate, skip_gain=skip_gain, cotangent=cotangent)


PRECISE = lax.Precision.HIGHEST
MASKED = 10000.0

def step_rates(step_raw, base_shift, tokens):
    base_codes = jnp.arange(5, dtype=jnp.int32)
    onehot = (tokens[:, None] == base_codes[None, :]).astype(jnp.float32)
    paired = jnp.where(tokens < 4, 3 - tokens, tokens).astype(jnp.int32)
    onehot_rc = (paired[:, None] == base_codes[None, :]).astype(jnp.float32)
    step_fwd = jax.nn.softplus(step_raw + jnp.dot(onehot, base_shift, precision=PRECISE))
    step_rc = jax.nn.softplus(step_raw + jnp.dot(onehot_rc, jnp.flip(base_shift, 1), precision=PRECISE))
    return (step_fwd, step_rc)

def block_step(memory, pieces, rate_vec):
    values, writes, reads, step_sizes = pieces
    block_len = values.shape[0]
    running = jnp.cumsum(step_sizes * rate_vec[None, :], axis=0)
    running_heads = running.T
    spread = running_heads[:, :, None] - running_heads[:, None, :]
    causal = jnp.tril(jnp.ones((block_len, block_len), dtype=jnp.bool_))
    fade_matrix = jnp.exp(-jnp.where(causal[None], spread, MASKED))
    scores = jnp.dot(reads, writes.T, precision=PRECISE)
    weights = fade_matrix * scores[None] * step_sizes.T[:, None, :]
    inner = jnp.einsum('hts,shp->thp', weights, values, precision=PRECISE)
    carried = jnp.exp(-running)[:, :, None] * jnp.einsum('tn,hpn->thp', reads, memory, precision=PRECISE)
    tail_weight = jnp.exp(running - running[-1][None, :]) * step_sizes
    updated = jnp.exp(-running[-1])[:, None, None] * memory + jnp.einsum('sh,shp,sn->hpn', tail_weight, values, writes, precision=PRECISE)
    return (updated, inner + carried)

def ssd_scan(values, writes, reads, step_sizes, rate_vec):
    block_count = LENGTH // SPAN

    def blocked(array):
        return array.reshape((block_count, SPAN) + array.shape[1:])

    def advance(memory, pieces):
        return block_step(memory, pieces, rate_vec)
    initial = jnp.zeros((HEADS, HEAD_DIM, STATE_DIM), jnp.float32)
    unused_final, emitted = lax.scan(jax.checkpoint(advance), initial, (blocked(values), blocked(writes), blocked(reads), blocked(step_sizes)))
    return emitted.reshape(LENGTH, HEADS, HEAD_DIM)

def mixed_layer(values, writes, reads, step_raw, skip_gain, base_shift, decay_rate, tokens):
    step_fwd, step_rc = step_rates(step_raw, base_shift, tokens)
    y_fwd = ssd_scan(values, writes, reads, step_fwd, decay_rate)
    y_rc = jnp.flip(ssd_scan(jnp.flip(values, 0), jnp.flip(writes, 0), jnp.flip(reads, 0), jnp.flip(step_rc, 0), jnp.flip(decay_rate)), 0)
    return y_fwd + y_rc + (skip_gain + jnp.flip(skip_gain))[None, :, None] * values

def reference(features, write_map, read_map, step_raw, tokens, base_shift, decay_rate, skip_gain, cotangent):
    values = features.astype(jnp.float32).reshape(LENGTH, HEADS, HEAD_DIM)
    writes = write_map.astype(jnp.float32)
    reads = read_map.astype(jnp.float32)

    def layer_fn(value_in, write_in, read_in, raw_in, gain_in):
        return mixed_layer(value_in, write_in, read_in, raw_in, gain_in, base_shift, decay_rate, tokens)
    mixed, pullback = jax.vjp(layer_fn, values, writes, reads, step_raw, skip_gain)
    grads = pullback(cotangent.astype(jnp.float32).reshape(LENGTH, HEADS, HEAD_DIM))
    norm_scale = 1.0 / math.sqrt(LENGTH * HEAD_DIM)
    return (mixed.reshape(LENGTH, HEADS * HEAD_DIM).astype(jnp.bfloat16), grads[0].reshape(LENGTH, HEADS * HEAD_DIM).astype(jnp.bfloat16), grads[1].astype(jnp.bfloat16), grads[2].astype(jnp.bfloat16), grads[3], grads[4] * norm_scale)
```

```python
import functools
import math

import jax
import jax.numpy as jnp
from jax import lax
from jax.experimental import pallas as pl
from jax.experimental.pallas import tpu as pltpu
from jax.sharding import PartitionSpec as P

F32 = jnp.float32
BF16 = jnp.bfloat16
EXACT = lax.Precision.HIGHEST
SPAN = 128
CHUNK = 256
EXTRA = 8
LOG2E = 1.4426950408889634
MESH = pl.DeviceIdType.MESH

NN = (((1,), (0,)), ((), ()))
NT = (((1,), (1,)), ((), ()))
TN = (((0,), (0,)), ((), ()))


def mm(a, b, dims=NN):
    return lax.dot_general(a, b, dims, preferred_element_type=F32)


def exact(a, b, dims=NN):
    return lax.dot_general(a, b, dims, precision=EXACT, preferred_element_type=F32)


def pieces(v):
    high = v.astype(BF16)
    return high, (v - high.astype(F32)).astype(BF16)


def iota(shape, dim):
    return lax.broadcasted_iota(jnp.int32, shape, dim)


def log1p_unit(z):
    s = z / (z + 2.0)
    q = s * s
    acc = jnp.full_like(q, 1.0 / 19.0)
    for k in range(8, -1, -1):
        acc = acc * q + 1.0 / (2 * k + 1)
    return 2.0 * s * acc


def kernel(
    dims,
    x_ref, y_ref, b_ref, c_ref, raw_ref, tok_ref, base_ref, rate_ref, gain_ref,
    out_ref, gx_ref, gb_ref, gc_ref, gs_ref, gg_ref,
    rowp, cols, wcol, spread, bt2, ct2, bb2, cc2, gmat, dmat, gwide, fades, wts,
    loc, iy, ix, gca, gba, csum, rsum, psum,
    zone, zsib, ein, eout, ent,
    zs_send, zs_recv, ch_send, ch_recv, ot_send, ot_recv,
):
    heads, count, blocks, parts, messages = dims
    size = CHUNK // heads_per(dims)
    hp = heads_per(dims)
    rows = blocks * SPAN
    width = parts * CHUNK
    wide_rows = SPAN + EXTRA

    group = lax.axis_index("groups")
    me = lax.axis_index("ctx")
    core = lax.rem(me, 2)
    chip = me // 2
    chips = count // 2
    mine = 1 - core
    step = 2 * core - 1
    place = jnp.where(core == 1, chip, chips - 1 - chip)
    other_place = chips - 1 - place
    sibling = me + 1 - 2 * core
    after = jnp.clip(me + 2 * step, 0, count - 1)
    before = jnp.clip(me - 2 * step, 0, count - 1)
    first, last = place == 0, place == chips - 1

    barrier = pltpu.get_barrier_semaphore()
    pl.semaphore_signal(barrier, inc=1, device_id=(group, sibling), device_id_type=MESH)

    @pl.when(jnp.logical_not(last))
    def _():
        pl.semaphore_signal(barrier, inc=1, device_id=(group, after), device_id_type=MESH)

    @pl.when(jnp.logical_not(first))
    def _():
        pl.semaphore_signal(barrier, inc=1, device_id=(group, before), device_id_type=MESH)

    pl.semaphore_wait(barrier, 3 - first.astype(jnp.int32) - last.astype(jnp.int32))

    eye = (iota((heads, heads), 0) == iota((heads, heads), 1)).astype(F32)
    anti = (iota((heads, heads), 0) + iota((heads, heads), 1) == heads - 1).astype(F32)
    raw_t = exact(eye, raw_ref[...], NT)
    base_f = exact(eye, base_ref[...], NT)
    base_r = exact(anti, base_ref[...], NT)
    rate_f = exact(eye, jnp.broadcast_to(rate_ref[...], (8, heads)), NT)[:, :1]
    rate_r = exact(anti, jnp.broadcast_to(rate_ref[...], (8, heads)), NT)[:, :1]
    gain_row = gain_ref[...] + exact(jnp.broadcast_to(gain_ref[...], (8, heads)), anti)[:1]
    gain_col = exact(eye, jnp.broadcast_to(gain_row, (8, heads)), NT)[:, :1]

    def stacked(make):
        return jnp.concatenate([make(k) for k in range(blocks)], axis=0)

    def logits(k, base, pair):
        tok = tok_ref[k : k + 1, :]
        value = raw_t[:, k * SPAN : (k + 1) * SPAN]
        for code in range(5):
            col = pair[code]
            value = value + jnp.where(tok == code, base[:, col : col + 1], 0.0)
        return value

    vf = stacked(lambda k: logits(k, base_f, (0, 1, 2, 3, 4)))
    vr = stacked(lambda k: logits(k, base_r, (3, 2, 1, 0, 4)))

    def steps_of(v):
        z = jnp.exp(-jnp.abs(v))
        s = jnp.maximum(v, 0.0) + log1p_unit(z)
        inv = 1.0 / (1.0 + z)
        return s, jnp.where(v >= 0.0, inv, z * inv)

    sf, slope_f = steps_of(vf)
    sr, slope_r = steps_of(vr)
    rates_f = jnp.concatenate([rate_f] * blocks, axis=0)
    rates_r = jnp.concatenate([rate_r] * blocks, axis=0)
    t_pos = iota((SPAN, SPAN), 0)
    s_pos = iota((SPAN, SPAN), 1)
    ahead_sum = (t_pos <= s_pos).astype(F32)
    behind_sum = (t_pos >= s_pos).astype(F32)
    nf = exact(sf * (rates_f * -LOG2E), ahead_sum)
    nr = exact(sr * (rates_r * -LOG2E), behind_sum)
    end_f, end_r = nf[:, SPAN - 1 :], nr[:, :1]
    ef, er = jnp.exp2(nf), jnp.exp2(nr)
    wf, wr = jnp.exp2(end_f - nf) * sf, jnp.exp2(end_r - nr) * sr
    mf, mr = nf - jnp.log2(sf), nr - jnp.log2(sr)
    both_log = jnp.log2(sf + sr)

    lane = iota((SPAN, SPAN), 1)
    for k in range(blocks):
        at = slice(k * heads, (k + 1) * heads)
        four = jnp.concatenate([ef[at], er[at], wf[at], wr[at]] * 2, axis=0)
        turned = four.T
        high, low = pieces(turned)
        wcol[k] = jnp.where(lane < 4 * heads, high.astype(F32), low.astype(F32)).astype(BF16)
        order = []
        for c in range(parts):
            sub = slice(k * heads + c * hp, k * heads + (c + 1) * hp)
            order += [nf[sub], nr[sub]]
            rowp[k * parts + c] = jnp.concatenate([mf[sub], mr[sub], both_log[sub], both_log[sub]], axis=0)
        pad = [jnp.zeros((SPAN - 2 * heads, SPAN), F32)]
        turned = jnp.concatenate(order + pad, axis=0).T
        for c in range(parts):
            cols[k * parts + c, :, 0 : 2 * hp] = turned[:, 2 * hp * c : 2 * hp * (c + 1)]
        here = slice(k * SPAN, (k + 1) * SPAN)
        bk, ck = b_ref[here, :], c_ref[here, :]
        bkt = bk.astype(F32).T.astype(BF16)
        ckt = ck.astype(F32).T.astype(BF16)
        bt2[k] = jnp.concatenate([bkt, bkt], axis=1)
        ct2[k] = jnp.concatenate([ckt, ckt], axis=1)
        bb2[k] = jnp.concatenate([bk, bk], axis=1)
        cc2[k] = jnp.concatenate([ck, ck], axis=1)
        gmat[k] = mm(ck, bk, NT)
        dmat[k] = jnp.zeros((SPAN, SPAN), F32)
        gca[k] = jnp.zeros((SPAN, SPAN), F32)
        gba[k] = jnp.zeros((SPAN, SPAN), F32)

    for c in range(parts):
        r = iota((SPAN, 4 * CHUNK), 0)
        j = iota((SPAN, 4 * CHUNK), 1)
        rr = lax.rem(r, 4 * heads)
        hit = (rr // heads == j // CHUNK) & (lax.rem(rr, heads) == c * hp + lax.rem(j, CHUNK) // size)
        spread[c] = hit.astype(F32).astype(BF16)
        hw = iota((heads, CHUNK), 0) == c * hp + iota((heads, CHUNK), 1) // size
        gwide[c] = exact(jnp.broadcast_to(gain_row, (8, heads)), hw.astype(F32))

    def zone_copy(m):
        return pltpu.make_async_remote_copy(
            src_ref=zone.at[1 - mine, m], dst_ref=zsib.at[m],
            send_sem=zs_send.at[m], recv_sem=zs_recv.at[m],
            device_id=(group, sibling), device_id_type=MESH,
        )

    def chain_copy(m):
        return pltpu.make_async_remote_copy(
            src_ref=eout.at[m], dst_ref=ein.at[m],
            send_sem=ch_send.at[m], recv_sem=ch_recv.at[m],
            device_id=(group, after), device_id_type=MESH,
        )

    def other_copy(m):
        return pltpu.make_async_remote_copy(
            src_ref=ein.at[m], dst_ref=ent.at[mine, m],
            send_sem=ot_send.at[m], recv_sem=ot_recv.at[m],
            device_id=(group, sibling), device_id_type=MESH,
        )

    top, fine = 2.0 ** grid_bits(dims), 2.0 ** (grid_bits(dims) + 21)
    finest = 2.0 ** (grid_bits(dims) + 42)
    one_row = iota((EXTRA, CHUNK), 0)

    @pl.loop(0, parts)
    def _(c):
        at_w = pl.ds(pl.multiple_of(c * CHUNK, CHUNK), CHUNK)

        def products(k, carry):
            state, adj, wt_f, wt_r, dot_xy = carry
            at_r = pl.ds(pl.multiple_of(k * SPAN, SPAN), SPAN)
            x = x_ref[at_r, at_w].astype(F32)
            y = y_ref[at_r, at_w].astype(F32)
            wides = mm(wcol[k], spread[c])
            ef_w, er_w = wides[:, :CHUNK], wides[:, CHUNK : 2 * CHUNK]
            wf_w, wr_w = wides[:, 2 * CHUNK : 3 * CHUNK], wides[:, 3 * CHUNK :]
            xf = jnp.concatenate(pieces(wf_w * x), axis=0)
            xr = jnp.concatenate(pieces(wr_w * x), axis=0)
            yf = jnp.concatenate(pieces(ef_w * y), axis=0)
            yr = jnp.concatenate(pieces(er_w * y), axis=0)
            fade_f, fade_r = ef_w[SPAN - 1 :], er_w[:1]
            fades[k, 0:1, at_w] = fade_f
            fades[k, 1:2, at_w] = fade_r
            wts[k, 0:1, at_w] = wt_f
            wts[k, 1:2, at_w] = wt_r
            loc[0, k, :, at_w] = state
            loc[1, k, :, at_w] = adj
            state = fade_f * state + mm(bt2[k], xf)
            adj = fade_r * adj + mm(ct2[k], yr)
            loc[2, k, :, at_w] = mm(ct2[k], yf)
            loc[3, k, :, at_w] = mm(bt2[k], xr)
            return state, adj, wt_f * fade_f, wt_r * fade_r, dot_xy + jnp.sum((x * y).reshape(SPAN // 8, 8, CHUNK), axis=0)

        zero = jnp.zeros((SPAN, CHUNK), F32)
        ones = jnp.ones((1, CHUNK), F32)
        state, adj, g_f, g_r, dot_xy = lax.fori_loop(
            0, blocks, products, (zero, zero, ones, ones, jnp.zeros((8, CHUNK), F32))
        )

        def back(i, carry):
            adj_f, state_r, wt_f, wt_r = carry
            k = blocks - 1 - i
            fade_f, fade_r = fades[k, 0:1, at_w], fades[k, 1:2, at_w]
            part_f, part_r = loc[2, k, :, at_w], loc[3, k, :, at_w]
            loc[2, k, :, at_w] = adj_f
            loc[3, k, :, at_w] = state_r
            wts[k, 2:3, at_w] = wt_f
            wts[k, 3:4, at_w] = wt_r
            return fade_f * adj_f + part_f, fade_r * state_r + part_r, wt_f * fade_f, wt_r * fade_r

        adj_f, state_r, _, _ = lax.fori_loop(0, blocks, back, (zero, zero, ones, ones))

        dot_row = jnp.sum(dot_xy, axis=0, keepdims=True)
        coarse = jnp.round(dot_row * top) * (1.0 / top)
        rest = dot_row - coarse
        middle = jnp.round(rest * fine) * (1.0 / fine)
        small = jnp.round((rest - middle) * finest) * (1.0 / finest)

        def put(flow, comp, value, g):
            m = c * 2 + comp
            zone[flow, m, 0:SPAN, :] = value
            zone[flow, m, SPAN:, :] = jnp.where(
                one_row == 0, g,
                jnp.where(one_row == 1, coarse, jnp.where(one_row == 2, middle, jnp.where(one_row == 3, small, 0.0))),
            )

        put(0, 0, state, g_f)
        put(0, 1, adj, g_r)
        put(1, 0, adj_f, g_f)
        put(1, 1, state_r, g_r)
        zone_copy(2 * c).start()
        zone_copy(2 * c + 1).start()

    is_state = iota((wide_rows, CHUNK), 0) < SPAN

    def chain_step(m):
        @pl.when(first)
        def _():
            ein[m] = jnp.zeros((wide_rows, CHUNK), F32)

        zone_copy(m).wait_recv()

        @pl.when(jnp.logical_not(first))
        def _():
            chain_copy(m).wait_recv()
            other_copy(m).start()

        near, own = zsib[m], zone[mine, m]
        g_near, g_own = near[SPAN : SPAN + 1], own[SPAN : SPAN + 1]
        entry = near + jnp.where(is_state, g_near, 1.0) * ein[m]
        ent[mine, m] = entry

        @pl.when(jnp.logical_not(last))
        def _():
            eout[m] = own + jnp.where(is_state, g_own, 1.0) * entry
            chain_copy(m).start()

    low = t_pos > s_pos
    diag = t_pos == s_pos
    half = iota((SPAN, SPAN), 1) < size

    def inner(i):
        c, k = i // blocks, lax.rem(i, blocks)
        at_r = pl.ds(pl.multiple_of(k * SPAN, SPAN), SPAN)
        g = gmat[k]
        col = cols[k * parts + c]
        row = rowp[k * parts + c]
        d_sum = dmat[k]
        lows, diags, lefts = [], [], []
        for p in range(CHUNK // SPAN):
            at_w = pl.ds(pl.multiple_of(c * CHUNK + p * SPAN, SPAN), SPAN)
            x, y = x_ref[at_r, at_w], y_ref[at_r, at_w]
            xs, ys, ws = [], [], []
            for q in range(SPAN // size):
                h = p * (SPAN // size) + q
                keep = half if q == 0 else jnp.logical_not(half)
                xm = jnp.where(keep, x.astype(F32), 0.0).astype(BF16)
                ym = jnp.where(keep, y.astype(F32), 0.0).astype(BF16)
                fall = col[:, h : h + 1] - row[h : h + 1]
                rise = col[:, hp + h : hp + h + 1] - row[hp + h : hp + h + 1]
                mid = row[2 * hp + h : 2 * hp + h + 1]
                w = jnp.exp2(jnp.where(low, fall, jnp.where(diag, mid, rise)))
                cross = mm(ym, x, NT)
                wg = w * g
                d_sum = d_sum + cross * w
                pull = jnp.where(low, cross * wg, 0.0)
                lows.append(jnp.sum(pull, axis=0, keepdims=True))
                lefts.append(jnp.sum(pull, axis=1, keepdims=True))
                diags.append(jnp.sum(jnp.where(diag, cross, 0.0), axis=0, keepdims=True))
                ws += list(pieces(wg))
                xs += [xm, xm]
                ys += [ym, ym]
            iy[k * parts + c, :, p * SPAN : (p + 1) * SPAN] = mm(
                jnp.concatenate(ws, axis=1), jnp.concatenate(xs, axis=0)
            )
            ix[k * parts + c, :, p * SPAN : (p + 1) * SPAN] = mm(
                jnp.concatenate(ws, axis=0), jnp.concatenate(ys, axis=0), TN
            )
        dmat[k] = d_sum
        csum[k * parts + c] = jnp.concatenate(lows + diags, axis=0)
        acc = jnp.zeros((SPAN, SPAN), F32)
        for h, value in enumerate(lefts):
            acc = jnp.where(lane == h, value, acc)
        rsum[k * parts + c] = acc

    reach, gap, pieces_n = 6, 3, blocks * parts

    @pl.loop(0, pieces_n)
    def _(i):
        inner(i)
        late = i - reach * place
        m = late // gap

        @pl.when((late >= 0) & (m < messages) & (lax.rem(late, gap) == 0))
        def _():
            chain_step(m)

    @pl.loop(0, messages)
    def _(m):
        @pl.when(reach * place + gap * m >= pieces_n)
        def _():
            chain_step(m)

    head_row = iota((8, CHUNK), 0) == iota((8, CHUNK), 1) // size
    pick = head_row.astype(F32)
    pick2 = jnp.concatenate([pick, pick], axis=1).astype(BF16)

    @pl.loop(0, parts)
    def _(c):
        at_w = pl.ds(pl.multiple_of(c * CHUNK, CHUNK), CHUNK)
        for comp in range(2):
            m = 2 * c + comp

            @pl.when(other_place == 0)
            def _():
                ent[1 - mine, m] = jnp.zeros((wide_rows, CHUNK), F32)

            @pl.when(other_place > 0)
            def _():
                other_copy(m).wait_recv()

        @pl.loop(0, blocks)
        def _(k):
            at_r = pl.ds(pl.multiple_of(k * SPAN, SPAN), SPAN)
            at = k * parts + c
            x = x_ref[at_r, at_w].astype(F32)
            y = y_ref[at_r, at_w].astype(F32)
            wides = mm(wcol[k], spread[c])
            ef_w, er_w = wides[:, :CHUNK], wides[:, CHUNK : 2 * CHUNK]
            wf_w, wr_w = wides[:, 2 * CHUNK : 3 * CHUNK], wides[:, 3 * CHUNK :]

            def entered(slot, row, flow, comp):
                return pieces(
                    loc[slot, k, :, at_w] + wts[k, row : row + 1, at_w] * ent[flow, 2 * c + comp, 0:SPAN, :]
                )

            sf_h, sf_l = entered(0, 0, 0, 0)
            ar_h, ar_l = entered(1, 1, 0, 1)
            af_h, af_l = entered(2, 2, 1, 0)
            sr_h, sr_l = entered(3, 3, 1, 1)
            cat = lambda *v: jnp.concatenate(v, axis=0)
            v_f = mm(cc2[k], cat(sf_h, sf_l))
            v_r = mm(cc2[k], cat(sr_h, sr_l))
            u_f = mm(bb2[k], cat(af_h, af_l))
            u_r = mm(bb2[k], cat(ar_h, ar_l))
            gain = gwide[c, 0:1]
            yf, yr, xf, xr = ef_w * y, er_w * y, wf_w * x, wr_w * x
            mixed = iy[at] + ef_w * v_f + er_w * v_r + gain * x
            grad_x = ix[at] + wf_w * u_f + wr_w * u_r + gain * y
            out_ref[at_r, at_w] = mixed.astype(BF16)
            gx_ref[at_r, at_w] = grad_x.astype(BF16)

            def joined(a, ah_al, b, bh_bl):
                a_h, a_l = pieces(a)
                b_h, b_l = pieces(b)
                left = jnp.concatenate([a_h, a_h, a_l, b_h, b_h, b_l], axis=1)
                right = jnp.concatenate(
                    [ah_al[0], ah_al[1], ah_al[0], bh_bl[0], bh_bl[1], bh_bl[0]], axis=1
                )
                return mm(left, right, NT)

            gca[k] += joined(yf, (sf_h, sf_l), yr, (sr_h, sr_l))
            gba[k] += joined(xf, (af_h, af_l), xr, (ar_h, ar_l))

            def narrow(v):
                return mm(pick2, jnp.concatenate(pieces(v), axis=1), NT)

            psum[at, 0:8] = narrow(yf * v_f)
            psum[at, 8:16] = narrow(xf * u_f)
            psum[at, 16:24] = narrow(y * mixed)
            psum[at, 24:32] = narrow(x * grad_x)

    def gathered(make):
        out = []
        for k in range(blocks):
            for c in range(parts):
                out.append(make(k, c))
        return jnp.concatenate(out, axis=0)

    def sums(first_row):
        return gathered(lambda k, c: psum[k * parts + c, first_row : first_row + hp])

    row_low = gathered(lambda k, c: rsum[k * parts + c].T[0:hp])
    col_low = gathered(lambda k, c: csum[k * parts + c, 0:hp])
    both = gathered(lambda k, c: csum[k * parts + c, hp : 2 * hp])
    center = stacked(
        lambda k: jnp.broadcast_to(
            jnp.sum(jnp.where(diag, gmat[k], 0.0), axis=0, keepdims=True), (heads, SPAN)
        )
    )
    ends_f, ends_r, gains = [], [], []
    for c in range(parts):
        for flow, comp, opp_flow, opp_comp, into in ((0, 0, 1, 0, ends_f), (1, 1, 0, 1, ends_r)):
            own = zone[flow, 2 * c + comp]
            leaving = own[:SPAN] + own[SPAN : SPAN + 1] * ent[flow, 2 * c + comp, 0:SPAN, :]
            held = exact(pick, leaving * ent[opp_flow, 2 * c + opp_comp, 0:SPAN, :], NT)
            into.append(jnp.sum(held, axis=1, keepdims=True)[0:hp])
        total = ent[0, 2 * c, SPAN:, :] + (zone[0, 2 * c, SPAN:, :] + ent[1, 2 * c, SPAN:, :])
        row = total[1:2] + (total[2:3] + total[3:4])
        spots = (iota((CHUNK, heads), 1) == c * hp + iota((CHUNK, heads), 0) // size).astype(F32)
        gains.append(exact(jnp.broadcast_to(row, (8, CHUNK)), spots))
    gain_sum = sum(gains)
    gg_ref[...] = (gain_sum + exact(gain_sum, anti)) * (1.0 / math.sqrt(rows * count * size))

    gain_all = jnp.concatenate([gain_col] * blocks, axis=0)
    own_terms = (gain_all + (sf + sr) * center) * both
    row_f = row_low + sums(0)
    col_f = col_low + sums(8)
    row_r = sums(16) - own_terms - row_f
    col_r = sums(24) - own_terms - col_f
    mid = center * both
    diff_f, diff_r = col_f - row_f, col_r - row_r
    tail_f = exact(diff_f, behind_sum)
    head_r = exact(diff_r, ahead_sum)
    later, earlier = [None] * blocks, [None] * blocks
    run = -jnp.concatenate(ends_f, axis=0)
    for k in range(blocks - 1, -1, -1):
        at = slice(k * heads, (k + 1) * heads)
        later[k] = run
        run = run + tail_f[at, :1]
    run = -jnp.concatenate(ends_r, axis=0)
    for k in range(blocks):
        at = slice(k * heads, (k + 1) * heads)
        earlier[k] = run
        run = run + head_r[at, SPAN - 1 :]
    drop_f = tail_f + jnp.concatenate(later, axis=0)
    drop_r = head_r + jnp.concatenate(earlier, axis=0)
    d_f = col_f / sf + mid + rates_f * drop_f
    d_r = col_r / sr + mid + rates_r * drop_r
    grad_s = d_f * slope_f + d_r * slope_r
    for k in range(blocks):
        here = slice(k * SPAN, (k + 1) * SPAN)
        gs_ref[here, :] = exact(grad_s[k * heads : (k + 1) * heads], eye, TN)
        d_h, d_l = pieces(dmat[k])
        gc_ref[here, :] = (gca[k] + mm(jnp.concatenate([d_h, d_l], axis=1), jnp.concatenate([b_ref[here, :]] * 2, axis=0))).astype(BF16)
        gb_ref[here, :] = (gba[k] + mm(jnp.concatenate([d_h, d_l], axis=0), jnp.concatenate([c_ref[here, :]] * 2, axis=0), TN)).astype(BF16)

    @pl.loop(0, messages)
    def _(m):
        zone_copy(m).wait_send()

        @pl.when(jnp.logical_not(first))
        def _():
            other_copy(m).wait_send()

        @pl.when(jnp.logical_not(last))
        def _():
            chain_copy(m).wait_send()


def heads_per(dims):
    return dims[0] // dims[3]


def grid_bits(dims):
    limit = 120 * dims[2] * SPAN * dims[1]
    return 23 - math.ceil(math.log2(limit))


def per_device(
    features, write_map, read_map, step_raw, tokens, base_shift, decay_rate, skip_gain, cotangent
):
    rows, width = features.shape
    state = write_map.shape[1]
    heads = decay_rate.shape[0]
    count = lax.axis_size("ctx")
    blocks, parts = rows // SPAN, width // CHUNK
    messages = 2 * parts
    dims = (heads, count, blocks, parts, messages)
    hp = heads // parts
    cells = blocks * parts
    wide_rows = SPAN + EXTRA
    vmem = pl.BlockSpec(memory_space=pltpu.VMEM)
    shape = jax.ShapeDtypeStruct
    outs = pl.pallas_call(
        functools.partial(kernel, dims),
        out_shape=(
            shape((rows, width), BF16),
            shape((rows, width), BF16),
            shape((rows, state), BF16),
            shape((rows, state), BF16),
            shape((rows, heads), F32),
            shape((8, heads), F32),
        ),
        in_specs=[vmem] * 9,
        out_specs=(vmem,) * 6,
        scratch_shapes=[
            pltpu.VMEM((cells, 4 * hp, SPAN), F32),
            pltpu.VMEM((cells, SPAN, SPAN), F32),
            pltpu.VMEM((blocks, SPAN, SPAN), BF16),
            pltpu.VMEM((parts, SPAN, 4 * CHUNK), BF16),
            pltpu.VMEM((blocks, SPAN, 2 * SPAN), BF16),
            pltpu.VMEM((blocks, SPAN, 2 * SPAN), BF16),
            pltpu.VMEM((blocks, SPAN, 2 * SPAN), BF16),
            pltpu.VMEM((blocks, SPAN, 2 * SPAN), BF16),
            pltpu.VMEM((blocks, SPAN, SPAN), F32),
            pltpu.VMEM((blocks, SPAN, SPAN), F32),
            pltpu.VMEM((parts, 8, CHUNK), F32),
            pltpu.VMEM((blocks, 8, width), F32),
            pltpu.VMEM((blocks, 8, width), F32),
            pltpu.VMEM((4, blocks, SPAN, width), F32),
            pltpu.VMEM((cells, SPAN, CHUNK), F32),
            pltpu.VMEM((cells, SPAN, CHUNK), F32),
            pltpu.VMEM((blocks, SPAN, SPAN), F32),
            pltpu.VMEM((blocks, SPAN, SPAN), F32),
            pltpu.VMEM((cells, 2 * hp, SPAN), F32),
            pltpu.VMEM((cells, SPAN, SPAN), F32),
            pltpu.VMEM((cells, 32, SPAN), F32),
            pltpu.VMEM((2, messages, wide_rows, CHUNK), F32),
            pltpu.VMEM((messages, wide_rows, CHUNK), F32),
            pltpu.VMEM((messages, wide_rows, CHUNK), F32),
            pltpu.VMEM((messages, wide_rows, CHUNK), F32),
            pltpu.VMEM((2, messages, wide_rows, CHUNK), F32),
        ]
        + [pltpu.SemaphoreType.DMA((messages,))] * 6,
        compiler_params=pltpu.CompilerParams(
            collective_id=0, has_side_effects=True, vmem_limit_bytes=60 * 1024 * 1024
        ),
    )(
        features, cotangent, write_map, read_map, step_raw, tokens.reshape(blocks, SPAN),
        base_shift, decay_rate.reshape(1, heads), skip_gain.reshape(1, heads),
    )
    mixed, grad_x, grad_b, grad_c, grad_s, gains = outs
    return mixed, grad_x, grad_b, grad_c, grad_s, gains[0]


def solution(mesh):
    split = P(("groups", "ctx"), None)
    return jax.shard_map(
        per_device,
        mesh=mesh,
        in_specs=(split, split, split, split, P(("groups", "ctx")), P(), P(), P(), split),
        out_specs=(split, split, split, split, split, P("groups")),
        check_vma=False,
    )
```

```python
import functools
import math

import jax
import jax.numpy as jnp
from jax import lax
from jax.experimental import pallas as pl
from jax.experimental.pallas import tpu as pltpu
from jax.sharding import PartitionSpec as P

F32 = jnp.float32
BF16 = jnp.bfloat16
EXACT = lax.Precision.HIGHEST
SPAN = 128
CHUNK = 256
EXTRA = 8
LOG2E = 1.4426950408889634
MESH = pl.DeviceIdType.MESH

NN = (((1,), (0,)), ((), ()))
NT = (((1,), (1,)), ((), ()))
TN = (((0,), (0,)), ((), ()))


def mm(a, b, dims=NN):
    return lax.dot_general(a, b, dims, preferred_element_type=F32)


def exact(a, b, dims=NN):
    return lax.dot_general(a, b, dims, precision=EXACT, preferred_element_type=F32)


def pieces(v):
    high = v.astype(BF16)
    return high, (v - high.astype(F32)).astype(BF16)


def iota(shape, dim):
    return lax.broadcasted_iota(jnp.int32, shape, dim)


def log1p_unit(z):
    s = z / (z + 2.0)
    q = s * s
    acc = jnp.full_like(q, 1.0 / 19.0)
    for k in range(8, -1, -1):
        acc = acc * q + 1.0 / (2 * k + 1)
    return 2.0 * s * acc


def kernel(
    dims,
    x_ref, y_ref, b_ref, c_ref, raw_ref, tok_ref, base_ref, rate_ref, gain_ref,
    out_ref, gx_ref, gb_ref, gc_ref, gs_ref, gg_ref,
    rowp, cols, wcol, spread, bt2, ct2, bb2, cc2, gmat, dmat, gwide, fades, wts, whole, turn,
    loc, iy, ix, gca, gba, csum, rsum, psum,
    zone, zsib, ein, eout, ent,
    zs_send, zs_recv, ch_send, ch_recv, ot_send, ot_recv,
):
    heads, count, blocks, parts, messages = dims
    size = CHUNK // heads_per(dims)
    hp = heads_per(dims)
    rows = blocks * SPAN
    width = parts * CHUNK
    wide_rows = SPAN + EXTRA

    group = lax.axis_index("groups")
    me = lax.axis_index("ctx")
    core = lax.rem(me, 2)
    chip = me // 2
    chips = count // 2
    mine = 1 - core
    step = 2 * core - 1
    place = jnp.where(core == 1, chip, chips - 1 - chip)
    other_place = chips - 1 - place
    sibling = me + 1 - 2 * core
    after = jnp.clip(me + 2 * step, 0, count - 1)
    before = jnp.clip(me - 2 * step, 0, count - 1)
    first, last = place == 0, place == chips - 1

    barrier = pltpu.get_barrier_semaphore()
    pl.semaphore_signal(barrier, inc=1, device_id=(group, sibling), device_id_type=MESH)

    @pl.when(jnp.logical_not(last))
    def _():
        pl.semaphore_signal(barrier, inc=1, device_id=(group, after), device_id_type=MESH)

    @pl.when(jnp.logical_not(first))
    def _():
        pl.semaphore_signal(barrier, inc=1, device_id=(group, before), device_id_type=MESH)

    pl.semaphore_wait(barrier, 3 - first.astype(jnp.int32) - last.astype(jnp.int32))

    eye = (iota((heads, heads), 0) == iota((heads, heads), 1)).astype(F32)
    anti = (iota((heads, heads), 0) + iota((heads, heads), 1) == heads - 1).astype(F32)
    raw_t = raw_ref[...]
    base_f = exact(eye, base_ref[...], NT)
    base_r = exact(anti, base_ref[...], NT)
    rate_f = exact(eye, jnp.broadcast_to(rate_ref[...], (8, heads)), NT)[:, :1]
    rate_r = exact(anti, jnp.broadcast_to(rate_ref[...], (8, heads)), NT)[:, :1]
    gain_row = gain_ref[...] + exact(jnp.broadcast_to(gain_ref[...], (8, heads)), anti)[:1]
    gain_col = exact(eye, jnp.broadcast_to(gain_row, (8, heads)), NT)[:, :1]

    def stacked(make):
        return jnp.concatenate([make(k) for k in range(blocks)], axis=0)

    def logits(k, base, pair):
        tok = tok_ref[k : k + 1, :]
        value = raw_t[:, k * SPAN : (k + 1) * SPAN]
        for code in range(5):
            col = pair[code]
            value = value + jnp.where(tok == code, base[:, col : col + 1], 0.0)
        return value

    vf = stacked(lambda k: logits(k, base_f, (0, 1, 2, 3, 4)))
    vr = stacked(lambda k: logits(k, base_r, (3, 2, 1, 0, 4)))

    def steps_of(v):
        z = jnp.exp(-jnp.abs(v))
        s = jnp.maximum(v, 0.0) + log1p_unit(z)
        inv = 1.0 / (1.0 + z)
        return s, jnp.where(v >= 0.0, inv, z * inv)

    sf, slope_f = steps_of(vf)
    sr, slope_r = steps_of(vr)
    rates_f = jnp.concatenate([rate_f] * blocks, axis=0)
    rates_r = jnp.concatenate([rate_r] * blocks, axis=0)
    t_pos = iota((SPAN, SPAN), 0)
    s_pos = iota((SPAN, SPAN), 1)
    ahead_sum = (t_pos <= s_pos).astype(F32)
    behind_sum = (t_pos >= s_pos).astype(F32)
    nf = exact(sf * (rates_f * -LOG2E), ahead_sum)
    nr = exact(sr * (rates_r * -LOG2E), behind_sum)
    end_f, end_r = nf[:, SPAN - 1 :], nr[:, :1]
    ef, er = jnp.exp2(nf), jnp.exp2(nr)
    wf, wr = jnp.exp2(end_f - nf) * sf, jnp.exp2(end_r - nr) * sr
    mf, mr = nf - jnp.log2(sf), nr - jnp.log2(sr)
    both_log = jnp.log2(sf + sr)

    lane = iota((SPAN, SPAN), 1)
    ends_at_last, ends_at_first = [], []
    for k in range(blocks):
        at = slice(k * heads, (k + 1) * heads)
        four = jnp.concatenate([ef[at], wr[at], er[at], wf[at]] * 2, axis=0)
        turned = four.T
        high, low = pieces(turned)
        joint = jnp.where(lane < 4 * heads, high.astype(F32), low.astype(F32))
        wcol[k] = joint.astype(BF16)
        ends_at_last.append(joint[SPAN - 1 :])
        ends_at_first.append(joint[:1])
        order = []
        for c in range(parts):
            sub = slice(k * heads + c * hp, k * heads + (c + 1) * hp)
            order += [nf[sub], nr[sub]]
            rowp[k * parts + c] = jnp.concatenate([mf[sub], mr[sub], both_log[sub], both_log[sub]], axis=0)
        pad = [jnp.zeros((SPAN - 2 * heads, SPAN), F32)]
        turned = jnp.concatenate(order + pad, axis=0).T
        for c in range(parts):
            cols[k * parts + c, :, 0 : 2 * hp] = turned[:, 2 * hp * c : 2 * hp * (c + 1)]
        here = slice(k * SPAN, (k + 1) * SPAN)
        bk, ck = b_ref[here, :], c_ref[here, :]
        bkt = bk.astype(F32).T.astype(BF16)
        ckt = ck.astype(F32).T.astype(BF16)
        bt2[k] = jnp.concatenate([bkt, bkt], axis=1)
        ct2[k] = jnp.concatenate([ckt, ckt], axis=1)
        bb2[k] = jnp.concatenate([bk, bk], axis=1)
        cc2[k] = jnp.concatenate([ck, ck], axis=1)
        gmat[k] = mm(ck, bk, NT)
        dmat[k] = jnp.zeros((SPAN, SPAN), F32)
        gca[k] = jnp.zeros((SPAN, SPAN), F32)
        gba[k] = jnp.zeros((SPAN, SPAN), F32)
        rsum[k] = jnp.zeros((SPAN, SPAN), F32)

    for c in range(parts):
        r = iota((SPAN, 4 * CHUNK), 0)
        j = iota((SPAN, 4 * CHUNK), 1)
        rr = lax.rem(r, 4 * heads)
        hit = (rr // heads == j // CHUNK) & (lax.rem(rr, heads) == c * hp + lax.rem(j, CHUNK) // size)
        spread[c] = hit.astype(F32).astype(BF16)
        hw = iota((heads, CHUNK), 0) == c * hp + iota((heads, CHUNK), 1) // size
        gwide[c] = exact(jnp.broadcast_to(gain_row, (8, heads)), hw.astype(F32))
        fade_f = mm(jnp.concatenate(ends_at_last, axis=0).astype(BF16), spread[c, :, :CHUNK])
        fade_r = mm(jnp.concatenate(ends_at_first, axis=0).astype(BF16), spread[c, :, 2 * CHUNK : 3 * CHUNK])
        fades[c, 0], fades[c, 1] = fade_f, fade_r
        for row, fade in ((0, fade_f), (1, fade_r)):
            run = jnp.ones((1, CHUNK), F32)
            for k in range(blocks):
                wts[c, row, k : k + 1, :] = run
                run = run * fade[k : k + 1]
            whole[c, row] = jnp.broadcast_to(run, (EXTRA, CHUNK))
            run = jnp.ones((1, CHUNK), F32)
            for k in range(blocks - 1, -1, -1):
                wts[c, row + 2, k : k + 1, :] = run
                run = run * fade[k : k + 1]

    def zone_copy(m):
        return pltpu.make_async_remote_copy(
            src_ref=zone.at[1 - mine, m], dst_ref=zsib.at[m],
            send_sem=zs_send.at[m], recv_sem=zs_recv.at[m],
            device_id=(group, sibling), device_id_type=MESH,
        )

    def chain_copy(m):
        return pltpu.make_async_remote_copy(
            src_ref=eout.at[m], dst_ref=ein.at[m],
            send_sem=ch_send.at[m], recv_sem=ch_recv.at[m],
            device_id=(group, after), device_id_type=MESH,
        )

    def other_copy(m):
        return pltpu.make_async_remote_copy(
            src_ref=ein.at[m], dst_ref=ent.at[mine, m],
            send_sem=ot_send.at[m], recv_sem=ot_recv.at[m],
            device_id=(group, sibling), device_id_type=MESH,
        )

    top, fine = 2.0 ** grid_bits(dims), 2.0 ** (grid_bits(dims) + 21)
    finest = 2.0 ** (grid_bits(dims) + 42)
    one_row = iota((EXTRA, CHUNK), 0)

    is_state = iota((wide_rows, CHUNK), 0) < SPAN

    def chain_step(m):
        @pl.when(first)
        def _():
            ein[m] = jnp.zeros((wide_rows, CHUNK), F32)

        zone_copy(m).wait_recv()

        @pl.when(jnp.logical_not(first))
        def _():
            chain_copy(m).wait_recv()
            other_copy(m).start()

        near, own = zsib[m], zone[mine, m]
        g_near, g_own = near[SPAN : SPAN + 1], own[SPAN : SPAN + 1]
        entry = near + jnp.where(is_state, g_near, 1.0) * ein[m]
        ent[mine, m] = entry

        @pl.when(jnp.logical_not(last))
        def _():
            eout[m] = own + jnp.where(is_state, g_own, 1.0) * entry
            chain_copy(m).start()

    zone_ticks, hop_ticks, cells = 6, 6, blocks * parts

    def due(m):
        return zone_ticks * (m // 2) + hop_ticks * place + lax.rem(m, 2)

    @pl.loop(0, parts)
    def _(c):
        at_w = pl.ds(pl.multiple_of(c * CHUNK, CHUNK), CHUNK)

        zero = jnp.zeros((SPAN, CHUNK), F32)
        loc[0, 0, :, at_w] = zero
        loc[1, 0, :, at_w] = zero
        loc[2, blocks, :, at_w] = zero
        loc[3, blocks, :, at_w] = zero

        def products(k, dot_xy):
            n = blocks - 1 - k
            at_k = pl.ds(pl.multiple_of(k * SPAN, SPAN), SPAN)
            at_n = pl.ds(pl.multiple_of(n * SPAN, SPAN), SPAN)
            x = x_ref[at_k, at_w].astype(F32)
            y = y_ref[at_k, at_w].astype(F32)
            turn[k * parts + c] = y.T.astype(BF16)
            wides = mm(wcol[k], spread[c, :, 2 * CHUNK :])
            xf = jnp.concatenate(pieces(wides[:, CHUNK:] * x), axis=0)
            yr = jnp.concatenate(pieces(wides[:, :CHUNK] * y), axis=0)
            fade_f = fades[c, 0, pl.ds(k, 1), :]
            fade_r = fades[c, 1, pl.ds(k, 1), :]
            loc[0, k + 1, :, at_w] = fade_f * loc[0, k, :, at_w] + mm(bt2[k], xf)
            loc[1, k + 1, :, at_w] = fade_r * loc[1, k, :, at_w] + mm(ct2[k], yr)
            wides = mm(wcol[n], spread[c, :, : 2 * CHUNK])
            yf = jnp.concatenate(pieces(wides[:, :CHUNK] * y_ref[at_n, at_w].astype(F32)), axis=0)
            xr = jnp.concatenate(pieces(wides[:, CHUNK:] * x_ref[at_n, at_w].astype(F32)), axis=0)
            fade_f = fades[c, 0, pl.ds(n, 1), :]
            fade_r = fades[c, 1, pl.ds(n, 1), :]
            loc[2, n, :, at_w] = fade_f * loc[2, n + 1, :, at_w] + mm(ct2[n], yf)
            loc[3, n, :, at_w] = fade_r * loc[3, n + 1, :, at_w] + mm(bt2[n], xr)
            return dot_xy + jnp.sum((x * y).reshape(SPAN // 8, 8, CHUNK), axis=0)

        dot_xy = lax.fori_loop(0, blocks, products, jnp.zeros((8, CHUNK), F32))

        dot_row = jnp.sum(dot_xy, axis=0, keepdims=True)
        coarse = jnp.round(dot_row * top) * (1.0 / top)
        rest = dot_row - coarse
        middle = jnp.round(rest * fine) * (1.0 / fine)
        small = jnp.round((rest - middle) * finest) * (1.0 / finest)

        def put(flow, comp, value, g):
            m = c * 2 + comp
            zone[flow, m, 0:SPAN, :] = value
            zone[flow, m, SPAN:, :] = jnp.where(
                one_row == 0, g,
                jnp.where(one_row == 1, coarse, jnp.where(one_row == 2, middle, jnp.where(one_row == 3, small, 0.0))),
            )

        put(0, 0, loc[0, blocks, :, at_w], whole[c, 0])
        put(0, 1, loc[1, blocks, :, at_w], whole[c, 1])
        put(1, 0, loc[2, 0, :, at_w], whole[c, 0])
        put(1, 1, loc[3, 0, :, at_w], whole[c, 1])
        zone_copy(2 * c).start()
        zone_copy(2 * c + 1).start()

        @pl.loop(0, 2 * c + 2)
        def _(m):
            @pl.when(due(m) // zone_ticks == c)
            def _():
                chain_step(m)

    low = t_pos > s_pos
    diag = t_pos == s_pos
    half = iota((SPAN, SPAN), 1) < size

    def inner(i):
        c, k = i // blocks, lax.rem(i, blocks)
        at_r = pl.ds(pl.multiple_of(k * SPAN, SPAN), SPAN)
        g = gmat[k]
        col = cols[k * parts + c]
        row = rowp[k * parts + c]
        d_sum = dmat[k]
        left = rsum[k]
        lows, diags = [], []
        for p in range(CHUNK // SPAN):
            at_w = pl.ds(pl.multiple_of(c * CHUNK + p * SPAN, SPAN), SPAN)
            x, y = x_ref[at_r, at_w], y_ref[at_r, at_w]
            tall, wide = [], []
            firsts = jnp.where(half, y.astype(F32), 0.0).astype(BF16)
            seconds = jnp.where(half, 0.0, y.astype(F32)).astype(BF16)
            crossed = mm(jnp.concatenate([firsts, seconds], axis=0), x, NT)
            for q in range(SPAN // size):
                h = p * (SPAN // size) + q
                fall = col[:, h : h + 1] - row[h : h + 1]
                rise = col[:, hp + h : hp + h + 1] - row[hp + h : hp + h + 1]
                mid = row[2 * hp + h : 2 * hp + h + 1]
                w = jnp.exp2(jnp.where(low, fall, jnp.where(diag, mid, rise)))
                cross = crossed[q * SPAN : (q + 1) * SPAN]
                wg = w * g
                d_sum = d_sum + cross * w
                pull = jnp.where(low, cross * wg, 0.0)
                lows.append(jnp.sum(pull, axis=0, keepdims=True))
                left = jnp.where(lane == c * hp + h, jnp.sum(pull, axis=1, keepdims=True), left)
                diags.append(jnp.sum(jnp.where(diag, cross, 0.0), axis=0, keepdims=True))
                w_h, w_l = pieces(wg)
                tall.append(jnp.concatenate([w_h, w_l], axis=1))
                y_t = turn[k * parts + c, h * size : (h + 1) * size, :]
                ix[k * parts + c, h * size : (h + 1) * size, :] = mm(
                    jnp.concatenate([y_t, y_t], axis=1), jnp.concatenate([w_h, w_l], axis=0)
                )
            both_y = mm(jnp.concatenate(tall, axis=0), jnp.concatenate([x, x], axis=0))
            iy[k * parts + c, :, p * SPAN : (p + 1) * SPAN] = jnp.where(half, both_y[:SPAN], both_y[SPAN:])
        dmat[k] = d_sum
        csum[k * parts + c] = jnp.concatenate(lows + diags, axis=0)
        rsum[k] = left

    first_tick = zone_ticks * parts

    @pl.loop(0, cells)
    def _(i):
        inner(i)
        late = first_tick + i - hop_ticks * place
        m = 2 * (late // zone_ticks) + lax.rem(late, zone_ticks)

        @pl.when((late >= 0) & (lax.rem(late, zone_ticks) < 2) & (m < messages))
        def _():
            chain_step(m)

    head_row = iota((8, CHUNK), 0) == iota((8, CHUNK), 1) // size
    pick = head_row.astype(F32)

    @pl.loop(0, parts)
    def _(c):
        at_w = pl.ds(pl.multiple_of(c * CHUNK, CHUNK), CHUNK)
        began = first_tick + cells + blocks * c
        for comp in range(2):
            m = 2 * c + comp

            @pl.when(due(m) >= began)
            def _():
                chain_step(m)

        for comp in range(2):
            m = 2 * c + comp

            @pl.when(other_place == 0)
            def _():
                ent[1 - mine, m] = jnp.zeros((wide_rows, CHUNK), F32)

            @pl.when(other_place > 0)
            def _():
                other_copy(m).wait_recv()

        @pl.loop(0, blocks)
        def _(k):
            at_r = pl.ds(pl.multiple_of(k * SPAN, SPAN), SPAN)
            at = k * parts + c
            x = x_ref[at_r, at_w].astype(F32)
            y = y_ref[at_r, at_w].astype(F32)
            wides = mm(wcol[k], spread[c])
            ef_w, wr_w = wides[:, :CHUNK], wides[:, CHUNK : 2 * CHUNK]
            er_w, wf_w = wides[:, 2 * CHUNK : 3 * CHUNK], wides[:, 3 * CHUNK :]

            def entered(slot, row, flow, comp):
                return pieces(
                    loc[slot, k + flow, :, at_w] + wts[c, row, pl.ds(k, 1), :] * ent[flow, 2 * c + comp, 0:SPAN, :]
                )

            sf_h, sf_l = entered(0, 0, 0, 0)
            ar_h, ar_l = entered(1, 1, 0, 1)
            af_h, af_l = entered(2, 2, 1, 0)
            sr_h, sr_l = entered(3, 3, 1, 1)
            cat = lambda *v: jnp.concatenate(v, axis=0)
            v_f = mm(cc2[k], cat(sf_h, sf_l))
            v_r = mm(cc2[k], cat(sr_h, sr_l))
            u_f = mm(bb2[k], cat(af_h, af_l))
            u_r = mm(bb2[k], cat(ar_h, ar_l))
            gain = gwide[c, 0:1]
            yf, yr, xf, xr = ef_w * y, er_w * y, wf_w * x, wr_w * x
            mixed = iy[at] + ef_w * v_f + er_w * v_r + gain * x
            grad_x = ix[at].T + wf_w * u_f + wr_w * u_r + gain * y
            out_ref[at_r, at_w] = mixed.astype(BF16)
            gx_ref[at_r, at_w] = grad_x.astype(BF16)

            def joined(a, ah_al, b, bh_bl):
                a_h, a_l = pieces(a)
                b_h, b_l = pieces(b)
                left = jnp.concatenate([a_h, a_h, a_l, b_h, b_h, b_l], axis=1)
                right = jnp.concatenate(
                    [ah_al[0], ah_al[1], ah_al[0], bh_bl[0], bh_bl[1], bh_bl[0]], axis=1
                )
                return mm(left, right, NT)

            gca[k] += joined(yf, (sf_h, sf_l), yr, (sr_h, sr_l))
            gba[k] += joined(xf, (af_h, af_l), xr, (ar_h, ar_l))

            def narrow(v):
                turned = v.T
                return jnp.concatenate(
                    [jnp.sum(turned[j * size : (j + 1) * size], axis=0, keepdims=True) for j in range(hp)], axis=0
                )

            psum[at, 0:hp] = narrow(yf * v_f)
            psum[at, hp : 2 * hp] = narrow(xf * u_f)
            psum[at, 2 * hp : 3 * hp] = narrow(y * mixed)
            psum[at, 3 * hp : 4 * hp] = narrow(x * grad_x)
            late = began + k - hop_ticks * place
            m = 2 * (late // zone_ticks) + lax.rem(late, zone_ticks)

            @pl.when((late >= 0) & (lax.rem(late, zone_ticks) < 2) & (m < messages) & (m >= 2 * c + 2))
            def _():
                chain_step(m)

    def gathered(make):
        out = []
        for k in range(blocks):
            for c in range(parts):
                out.append(make(k, c))
        return jnp.concatenate(out, axis=0)

    def sums(first_row):
        return gathered(lambda k, c: psum[k * parts + c, first_row : first_row + hp])

    row_low = stacked(lambda k: rsum[k].T[0:heads])
    col_low = gathered(lambda k, c: csum[k * parts + c, 0:hp])
    both = gathered(lambda k, c: csum[k * parts + c, hp : 2 * hp])
    center = stacked(
        lambda k: jnp.broadcast_to(
            jnp.sum(jnp.where(diag, gmat[k], 0.0), axis=0, keepdims=True), (heads, SPAN)
        )
    )
    ends_f, ends_r, gains = [], [], []
    for c in range(parts):
        for flow, comp, opp_flow, opp_comp, into in ((0, 0, 1, 0, ends_f), (1, 1, 0, 1, ends_r)):
            own = zone[flow, 2 * c + comp]
            leaving = own[:SPAN] + own[SPAN : SPAN + 1] * ent[flow, 2 * c + comp, 0:SPAN, :]
            held = exact(pick, leaving * ent[opp_flow, 2 * c + opp_comp, 0:SPAN, :], NT)
            into.append(jnp.sum(held, axis=1, keepdims=True)[0:hp])
        total = ent[0, 2 * c, SPAN:, :] + (zone[0, 2 * c, SPAN:, :] + ent[1, 2 * c, SPAN:, :])
        row = total[1:2] + (total[2:3] + total[3:4])
        spots = (iota((CHUNK, heads), 1) == c * hp + iota((CHUNK, heads), 0) // size).astype(F32)
        gains.append(exact(jnp.broadcast_to(row, (8, CHUNK)), spots))
    gain_sum = sum(gains)
    gg_ref[...] = ((gain_sum + exact(gain_sum, anti)) * (1.0 / math.sqrt(rows * count * size)))[:1]

    gain_all = jnp.concatenate([gain_col] * blocks, axis=0)
    own_terms = (gain_all + (sf + sr) * center) * both
    row_f = row_low + sums(0 * hp)
    col_f = col_low + sums(hp)
    row_r = sums(2 * hp) - own_terms - row_f
    col_r = sums(3 * hp) - own_terms - col_f
    mid = center * both
    diff_f, diff_r = col_f - row_f, col_r - row_r
    tail_f = exact(diff_f, behind_sum)
    head_r = exact(diff_r, ahead_sum)
    later, earlier = [None] * blocks, [None] * blocks
    run = -jnp.concatenate(ends_f, axis=0)
    for k in range(blocks - 1, -1, -1):
        at = slice(k * heads, (k + 1) * heads)
        later[k] = run
        run = run + tail_f[at, :1]
    run = -jnp.concatenate(ends_r, axis=0)
    for k in range(blocks):
        at = slice(k * heads, (k + 1) * heads)
        earlier[k] = run
        run = run + head_r[at, SPAN - 1 :]
    drop_f = tail_f + jnp.concatenate(later, axis=0)
    drop_r = head_r + jnp.concatenate(earlier, axis=0)
    d_f = col_f / sf + mid + rates_f * drop_f
    d_r = col_r / sr + mid + rates_r * drop_r
    grad_s = d_f * slope_f + d_r * slope_r
    for k in range(blocks):
        here = slice(k * SPAN, (k + 1) * SPAN)
        gs_ref[:, here] = grad_s[k * heads : (k + 1) * heads]
        d_h, d_l = pieces(dmat[k])
        gc_ref[here, :] = (gca[k] + mm(jnp.concatenate([d_h, d_l], axis=1), jnp.concatenate([b_ref[here, :]] * 2, axis=0))).astype(BF16)
        gb_ref[here, :] = (gba[k] + mm(jnp.concatenate([d_h, d_l], axis=0), jnp.concatenate([c_ref[here, :]] * 2, axis=0), TN)).astype(BF16)

    @pl.loop(0, messages)
    def _(m):
        zone_copy(m).wait_send()

        @pl.when(jnp.logical_not(first))
        def _():
            other_copy(m).wait_send()

        @pl.when(jnp.logical_not(last))
        def _():
            chain_copy(m).wait_send()


def write_out(*refs):
    sems = refs[-1]
    copies = [pltpu.make_async_copy(refs[i], refs[6 + i], sems.at[i]) for i in range(6)]
    for copy in copies:
        copy.start()
    for copy in copies:
        copy.wait()


def heads_per(dims):
    return dims[0] // dims[3]


def grid_bits(dims):
    limit = 120 * dims[2] * SPAN * dims[1]
    return 23 - math.ceil(math.log2(limit))


def per_device(
    features, write_map, read_map, step_raw, tokens, base_shift, decay_rate, skip_gain, cotangent
):
    rows, width = features.shape
    state = write_map.shape[1]
    heads = decay_rate.shape[0]
    count = lax.axis_size("ctx")
    blocks, parts = rows // SPAN, width // CHUNK
    messages = 2 * parts
    dims = (heads, count, blocks, parts, messages)
    hp = heads // parts
    cells = blocks * parts
    wide_rows = SPAN + EXTRA
    vmem = pl.BlockSpec(memory_space=pltpu.VMEM)
    results = (
        ((rows, width), BF16),
        ((rows, width), BF16),
        ((rows, state), BF16),
        ((rows, state), BF16),
        ((heads, rows), F32),
        ((1, heads), F32),
    )
    outs = pl.pallas_call(
        functools.partial(kernel, dims),
        out_shape=tuple(pltpu.VMEM(dims_of, kind) for dims_of, kind in results),
        in_specs=[vmem] * 9,
        out_specs=(vmem,) * 6,
        scratch_shapes=[
            pltpu.VMEM((cells, 4 * hp, SPAN), F32),
            pltpu.VMEM((cells, SPAN, SPAN), F32),
            pltpu.VMEM((blocks, SPAN, SPAN), BF16),
            pltpu.VMEM((parts, SPAN, 4 * CHUNK), BF16),
            pltpu.VMEM((blocks, SPAN, 2 * SPAN), BF16),
            pltpu.VMEM((blocks, SPAN, 2 * SPAN), BF16),
            pltpu.VMEM((blocks, SPAN, 2 * SPAN), BF16),
            pltpu.VMEM((blocks, SPAN, 2 * SPAN), BF16),
            pltpu.VMEM((blocks, SPAN, SPAN), F32),
            pltpu.VMEM((blocks, SPAN, SPAN), F32),
            pltpu.VMEM((parts, 8, CHUNK), F32),
            pltpu.VMEM((parts, 2, blocks, CHUNK), F32),
            pltpu.VMEM((parts, 4, blocks, CHUNK), F32),
            pltpu.VMEM((parts, 2, EXTRA, CHUNK), F32),
            pltpu.VMEM((cells, CHUNK, SPAN), BF16),
            pltpu.VMEM((4, blocks + 1, SPAN, width), F32),
            pltpu.VMEM((cells, SPAN, CHUNK), F32),
            pltpu.VMEM((cells, CHUNK, SPAN), F32),
            pltpu.VMEM((blocks, SPAN, SPAN), F32),
            pltpu.VMEM((blocks, SPAN, SPAN), F32),
            pltpu.VMEM((cells, 2 * hp, SPAN), F32),
            pltpu.VMEM((blocks, SPAN, SPAN), F32),
            pltpu.VMEM((cells, 4 * hp, SPAN), F32),
            pltpu.VMEM((2, messages, wide_rows, CHUNK), F32),
            pltpu.VMEM((messages, wide_rows, CHUNK), F32),
            pltpu.VMEM((messages, wide_rows, CHUNK), F32),
            pltpu.VMEM((messages, wide_rows, CHUNK), F32),
            pltpu.VMEM((2, messages, wide_rows, CHUNK), F32),
        ]
        + [pltpu.SemaphoreType.DMA((messages,))] * 6,
        compiler_params=pltpu.CompilerParams(
            collective_id=0, has_side_effects=True, vmem_limit_bytes=56 * 1024 * 1024
        ),
    )(
        features, cotangent, write_map, read_map, step_raw.T, tokens.reshape(blocks, SPAN),
        base_shift, decay_rate.reshape(1, heads), skip_gain.reshape(1, heads),
    )
    anywhere = pl.BlockSpec(memory_space=pl.ANY)
    mixed, grad_x, grad_b, grad_c, grad_s, gains = pl.pallas_call(
        write_out,
        out_shape=tuple(jax.ShapeDtypeStruct(dims_of, kind) for dims_of, kind in results),
        in_specs=[anywhere] * 6,
        out_specs=(anywhere,) * 6,
        scratch_shapes=[pltpu.SemaphoreType.DMA((6,))],
        compiler_params=pltpu.CompilerParams(vmem_limit_bytes=1024 * 1024),
    )(*outs)
    return mixed, grad_x, grad_b, grad_c, grad_s.T, gains.reshape(heads)


def solution(mesh):
    split = P(("groups", "ctx"), None)
    return jax.shard_map(
        per_device,
        mesh=mesh,
        in_specs=(split, split, split, split, P(("groups", "ctx")), P(), P(), P(), split),
        out_specs=(split, split, split, split, split, P("groups")),
        check_vma=False,
    )
```

```python
import functools
import math

import jax
import jax.numpy as jnp
from jax import lax
from jax.experimental import pallas as pl
from jax.experimental.pallas import tpu as pltpu
from jax.sharding import PartitionSpec as P

F32 = jnp.float32
BF16 = jnp.bfloat16
EXACT = lax.Precision.HIGHEST
SPAN = 128
CHUNK = 256
EXTRA = 8
PIECE = 128
PER = 2 * CHUNK // PIECE
LOG2E = 1.4426950408889634
MESH = pl.DeviceIdType.MESH

NN = (((1,), (0,)), ((), ()))
NT = (((1,), (1,)), ((), ()))
TN = (((0,), (0,)), ((), ()))


def mm(a, b, dims=NN):
    return lax.dot_general(a, b, dims, preferred_element_type=F32)


def exact(a, b, dims=NN):
    return lax.dot_general(a, b, dims, precision=EXACT, preferred_element_type=F32)


def pieces(v):
    high = v.astype(BF16)
    return high, (v - high.astype(F32)).astype(BF16)


def iota(shape, dim):
    return lax.broadcasted_iota(jnp.int32, shape, dim)


def log1p_unit(z):
    s = z / (z + 2.0)
    q = s * s
    acc = jnp.full_like(q, 1.0 / 19.0)
    for k in range(8, -1, -1):
        acc = acc * q + 1.0 / (2 * k + 1)
    return 2.0 * s * acc


def kernel(
    dims,
    x_ref, y_ref, b_ref, c_ref, raw_ref, tok_ref, base_ref, rate_ref, gain_ref,
    out_ref, gx_ref, gb_ref, gc_ref, gs_ref, gg_ref,
    rowp, cols, wcol, spread, bt2, ct2, bb2, cc2, gmat, dmat, gwide, fades, wts, whole, turn,
    loc, iy, ix, gca, gba, csum, rsum, psum,
    zone, zsib, ein, eout, ent, zpair, esib,
    zs_send, zs_recv, ch_send, ch_recv, ot_send, ot_recv, zp_send, zp_recv, mt_send,
):
    heads, count, blocks, parts, messages = dims
    size = CHUNK // heads_per(dims)
    hp = heads_per(dims)
    rows = blocks * SPAN
    width = parts * CHUNK
    wide_rows = SPAN + EXTRA

    group = lax.axis_index("groups")
    me = lax.axis_index("ctx")
    core = lax.rem(me, 2)
    chip = me // 2
    chips = count // 2
    mine = 1 - core
    step = 2 * core - 1
    odd = lax.rem(chip, 2)
    second = odd == core
    pairs = chips // 2
    place = jnp.where(core == 1, chip // 2, pairs - 1 - chip // 2)
    first, last = place == 0, place == pairs - 1
    sibling = me + 1 - 2 * core
    mate = me + 2 - 4 * odd
    after = jnp.clip(me + 4 * step, 0, count - 1)
    before = jnp.clip(me - 4 * step, 0, count - 1)
    has_after = second & jnp.logical_not(last)
    has_before = second & jnp.logical_not(first)
    alone = second & last

    barrier = pltpu.get_barrier_semaphore()
    pl.semaphore_signal(barrier, inc=1, device_id=(group, sibling), device_id_type=MESH)
    pl.semaphore_signal(barrier, inc=1, device_id=(group, mate), device_id_type=MESH)

    @pl.when(has_after)
    def _():
        pl.semaphore_signal(barrier, inc=1, device_id=(group, after), device_id_type=MESH)

    @pl.when(has_before)
    def _():
        pl.semaphore_signal(barrier, inc=1, device_id=(group, before), device_id_type=MESH)

    pl.semaphore_wait(barrier, 2 + has_after.astype(jnp.int32) + has_before.astype(jnp.int32))

    eye = (iota((heads, heads), 0) == iota((heads, heads), 1)).astype(F32)
    anti = (iota((heads, heads), 0) + iota((heads, heads), 1) == heads - 1).astype(F32)
    raw_t = raw_ref[...]
    base_f = exact(eye, base_ref[...], NT)
    base_r = exact(anti, base_ref[...], NT)
    rate_f = exact(eye, jnp.broadcast_to(rate_ref[...], (8, heads)), NT)[:, :1]
    rate_r = exact(anti, jnp.broadcast_to(rate_ref[...], (8, heads)), NT)[:, :1]
    gain_row = gain_ref[...] + exact(jnp.broadcast_to(gain_ref[...], (8, heads)), anti)[:1]
    gain_col = exact(eye, jnp.broadcast_to(gain_row, (8, heads)), NT)[:, :1]

    def stacked(make):
        return jnp.concatenate([make(k) for k in range(blocks)], axis=0)

    def logits(k, base, pair):
        tok = tok_ref[k : k + 1, :]
        value = raw_t[:, k * SPAN : (k + 1) * SPAN]
        for code in range(5):
            col = pair[code]
            value = value + jnp.where(tok == code, base[:, col : col + 1], 0.0)
        return value

    vf = stacked(lambda k: logits(k, base_f, (0, 1, 2, 3, 4)))
    vr = stacked(lambda k: logits(k, base_r, (3, 2, 1, 0, 4)))

    def steps_of(v):
        z = jnp.exp(-jnp.abs(v))
        s = jnp.maximum(v, 0.0) + log1p_unit(z)
        inv = 1.0 / (1.0 + z)
        return s, jnp.where(v >= 0.0, inv, z * inv)

    sf, slope_f = steps_of(vf)
    sr, slope_r = steps_of(vr)
    rates_f = jnp.concatenate([rate_f] * blocks, axis=0)
    rates_r = jnp.concatenate([rate_r] * blocks, axis=0)
    t_pos = iota((SPAN, SPAN), 0)
    s_pos = iota((SPAN, SPAN), 1)
    ahead_sum = (t_pos <= s_pos).astype(F32)
    behind_sum = (t_pos >= s_pos).astype(F32)
    nf = exact(sf * (rates_f * -LOG2E), ahead_sum)
    nr = exact(sr * (rates_r * -LOG2E), behind_sum)
    end_f, end_r = nf[:, SPAN - 1 :], nr[:, :1]
    ef, er = jnp.exp2(nf), jnp.exp2(nr)
    wf, wr = jnp.exp2(end_f - nf) * sf, jnp.exp2(end_r - nr) * sr
    mf, mr = nf - jnp.log2(sf), nr - jnp.log2(sr)
    both_log = jnp.log2(sf + sr)

    lane = iota((SPAN, SPAN), 1)
    ends_at_last, ends_at_first = [], []
    for k in range(blocks):
        at = slice(k * heads, (k + 1) * heads)
        four = jnp.concatenate([ef[at], wr[at], er[at], wf[at]] * 2, axis=0)
        turned = four.T
        high, low = pieces(turned)
        joint = jnp.where(lane < 4 * heads, high.astype(F32), low.astype(F32))
        wcol[k] = joint.astype(BF16)
        ends_at_last.append(joint[SPAN - 1 :])
        ends_at_first.append(joint[:1])
        order = []
        for c in range(parts):
            sub = slice(k * heads + c * hp, k * heads + (c + 1) * hp)
            order += [nf[sub], nr[sub]]
            rowp[k * parts + c] = jnp.concatenate([mf[sub], mr[sub], both_log[sub], both_log[sub]], axis=0)
        pad = [jnp.zeros((SPAN - 2 * heads, SPAN), F32)]
        turned = jnp.concatenate(order + pad, axis=0).T
        for c in range(parts):
            cols[k * parts + c, :, 0 : 2 * hp] = turned[:, 2 * hp * c : 2 * hp * (c + 1)]
        here = slice(k * SPAN, (k + 1) * SPAN)
        bk, ck = b_ref[here, :], c_ref[here, :]
        bkt = bk.astype(F32).T.astype(BF16)
        ckt = ck.astype(F32).T.astype(BF16)
        bt2[k] = jnp.concatenate([bkt, bkt], axis=1)
        ct2[k] = jnp.concatenate([ckt, ckt], axis=1)
        bb2[k] = jnp.concatenate([bk, bk], axis=1)
        cc2[k] = jnp.concatenate([ck, ck], axis=1)
        gmat[k] = mm(ck, bk, NT)
        dmat[k] = jnp.zeros((SPAN, SPAN), F32)
        gca[k] = jnp.zeros((SPAN, SPAN), F32)
        gba[k] = jnp.zeros((SPAN, SPAN), F32)
        rsum[k] = jnp.zeros((SPAN, SPAN), F32)

    for c in range(parts):
        r = iota((SPAN, 4 * CHUNK), 0)
        j = iota((SPAN, 4 * CHUNK), 1)
        rr = lax.rem(r, 4 * heads)
        hit = (rr // heads == j // CHUNK) & (lax.rem(rr, heads) == c * hp + lax.rem(j, CHUNK) // size)
        spread[c] = hit.astype(F32).astype(BF16)
        hw = iota((heads, CHUNK), 0) == c * hp + iota((heads, CHUNK), 1) // size
        gwide[c] = exact(jnp.broadcast_to(gain_row, (8, heads)), hw.astype(F32))
        fade_f = mm(jnp.concatenate(ends_at_last, axis=0).astype(BF16), spread[c, :, :CHUNK])
        fade_r = mm(jnp.concatenate(ends_at_first, axis=0).astype(BF16), spread[c, :, 2 * CHUNK : 3 * CHUNK])
        fades[c, 0], fades[c, 1] = fade_f, fade_r
        for row, fade in ((0, fade_f), (1, fade_r)):
            run = jnp.ones((1, CHUNK), F32)
            for k in range(blocks):
                wts[c, row, k : k + 1, :] = run
                run = run * fade[k : k + 1]
            whole[c, row] = jnp.broadcast_to(run, (EXTRA, CHUNK))
            run = jnp.ones((1, CHUNK), F32)
            for k in range(blocks - 1, -1, -1):
                wts[c, row + 2, k : k + 1, :] = run
                run = run * fade[k : k + 1]

    def zone_copy(m):
        return pltpu.make_async_remote_copy(
            src_ref=zone.at[1 - mine, m], dst_ref=zsib.at[m],
            send_sem=zs_send.at[m], recv_sem=zs_recv.at[m],
            device_id=(group, sibling), device_id_type=MESH,
        )

    def chain_copy(m):
        return pltpu.make_async_remote_copy(
            src_ref=eout.at[m], dst_ref=ein.at[m],
            send_sem=ch_send.at[m], recv_sem=ch_recv.at[m],
            device_id=(group, after), device_id_type=MESH,
        )

    def remote(source, target, m, send, recv, device):
        return pltpu.make_async_remote_copy(
            src_ref=source, dst_ref=target, send_sem=send.at[m], recv_sem=recv.at[m],
            device_id=(group, device), device_id_type=MESH,
        )

    def pass_on(m):
        return remote(ein.at[m], ent.at[mine, m], m, ot_send, ot_recv, sibling)

    def give(m):
        return remote(esib.at[m], ent.at[mine, m], m, ot_send, ot_recv, sibling)

    def pair_copy(m):
        return remote(eout.at[m], zpair.at[m], m, zp_send, zp_recv, mate)

    def mate_copy(m):
        return remote(ein.at[m], ein.at[m], m, mt_send, ch_recv, mate)

    top, fine = 2.0 ** grid_bits(dims), 2.0 ** (grid_bits(dims) + 21)
    finest = 2.0 ** (grid_bits(dims) + 42)
    one_row = iota((EXTRA, CHUNK), 0)

    is_state = iota((wide_rows, PIECE), 0) < SPAN

    def over(near, value):
        return near + jnp.where(is_state, near[SPAN : SPAN + 1], 1.0) * value

    def join_step(m):
        zone_copy(m).wait_recv()
        near, own = zsib[m], zone[mine, m]
        eout[m] = over(own, near)
        eout[m, SPAN : SPAN + 1, :] = own[SPAN : SPAN + 1] * near[SPAN : SPAN + 1]
        pair_copy(m).start()

    def chain_step(m):
        @pl.when(first)
        def _():
            ein[m] = jnp.zeros((wide_rows, PIECE), F32)

        @pl.when(jnp.logical_not(first))
        def _():
            chain_copy(m).wait_recv()

        @pl.when(jnp.logical_not(second))
        def _():
            @pl.when(jnp.logical_not(first))
            def _():
                pass_on(m).start()

            ent[mine, m] = over(zsib[m], ein[m])

        @pl.when(second)
        def _():
            @pl.when(jnp.logical_not(first))
            def _():
                mate_copy(m).start()

            zone_copy(m).wait_recv()
            pair_copy(m).wait_recv()
            theirs = over(zpair[m], ein[m])
            esib[m] = theirs
            give(m).start()
            entry = over(zsib[m], theirs)
            ent[mine, m] = entry

            @pl.when(jnp.logical_not(last))
            def _():
                eout[m] = over(zone[mine, m], entry)
                chain_copy(m).start()

    zone_ticks, join_tick, cells = 8, 5, blocks * parts
    chain_tick = 14 + 12 * place + jnp.where(second, 0, 12)

    def due(m):
        return zone_ticks * (m // PER) + chain_tick + lax.rem(m, PER)

    def tick(t, least, joins):
        def run(late, allowed, do):
            m = PER * (late // zone_ticks) + lax.rem(late, zone_ticks)

            @pl.when(allowed & (late >= 0) & (lax.rem(late, zone_ticks) < PER) & (m >= least) & (m < messages))
            def _():
                do(m)

        if joins:
            run(t - join_tick, jnp.logical_not(second), join_step)
        run(t - chain_tick, True, chain_step)

    @pl.loop(0, parts)
    def _(c):
        at_w = pl.ds(pl.multiple_of(c * CHUNK, CHUNK), CHUNK)

        zero = jnp.zeros((SPAN, CHUNK), F32)
        loc[0, 0, :, at_w] = zero
        loc[1, 0, :, at_w] = zero
        loc[2, blocks, :, at_w] = zero
        loc[3, blocks, :, at_w] = zero

        def products(k, dot_xy):
            n = blocks - 1 - k
            at_k = pl.ds(pl.multiple_of(k * SPAN, SPAN), SPAN)
            at_n = pl.ds(pl.multiple_of(n * SPAN, SPAN), SPAN)
            x = x_ref[at_k, at_w].astype(F32)
            y = y_ref[at_k, at_w].astype(F32)
            turn[k * parts + c] = y.T.astype(BF16)
            wides = mm(wcol[k], spread[c, :, 2 * CHUNK :])
            xf = jnp.concatenate(pieces(wides[:, CHUNK:] * x), axis=0)
            yr = jnp.concatenate(pieces(wides[:, :CHUNK] * y), axis=0)
            fade_f = fades[c, 0, pl.ds(k, 1), :]
            fade_r = fades[c, 1, pl.ds(k, 1), :]
            loc[0, k + 1, :, at_w] = fade_f * loc[0, k, :, at_w] + mm(bt2[k], xf)
            loc[1, k + 1, :, at_w] = fade_r * loc[1, k, :, at_w] + mm(ct2[k], yr)
            wides = mm(wcol[n], spread[c, :, : 2 * CHUNK])
            yf = jnp.concatenate(pieces(wides[:, :CHUNK] * y_ref[at_n, at_w].astype(F32)), axis=0)
            xr = jnp.concatenate(pieces(wides[:, CHUNK:] * x_ref[at_n, at_w].astype(F32)), axis=0)
            fade_f = fades[c, 0, pl.ds(n, 1), :]
            fade_r = fades[c, 1, pl.ds(n, 1), :]
            loc[2, n, :, at_w] = fade_f * loc[2, n + 1, :, at_w] + mm(ct2[n], yf)
            loc[3, n, :, at_w] = fade_r * loc[3, n + 1, :, at_w] + mm(bt2[n], xr)
            return dot_xy + jnp.sum((x * y).reshape(SPAN // 8, 8, CHUNK), axis=0)

        dot_xy = lax.fori_loop(0, blocks, products, jnp.zeros((8, CHUNK), F32))

        dot_row = jnp.sum(dot_xy, axis=0, keepdims=True)
        coarse = jnp.round(dot_row * top) * (1.0 / top)
        rest = dot_row - coarse
        middle = jnp.round(rest * fine) * (1.0 / fine)
        small = jnp.round((rest - middle) * finest) * (1.0 / finest)

        def put(flow, comp, value, g):
            tail = jnp.where(
                one_row == 0, g,
                jnp.where(one_row == 1, coarse, jnp.where(one_row == 2, middle, jnp.where(one_row == 3, small, 0.0))),
            )
            for j in range(CHUNK // PIECE):
                m = c * PER + comp * (CHUNK // PIECE) + j
                zone[flow, m, 0:SPAN, :] = value[:, j * PIECE : (j + 1) * PIECE]
                zone[flow, m, SPAN:, :] = tail[:, j * PIECE : (j + 1) * PIECE]

        put(0, 0, loc[0, blocks, :, at_w], whole[c, 0])
        put(0, 1, loc[1, blocks, :, at_w], whole[c, 1])
        put(1, 0, loc[2, 0, :, at_w], whole[c, 0])
        put(1, 1, loc[3, 0, :, at_w], whole[c, 1])
        for j in range(PER):
            zone_copy(PER * c + j).start()

        @pl.loop(0, zone_ticks)
        def _(t):
            tick(zone_ticks * c + t, 0, True)

    low = t_pos > s_pos
    diag = t_pos == s_pos
    half = iota((SPAN, SPAN), 1) < size

    def inner(i):
        c, k = i // blocks, lax.rem(i, blocks)
        at_r = pl.ds(pl.multiple_of(k * SPAN, SPAN), SPAN)
        g = gmat[k]
        col = cols[k * parts + c]
        row = rowp[k * parts + c]
        d_sum = dmat[k]
        left = rsum[k]
        lows, diags = [], []
        for p in range(CHUNK // SPAN):
            at_w = pl.ds(pl.multiple_of(c * CHUNK + p * SPAN, SPAN), SPAN)
            x, y = x_ref[at_r, at_w], y_ref[at_r, at_w]
            tall, wide = [], []
            firsts = jnp.where(half, y.astype(F32), 0.0).astype(BF16)
            seconds = jnp.where(half, 0.0, y.astype(F32)).astype(BF16)
            crossed = mm(jnp.concatenate([firsts, seconds], axis=0), x, NT)
            for q in range(SPAN // size):
                h = p * (SPAN // size) + q
                fall = col[:, h : h + 1] - row[h : h + 1]
                rise = col[:, hp + h : hp + h + 1] - row[hp + h : hp + h + 1]
                mid = row[2 * hp + h : 2 * hp + h + 1]
                w = jnp.exp2(jnp.where(low, fall, jnp.where(diag, mid, rise)))
                cross = crossed[q * SPAN : (q + 1) * SPAN]
                wg = w * g
                d_sum = d_sum + cross * w
                pull = jnp.where(low, cross * wg, 0.0)
                lows.append(jnp.sum(pull, axis=0, keepdims=True))
                left = jnp.where(lane == c * hp + h, jnp.sum(pull, axis=1, keepdims=True), left)
                diags.append(jnp.sum(jnp.where(diag, cross, 0.0), axis=0, keepdims=True))
                w_h, w_l = pieces(wg)
                tall.append(jnp.concatenate([w_h, w_l], axis=1))
                y_t = turn[k * parts + c, h * size : (h + 1) * size, :]
                ix[k * parts + c, h * size : (h + 1) * size, :] = mm(
                    jnp.concatenate([y_t, y_t], axis=1), jnp.concatenate([w_h, w_l], axis=0)
                )
            both_y = mm(jnp.concatenate(tall, axis=0), jnp.concatenate([x, x], axis=0))
            iy[k * parts + c, :, p * SPAN : (p + 1) * SPAN] = jnp.where(half, both_y[:SPAN], both_y[SPAN:])
        dmat[k] = d_sum
        csum[k * parts + c] = jnp.concatenate(lows + diags, axis=0)
        rsum[k] = left

    first_tick = zone_ticks * parts

    @pl.loop(0, cells)
    def _(i):
        inner(i)
        tick(first_tick + i, 0, True)

    def side(array, flow, c, comp, low_row, high_row):
        m = PER * c + comp * (CHUNK // PIECE)
        return jnp.concatenate([array[flow, m + j, low_row:high_row, :] for j in range(CHUNK // PIECE)], axis=1)

    head_row = iota((8, CHUNK), 0) == iota((8, CHUNK), 1) // size
    pick = head_row.astype(F32)

    @pl.loop(0, parts)
    def _(c):
        at_w = pl.ds(pl.multiple_of(c * CHUNK, CHUNK), CHUNK)
        began = first_tick + cells + blocks * c
        for j in range(PER):
            m = PER * c + j

            @pl.when(due(m) >= began)
            def _():
                chain_step(m)

        for j in range(PER):
            m = PER * c + j

            @pl.when(alone)
            def _():
                ent[1 - mine, m] = jnp.zeros((wide_rows, PIECE), F32)

            @pl.when(jnp.logical_not(alone))
            def _():
                give(m).wait_recv()

        @pl.loop(0, blocks)
        def _(k):
            at_r = pl.ds(pl.multiple_of(k * SPAN, SPAN), SPAN)
            at = k * parts + c
            x = x_ref[at_r, at_w].astype(F32)
            y = y_ref[at_r, at_w].astype(F32)
            wides = mm(wcol[k], spread[c])
            ef_w, wr_w = wides[:, :CHUNK], wides[:, CHUNK : 2 * CHUNK]
            er_w, wf_w = wides[:, 2 * CHUNK : 3 * CHUNK], wides[:, 3 * CHUNK :]

            def entered(slot, row, flow, comp):
                return pieces(
                    loc[slot, k + flow, :, at_w] + wts[c, row, pl.ds(k, 1), :] * side(ent, flow, c, comp, 0, SPAN)
                )

            sf_h, sf_l = entered(0, 0, 0, 0)
            ar_h, ar_l = entered(1, 1, 0, 1)
            af_h, af_l = entered(2, 2, 1, 0)
            sr_h, sr_l = entered(3, 3, 1, 1)
            cat = lambda *v: jnp.concatenate(v, axis=0)
            v_f = mm(cc2[k], cat(sf_h, sf_l))
            v_r = mm(cc2[k], cat(sr_h, sr_l))
            u_f = mm(bb2[k], cat(af_h, af_l))
            u_r = mm(bb2[k], cat(ar_h, ar_l))
            gain = gwide[c, 0:1]
            yf, yr, xf, xr = ef_w * y, er_w * y, wf_w * x, wr_w * x
            mixed = iy[at] + ef_w * v_f + er_w * v_r + gain * x
            grad_x = ix[at].T + wf_w * u_f + wr_w * u_r + gain * y
            out_ref[at_r, at_w] = mixed.astype(BF16)
            gx_ref[at_r, at_w] = grad_x.astype(BF16)

            def joined(a, ah_al, b, bh_bl):
                a_h, a_l = pieces(a)
                b_h, b_l = pieces(b)
                left = jnp.concatenate([a_h, a_h, a_l, b_h, b_h, b_l], axis=1)
                right = jnp.concatenate(
                    [ah_al[0], ah_al[1], ah_al[0], bh_bl[0], bh_bl[1], bh_bl[0]], axis=1
                )
                return mm(left, right, NT)

            gca[k] += joined(yf, (sf_h, sf_l), yr, (sr_h, sr_l))
            gba[k] += joined(xf, (af_h, af_l), xr, (ar_h, ar_l))

            def narrow(v):
                turned = v.T
                return jnp.concatenate(
                    [jnp.sum(turned[j * size : (j + 1) * size], axis=0, keepdims=True) for j in range(hp)], axis=0
                )

            psum[at, 0:hp] = narrow(yf * v_f)
            psum[at, hp : 2 * hp] = narrow(xf * u_f)
            psum[at, 2 * hp : 3 * hp] = narrow(y * mixed)
            psum[at, 3 * hp : 4 * hp] = narrow(x * grad_x)
            tick(began + k, PER * c + PER, False)

    def gathered(make):
        out = []
        for k in range(blocks):
            for c in range(parts):
                out.append(make(k, c))
        return jnp.concatenate(out, axis=0)

    def sums(first_row):
        return gathered(lambda k, c: psum[k * parts + c, first_row : first_row + hp])

    row_low = stacked(lambda k: rsum[k].T[0:heads])
    col_low = gathered(lambda k, c: csum[k * parts + c, 0:hp])
    both = gathered(lambda k, c: csum[k * parts + c, hp : 2 * hp])
    center = stacked(
        lambda k: jnp.broadcast_to(
            jnp.sum(jnp.where(diag, gmat[k], 0.0), axis=0, keepdims=True), (heads, SPAN)
        )
    )
    ends_f, ends_r, gains = [], [], []
    for c in range(parts):
        for flow, comp, opp_flow, opp_comp, into in ((0, 0, 1, 0, ends_f), (1, 1, 0, 1, ends_r)):
            own = side(zone, flow, c, comp, 0, SPAN)
            faded = side(zone, flow, c, comp, SPAN, wide_rows)[:1] * side(ent, flow, c, comp, 0, SPAN)
            held = exact(pick, (own + faded) * side(ent, opp_flow, c, opp_comp, 0, SPAN), NT)
            into.append(jnp.sum(held, axis=1, keepdims=True)[0:hp])
        total = side(ent, 0, c, 0, SPAN, wide_rows) + (
            side(zone, 0, c, 0, SPAN, wide_rows) + side(ent, 1, c, 0, SPAN, wide_rows)
        )
        row = total[1:2] + (total[2:3] + total[3:4])
        spots = (iota((CHUNK, heads), 1) == c * hp + iota((CHUNK, heads), 0) // size).astype(F32)
        gains.append(exact(jnp.broadcast_to(row, (8, CHUNK)), spots))
    gain_sum = sum(gains)
    gg_ref[...] = ((gain_sum + exact(gain_sum, anti)) * (1.0 / math.sqrt(rows * count * size)))[:1]

    gain_all = jnp.concatenate([gain_col] * blocks, axis=0)
    own_terms = (gain_all + (sf + sr) * center) * both
    row_f = row_low + sums(0 * hp)
    col_f = col_low + sums(hp)
    row_r = sums(2 * hp) - own_terms - row_f
    col_r = sums(3 * hp) - own_terms - col_f
    mid = center * both
    diff_f, diff_r = col_f - row_f, col_r - row_r
    tail_f = exact(diff_f, behind_sum)
    head_r = exact(diff_r, ahead_sum)
    later, earlier = [None] * blocks, [None] * blocks
    run = -jnp.concatenate(ends_f, axis=0)
    for k in range(blocks - 1, -1, -1):
        at = slice(k * heads, (k + 1) * heads)
        later[k] = run
        run = run + tail_f[at, :1]
    run = -jnp.concatenate(ends_r, axis=0)
    for k in range(blocks):
        at = slice(k * heads, (k + 1) * heads)
        earlier[k] = run
        run = run + head_r[at, SPAN - 1 :]
    drop_f = tail_f + jnp.concatenate(later, axis=0)
    drop_r = head_r + jnp.concatenate(earlier, axis=0)
    d_f = col_f / sf + mid + rates_f * drop_f
    d_r = col_r / sr + mid + rates_r * drop_r
    grad_s = d_f * slope_f + d_r * slope_r
    for k in range(blocks):
        here = slice(k * SPAN, (k + 1) * SPAN)
        gs_ref[:, here] = grad_s[k * heads : (k + 1) * heads]
        d_h, d_l = pieces(dmat[k])
        gc_ref[here, :] = (gca[k] + mm(jnp.concatenate([d_h, d_l], axis=1), jnp.concatenate([b_ref[here, :]] * 2, axis=0))).astype(BF16)
        gb_ref[here, :] = (gba[k] + mm(jnp.concatenate([d_h, d_l], axis=0), jnp.concatenate([c_ref[here, :]] * 2, axis=0), TN)).astype(BF16)

    @pl.loop(0, messages)
    def _(m):
        zone_copy(m).wait_send()

        @pl.when(second)
        def _():
            give(m).wait_send()

            @pl.when(jnp.logical_not(first))
            def _():
                mate_copy(m).wait_send()

            @pl.when(jnp.logical_not(last))
            def _():
                chain_copy(m).wait_send()

        @pl.when(jnp.logical_not(second))
        def _():
            pair_copy(m).wait_send()

            @pl.when(jnp.logical_not(first))
            def _():
                pass_on(m).wait_send()


def write_out(*refs):
    sems = refs[-1]
    copies = [pltpu.make_async_copy(refs[i], refs[6 + i], sems.at[i]) for i in range(6)]
    for copy in copies:
        copy.start()
    for copy in copies:
        copy.wait()


def heads_per(dims):
    return dims[0] // dims[3]


def grid_bits(dims):
    limit = 120 * dims[2] * SPAN * dims[1]
    return 23 - math.ceil(math.log2(limit))


def per_device(
    features, write_map, read_map, step_raw, tokens, base_shift, decay_rate, skip_gain, cotangent
):
    rows, width = features.shape
    state = write_map.shape[1]
    heads = decay_rate.shape[0]
    count = lax.axis_size("ctx")
    blocks, parts = rows // SPAN, width // CHUNK
    messages = PER * parts
    dims = (heads, count, blocks, parts, messages)
    hp = heads // parts
    cells = blocks * parts
    wide_rows = SPAN + EXTRA
    vmem = pl.BlockSpec(memory_space=pltpu.VMEM)
    results = (
        ((rows, width), BF16),
        ((rows, width), BF16),
        ((rows, state), BF16),
        ((rows, state), BF16),
        ((heads, rows), F32),
        ((1, heads), F32),
    )
    outs = pl.pallas_call(
        functools.partial(kernel, dims),
        out_shape=tuple(pltpu.VMEM(dims_of, kind) for dims_of, kind in results),
        in_specs=[vmem] * 9,
        out_specs=(vmem,) * 6,
        scratch_shapes=[
            pltpu.VMEM((cells, 4 * hp, SPAN), F32),
            pltpu.VMEM((cells, SPAN, SPAN), F32),
            pltpu.VMEM((blocks, SPAN, SPAN), BF16),
            pltpu.VMEM((parts, SPAN, 4 * CHUNK), BF16),
            pltpu.VMEM((blocks, SPAN, 2 * SPAN), BF16),
            pltpu.VMEM((blocks, SPAN, 2 * SPAN), BF16),
            pltpu.VMEM((blocks, SPAN, 2 * SPAN), BF16),
            pltpu.VMEM((blocks, SPAN, 2 * SPAN), BF16),
            pltpu.VMEM((blocks, SPAN, SPAN), F32),
            pltpu.VMEM((blocks, SPAN, SPAN), F32),
            pltpu.VMEM((parts, 8, CHUNK), F32),
            pltpu.VMEM((parts, 2, blocks, CHUNK), F32),
            pltpu.VMEM((parts, 4, blocks, CHUNK), F32),
            pltpu.VMEM((parts, 2, EXTRA, CHUNK), F32),
            pltpu.VMEM((cells, CHUNK, SPAN), BF16),
            pltpu.VMEM((4, blocks + 1, SPAN, width), F32),
            pltpu.VMEM((cells, SPAN, CHUNK), F32),
            pltpu.VMEM((cells, CHUNK, SPAN), F32),
            pltpu.VMEM((blocks, SPAN, SPAN), F32),
            pltpu.VMEM((blocks, SPAN, SPAN), F32),
            pltpu.VMEM((cells, 2 * hp, SPAN), F32),
            pltpu.VMEM((blocks, SPAN, SPAN), F32),
            pltpu.VMEM((cells, 4 * hp, SPAN), F32),
            pltpu.VMEM((2, messages, wide_rows, PIECE), F32),
            pltpu.VMEM((messages, wide_rows, PIECE), F32),
            pltpu.VMEM((messages, wide_rows, PIECE), F32),
            pltpu.VMEM((messages, wide_rows, PIECE), F32),
            pltpu.VMEM((2, messages, wide_rows, PIECE), F32),
            pltpu.VMEM((messages, wide_rows, PIECE), F32),
            pltpu.VMEM((messages, wide_rows, PIECE), F32),
        ]
        + [pltpu.SemaphoreType.DMA((messages,))] * 9,
        compiler_params=pltpu.CompilerParams(
            collective_id=0, has_side_effects=True, vmem_limit_bytes=58 * 1024 * 1024
        ),
    )(
        features, cotangent, write_map, read_map, step_raw.T, tokens.reshape(blocks, SPAN),
        base_shift, decay_rate.reshape(1, heads), skip_gain.reshape(1, heads),
    )
    anywhere = pl.BlockSpec(memory_space=pl.ANY)
    mixed, grad_x, grad_b, grad_c, grad_s, gains = pl.pallas_call(
        write_out,
        out_shape=tuple(jax.ShapeDtypeStruct(dims_of, kind) for dims_of, kind in results),
        in_specs=[anywhere] * 6,
        out_specs=(anywhere,) * 6,
        scratch_shapes=[pltpu.SemaphoreType.DMA((6,))],
        compiler_params=pltpu.CompilerParams(vmem_limit_bytes=1024 * 1024),
    )(*outs)
    return mixed, grad_x, grad_b, grad_c, grad_s.T, gains.reshape(heads)


def solution(mesh):
    split = P(("groups", "ctx"), None)
    return jax.shard_map(
        per_device,
        mesh=mesh,
        in_specs=(split, split, split, split, P(("groups", "ctx")), P(), P(), P(), split),
        out_specs=(split, split, split, split, split, P("groups")),
        check_vma=False,
    )
```

```python
import functools
import math

import jax
import jax.numpy as jnp
from jax import lax
from jax.experimental import pallas as pl
from jax.experimental.pallas import tpu as pltpu
from jax.sharding import PartitionSpec as P

F32 = jnp.float32
BF16 = jnp.bfloat16
EXACT = lax.Precision.HIGHEST
SPAN = 128
CHUNK = 256
EXTRA = 8
PIECE = 128
PER = 2 * CHUNK // PIECE
LOG2E = 1.4426950408889634
MESH = pl.DeviceIdType.MESH

NN = (((1,), (0,)), ((), ()))
NT = (((1,), (1,)), ((), ()))
TN = (((0,), (0,)), ((), ()))


def mm(a, b, dims=NN):
    return lax.dot_general(a, b, dims, preferred_element_type=F32)


def exact(a, b, dims=NN):
    return lax.dot_general(a, b, dims, precision=EXACT, preferred_element_type=F32)


def pieces(v):
    high = v.astype(BF16)
    return high, (v - high.astype(F32)).astype(BF16)


def iota(shape, dim):
    return lax.broadcasted_iota(jnp.int32, shape, dim)


def log1p_unit(z):
    s = z / (z + 2.0)
    q = s * s
    acc = jnp.full_like(q, 1.0 / 19.0)
    for k in range(8, -1, -1):
        acc = acc * q + 1.0 / (2 * k + 1)
    return 2.0 * s * acc


def kernel(
    dims,
    x_ref, y_ref, b_ref, c_ref, raw_ref, tok_ref, base_ref, rate_ref, gain_ref,
    out_ref, gx_ref, gb_ref, gc_ref, gs_ref, gg_ref,
    rowp, cols, wcol, spread, bt2, ct2, bb2, cc2, gmat, dmat, gwide, fades, wts, whole, turn,
    loc, iy, ix, gca, gba, csum, rsum, psum,
    zone, zsib, ein, eout, ent, zpair, esib,
    zs_send, zs_recv, ch_send, ch_recv, ot_send, ot_recv, zp_send, zp_recv, mt_send,
):
    heads, count, blocks, parts, messages = dims
    size = CHUNK // heads_per(dims)
    hp = heads_per(dims)
    rows = blocks * SPAN
    width = parts * CHUNK
    wide_rows = SPAN + EXTRA

    group = lax.axis_index("groups")
    me = lax.axis_index("ctx")
    core = lax.rem(me, 2)
    chip = me // 2
    chips = count // 2
    mine = 1 - core
    step = 2 * core - 1
    odd = lax.rem(chip, 2)
    second = odd == core
    pairs = chips // 2
    place = jnp.where(core == 1, chip // 2, pairs - 1 - chip // 2)
    first, last = place == 0, place == pairs - 1
    sibling = me + 1 - 2 * core
    mate = me + 2 - 4 * odd
    after = jnp.clip(me + 4 * step, 0, count - 1)
    before = jnp.clip(me - 4 * step, 0, count - 1)
    has_after = second & jnp.logical_not(last)
    has_before = second & jnp.logical_not(first)
    alone = second & last

    barrier = pltpu.get_barrier_semaphore()
    pl.semaphore_signal(barrier, inc=1, device_id=(group, sibling), device_id_type=MESH)
    pl.semaphore_signal(barrier, inc=1, device_id=(group, mate), device_id_type=MESH)

    @pl.when(has_after)
    def _():
        pl.semaphore_signal(barrier, inc=1, device_id=(group, after), device_id_type=MESH)

    @pl.when(has_before)
    def _():
        pl.semaphore_signal(barrier, inc=1, device_id=(group, before), device_id_type=MESH)

    pl.semaphore_wait(barrier, 2 + has_after.astype(jnp.int32) + has_before.astype(jnp.int32))

    eye = (iota((heads, heads), 0) == iota((heads, heads), 1)).astype(F32)
    anti = (iota((heads, heads), 0) + iota((heads, heads), 1) == heads - 1).astype(F32)
    raw_t = raw_ref[...]
    base_f = exact(eye, base_ref[...], NT)
    base_r = exact(anti, base_ref[...], NT)
    rate_f = exact(eye, jnp.broadcast_to(rate_ref[...], (8, heads)), NT)[:, :1]
    rate_r = exact(anti, jnp.broadcast_to(rate_ref[...], (8, heads)), NT)[:, :1]
    gain_row = gain_ref[...] + exact(jnp.broadcast_to(gain_ref[...], (8, heads)), anti)[:1]
    gain_col = exact(eye, jnp.broadcast_to(gain_row, (8, heads)), NT)[:, :1]

    def stacked(make):
        return jnp.concatenate([make(k) for k in range(blocks)], axis=0)

    def logits(k, base, pair):
        tok = tok_ref[k : k + 1, :]
        value = raw_t[:, k * SPAN : (k + 1) * SPAN]
        for code in range(5):
            col = pair[code]
            value = value + jnp.where(tok == code, base[:, col : col + 1], 0.0)
        return value

    vf = stacked(lambda k: logits(k, base_f, (0, 1, 2, 3, 4)))
    vr = stacked(lambda k: logits(k, base_r, (3, 2, 1, 0, 4)))

    def steps_of(v):
        z = jnp.exp(-jnp.abs(v))
        s = jnp.maximum(v, 0.0) + log1p_unit(z)
        inv = 1.0 / (1.0 + z)
        return s, jnp.where(v >= 0.0, inv, z * inv)

    sf, slope_f = steps_of(vf)
    sr, slope_r = steps_of(vr)
    rates_f = jnp.concatenate([rate_f] * blocks, axis=0)
    rates_r = jnp.concatenate([rate_r] * blocks, axis=0)
    t_pos = iota((SPAN, SPAN), 0)
    s_pos = iota((SPAN, SPAN), 1)
    ahead_sum = (t_pos <= s_pos).astype(F32)
    behind_sum = (t_pos >= s_pos).astype(F32)
    nf = exact(sf * (rates_f * -LOG2E), ahead_sum)
    nr = exact(sr * (rates_r * -LOG2E), behind_sum)
    end_f, end_r = nf[:, SPAN - 1 :], nr[:, :1]
    ef, er = jnp.exp2(nf), jnp.exp2(nr)
    wf, wr = jnp.exp2(end_f - nf) * sf, jnp.exp2(end_r - nr) * sr
    mf, mr = nf - jnp.log2(sf), nr - jnp.log2(sr)
    both_log = jnp.log2(sf + sr)

    lane = iota((SPAN, SPAN), 1)
    ends_at_last, ends_at_first = [], []
    for k in range(blocks):
        at = slice(k * heads, (k + 1) * heads)
        four = jnp.concatenate([ef[at], wr[at], er[at], wf[at]] * 2, axis=0)
        turned = four.T
        high, low = pieces(turned)
        joint = jnp.where(lane < 4 * heads, high.astype(F32), low.astype(F32))
        wcol[k] = joint.astype(BF16)
        ends_at_last.append(joint[SPAN - 1 :])
        ends_at_first.append(joint[:1])
        order = []
        for c in range(parts):
            sub = slice(k * heads + c * hp, k * heads + (c + 1) * hp)
            order += [nf[sub], nr[sub]]
            rowp[k * parts + c] = jnp.concatenate([mf[sub], mr[sub], both_log[sub], both_log[sub]], axis=0)
        pad = [jnp.zeros((SPAN - 2 * heads, SPAN), F32)]
        turned = jnp.concatenate(order + pad, axis=0).T
        for c in range(parts):
            cols[k * parts + c, :, 0 : 2 * hp] = turned[:, 2 * hp * c : 2 * hp * (c + 1)]
        here = slice(k * SPAN, (k + 1) * SPAN)
        bk, ck = b_ref[here, :], c_ref[here, :]
        bkt, ckt = bk.T, ck.T
        bt2[k] = jnp.concatenate([bkt, bkt], axis=1)
        ct2[k] = jnp.concatenate([ckt, ckt], axis=1)
        bb2[k] = jnp.concatenate([bk, bk], axis=1)
        cc2[k] = jnp.concatenate([ck, ck], axis=1)
        gmat[k] = mm(ck, bk, NT)
        dmat[k] = jnp.zeros((SPAN, SPAN), F32)
        gca[k] = jnp.zeros((SPAN, SPAN), F32)
        gba[k] = jnp.zeros((SPAN, SPAN), F32)
        rsum[k] = jnp.zeros((SPAN, SPAN), F32)

    for c in range(parts):
        r = iota((SPAN, 4 * CHUNK), 0)
        j = iota((SPAN, 4 * CHUNK), 1)
        rr = lax.rem(r, 4 * heads)
        hit = (rr // heads == j // CHUNK) & (lax.rem(rr, heads) == c * hp + lax.rem(j, CHUNK) // size)
        spread[c] = hit.astype(F32).astype(BF16)
        hw = iota((heads, CHUNK), 0) == c * hp + iota((heads, CHUNK), 1) // size
        gwide[c] = exact(jnp.broadcast_to(gain_row, (8, heads)), hw.astype(F32))
        fade_f = mm(jnp.concatenate(ends_at_last, axis=0).astype(BF16), spread[c, :, :CHUNK])
        fade_r = mm(jnp.concatenate(ends_at_first, axis=0).astype(BF16), spread[c, :, 2 * CHUNK : 3 * CHUNK])
        fades[c, 0], fades[c, 1] = fade_f, fade_r
        for row, fade in ((0, fade_f), (1, fade_r)):
            run = jnp.ones((1, CHUNK), F32)
            for k in range(blocks):
                wts[c, row, k : k + 1, :] = run
                run = run * fade[k : k + 1]
            whole[c, row] = jnp.broadcast_to(run, (EXTRA, CHUNK))
            run = jnp.ones((1, CHUNK), F32)
            for k in range(blocks - 1, -1, -1):
                wts[c, row + 2, k : k + 1, :] = run
                run = run * fade[k : k + 1]

    def zone_copy(m):
        return pltpu.make_async_remote_copy(
            src_ref=zone.at[1 - mine, m], dst_ref=zsib.at[m],
            send_sem=zs_send.at[m], recv_sem=zs_recv.at[m],
            device_id=(group, sibling), device_id_type=MESH,
        )

    def chain_copy(m):
        return pltpu.make_async_remote_copy(
            src_ref=eout.at[m], dst_ref=ein.at[m],
            send_sem=ch_send.at[m], recv_sem=ch_recv.at[m],
            device_id=(group, after), device_id_type=MESH,
        )

    def remote(source, target, m, send, recv, device):
        return pltpu.make_async_remote_copy(
            src_ref=source, dst_ref=target, send_sem=send.at[m], recv_sem=recv.at[m],
            device_id=(group, device), device_id_type=MESH,
        )

    def pass_on(m):
        return remote(ein.at[m], ent.at[mine, m], m, ot_send, ot_recv, sibling)

    def give(m):
        return remote(esib.at[m], ent.at[mine, m], m, ot_send, ot_recv, sibling)

    def pair_copy(m):
        return remote(eout.at[m], zpair.at[m], m, zp_send, zp_recv, mate)

    def mate_copy(m):
        return remote(ein.at[m], ein.at[m], m, mt_send, ch_recv, mate)

    top, fine = 2.0 ** grid_bits(dims), 2.0 ** (grid_bits(dims) + 21)
    finest = 2.0 ** (grid_bits(dims) + 42)
    one_row = iota((EXTRA, CHUNK), 0)

    is_state = iota((wide_rows, PIECE), 0) < SPAN

    def over(near, value):
        return near + jnp.where(is_state, near[SPAN : SPAN + 1], 1.0) * value

    def join_step(m):
        zone_copy(m).wait_recv()
        near, own = zsib[m], zone[mine, m]
        eout[m] = over(own, near)
        eout[m, SPAN : SPAN + 1, :] = own[SPAN : SPAN + 1] * near[SPAN : SPAN + 1]
        pair_copy(m).start()

    def chain_step(m):
        @pl.when(first)
        def _():
            ein[m] = jnp.zeros((wide_rows, PIECE), F32)

        @pl.when(jnp.logical_not(first))
        def _():
            chain_copy(m).wait_recv()

        @pl.when(jnp.logical_not(second))
        def _():
            @pl.when(jnp.logical_not(first))
            def _():
                pass_on(m).start()

            ent[mine, m] = over(zsib[m], ein[m])

        @pl.when(second)
        def _():
            @pl.when(jnp.logical_not(first))
            def _():
                mate_copy(m).start()

            zone_copy(m).wait_recv()
            pair_copy(m).wait_recv()
            theirs = over(zpair[m], ein[m])
            esib[m] = theirs
            give(m).start()
            entry = over(zsib[m], theirs)
            ent[mine, m] = entry

            @pl.when(jnp.logical_not(last))
            def _():
                eout[m] = over(zone[mine, m], entry)
                chain_copy(m).start()

    zone_ticks, join_tick, cells = 8, 5, blocks * parts
    chain_tick = 14 + 12 * place + jnp.where(second, 0, 12)

    def due(m):
        return zone_ticks * (m // PER) + chain_tick + lax.rem(m, PER)

    def tick(t, least, joins):
        def run(late, allowed, do):
            m = PER * (late // zone_ticks) + lax.rem(late, zone_ticks)

            @pl.when(allowed & (late >= 0) & (lax.rem(late, zone_ticks) < PER) & (m >= least) & (m < messages))
            def _():
                do(m)

        if joins:
            run(t - join_tick, jnp.logical_not(second), join_step)
        run(t - chain_tick, True, chain_step)

    @pl.loop(0, parts)
    def _(c):
        at_w = pl.ds(pl.multiple_of(c * CHUNK, CHUNK), CHUNK)

        zero = jnp.zeros((SPAN, CHUNK), F32)
        loc[0, 0, :, at_w] = zero
        loc[1, 0, :, at_w] = zero
        loc[2, blocks, :, at_w] = zero
        loc[3, blocks, :, at_w] = zero

        def products(k, dot_xy):
            n = blocks - 1 - k
            at_k = pl.ds(pl.multiple_of(k * SPAN, SPAN), SPAN)
            at_n = pl.ds(pl.multiple_of(n * SPAN, SPAN), SPAN)
            x = x_ref[at_k, at_w].astype(F32)
            y = y_ref[at_k, at_w].astype(F32)
            turn[k * parts + c] = y.T.astype(BF16)
            wides = mm(wcol[k], spread[c, :, 2 * CHUNK :])
            xf = jnp.concatenate(pieces(wides[:, CHUNK:] * x), axis=0)
            yr = jnp.concatenate(pieces(wides[:, :CHUNK] * y), axis=0)
            fade_f = fades[c, 0, pl.ds(k, 1), :]
            fade_r = fades[c, 1, pl.ds(k, 1), :]
            loc[0, k + 1, :, at_w] = fade_f * loc[0, k, :, at_w] + mm(bt2[k], xf)
            loc[1, k + 1, :, at_w] = fade_r * loc[1, k, :, at_w] + mm(ct2[k], yr)
            wides = mm(wcol[n], spread[c, :, : 2 * CHUNK])
            yf = jnp.concatenate(pieces(wides[:, :CHUNK] * y_ref[at_n, at_w].astype(F32)), axis=0)
            xr = jnp.concatenate(pieces(wides[:, CHUNK:] * x_ref[at_n, at_w].astype(F32)), axis=0)
            fade_f = fades[c, 0, pl.ds(n, 1), :]
            fade_r = fades[c, 1, pl.ds(n, 1), :]
            loc[2, n, :, at_w] = fade_f * loc[2, n + 1, :, at_w] + mm(ct2[n], yf)
            loc[3, n, :, at_w] = fade_r * loc[3, n + 1, :, at_w] + mm(bt2[n], xr)
            return dot_xy + jnp.sum((x * y).reshape(SPAN // 8, 8, CHUNK), axis=0)

        dot_xy = lax.fori_loop(0, blocks, products, jnp.zeros((8, CHUNK), F32), unroll=4)

        dot_row = jnp.sum(dot_xy, axis=0, keepdims=True)
        coarse = jnp.round(dot_row * top) * (1.0 / top)
        rest = dot_row - coarse
        middle = jnp.round(rest * fine) * (1.0 / fine)
        small = jnp.round((rest - middle) * finest) * (1.0 / finest)

        def put(flow, comp, value, g):
            tail = jnp.where(
                one_row == 0, g,
                jnp.where(one_row == 1, coarse, jnp.where(one_row == 2, middle, jnp.where(one_row == 3, small, 0.0))),
            )
            for j in range(CHUNK // PIECE):
                m = c * PER + comp * (CHUNK // PIECE) + j
                zone[flow, m, 0:SPAN, :] = value[:, j * PIECE : (j + 1) * PIECE]
                zone[flow, m, SPAN:, :] = tail[:, j * PIECE : (j + 1) * PIECE]

        put(0, 0, loc[0, blocks, :, at_w], whole[c, 0])
        put(0, 1, loc[1, blocks, :, at_w], whole[c, 1])
        put(1, 0, loc[2, 0, :, at_w], whole[c, 0])
        put(1, 1, loc[3, 0, :, at_w], whole[c, 1])
        for j in range(PER):
            zone_copy(PER * c + j).start()

        @pl.loop(0, zone_ticks)
        def _(t):
            tick(zone_ticks * c + t, 0, True)

    low = t_pos > s_pos
    diag = t_pos == s_pos
    half = iota((SPAN, SPAN), 1) < size

    def inner(i):
        c, k = i // blocks, lax.rem(i, blocks)
        at_r = pl.ds(pl.multiple_of(k * SPAN, SPAN), SPAN)
        g = gmat[k]
        col = cols[k * parts + c]
        row = rowp[k * parts + c]
        d_sum = jnp.zeros((SPAN, SPAN), F32)
        left = jnp.zeros((SPAN, SPAN), F32)
        lows, diags = [], []
        for p in range(CHUNK // SPAN):
            at_w = pl.ds(pl.multiple_of(c * CHUNK + p * SPAN, SPAN), SPAN)
            x, y = x_ref[at_r, at_w], y_ref[at_r, at_w]
            tall, wide = [], []
            firsts = jnp.where(half, y.astype(F32), 0.0).astype(BF16)
            seconds = jnp.where(half, 0.0, y.astype(F32)).astype(BF16)
            crossed = mm(jnp.concatenate([firsts, seconds], axis=0), x, NT)
            for q in range(SPAN // size):
                h = p * (SPAN // size) + q
                fall = col[:, h : h + 1] - row[h : h + 1]
                rise = col[:, hp + h : hp + h + 1] - row[hp + h : hp + h + 1]
                mid = row[2 * hp + h : 2 * hp + h + 1]
                w = jnp.exp2(jnp.where(low, fall, jnp.where(diag, mid, rise)))
                cross = crossed[q * SPAN : (q + 1) * SPAN]
                wg = w * g
                d_sum = d_sum + cross * w
                pull = jnp.where(low, cross * wg, 0.0)
                lows.append(jnp.sum(pull, axis=0, keepdims=True))
                left = jnp.where(lane == c * hp + h, jnp.sum(pull, axis=1, keepdims=True), left)
                diags.append(jnp.sum(jnp.where(diag, cross, 0.0), axis=0, keepdims=True))
                w_h, w_l = pieces(wg)
                tall.append(jnp.concatenate([w_h, w_l], axis=1))
                y_t = turn[k * parts + c, h * size : (h + 1) * size, :]
                ix[k * parts + c, h * size : (h + 1) * size, :] = mm(
                    jnp.concatenate([y_t, y_t], axis=1), jnp.concatenate([w_h, w_l], axis=0)
                )
            both_y = mm(jnp.concatenate(tall, axis=0), jnp.concatenate([x, x], axis=0))
            iy[k * parts + c, :, p * SPAN : (p + 1) * SPAN] = jnp.where(half, both_y[:SPAN], both_y[SPAN:])
        dmat[k] += d_sum
        csum[k * parts + c] = jnp.concatenate(lows + diags, axis=0)
        rsum[k] += left

    first_tick = zone_ticks * parts

    @pl.loop(0, cells // 2)
    def _(i):
        for j in range(2):
            inner(2 * i + j)
        for j in range(2):
            tick(first_tick + 2 * i + j, 0, True)

    def side(array, flow, c, comp, low_row, high_row):
        m = PER * c + comp * (CHUNK // PIECE)
        return jnp.concatenate([array[flow, m + j, low_row:high_row, :] for j in range(CHUNK // PIECE)], axis=1)

    head_row = iota((8, CHUNK), 0) == iota((8, CHUNK), 1) // size
    pick = head_row.astype(F32)

    @pl.loop(0, parts)
    def _(c):
        at_w = pl.ds(pl.multiple_of(c * CHUNK, CHUNK), CHUNK)
        began = first_tick + cells + blocks * c
        for j in range(PER):
            m = PER * c + j

            @pl.when(due(m) >= began)
            def _():
                chain_step(m)

        for j in range(PER):
            m = PER * c + j

            @pl.when(alone)
            def _():
                ent[1 - mine, m] = jnp.zeros((wide_rows, PIECE), F32)

            @pl.when(jnp.logical_not(alone))
            def _():
                give(m).wait_recv()

        def finish(k):
            at_r = pl.ds(pl.multiple_of(k * SPAN, SPAN), SPAN)
            at = k * parts + c
            x = x_ref[at_r, at_w].astype(F32)
            y = y_ref[at_r, at_w].astype(F32)
            wides = mm(wcol[k], spread[c])
            ef_w, wr_w = wides[:, :CHUNK], wides[:, CHUNK : 2 * CHUNK]
            er_w, wf_w = wides[:, 2 * CHUNK : 3 * CHUNK], wides[:, 3 * CHUNK :]

            def entered(slot, row, flow, comp):
                return pieces(
                    loc[slot, k + flow, :, at_w] + wts[c, row, pl.ds(k, 1), :] * side(ent, flow, c, comp, 0, SPAN)
                )

            sf_h, sf_l = entered(0, 0, 0, 0)
            ar_h, ar_l = entered(1, 1, 0, 1)
            af_h, af_l = entered(2, 2, 1, 0)
            sr_h, sr_l = entered(3, 3, 1, 1)
            cat = lambda *v: jnp.concatenate(v, axis=0)
            v_f = mm(cc2[k], cat(sf_h, sf_l))
            v_r = mm(cc2[k], cat(sr_h, sr_l))
            u_f = mm(bb2[k], cat(af_h, af_l))
            u_r = mm(bb2[k], cat(ar_h, ar_l))
            gain = gwide[c, 0:1]
            yf, yr, xf, xr = ef_w * y, er_w * y, wf_w * x, wr_w * x
            mixed = iy[at] + ef_w * v_f + er_w * v_r + gain * x
            grad_x = ix[at].T + wf_w * u_f + wr_w * u_r + gain * y
            out_ref[at_r, at_w] = mixed.astype(BF16)
            gx_ref[at_r, at_w] = grad_x.astype(BF16)

            def joined(a, ah_al, b, bh_bl):
                a_h, a_l = pieces(a)
                b_h, b_l = pieces(b)
                left = jnp.concatenate([a_h, a_h, a_l, b_h, b_h, b_l], axis=1)
                right = jnp.concatenate(
                    [ah_al[0], ah_al[1], ah_al[0], bh_bl[0], bh_bl[1], bh_bl[0]], axis=1
                )
                return mm(left, right, NT)

            gca[k] += joined(yf, (sf_h, sf_l), yr, (sr_h, sr_l))
            gba[k] += joined(xf, (af_h, af_l), xr, (ar_h, ar_l))

            def narrow(v):
                turned = v.T
                return jnp.concatenate(
                    [jnp.sum(turned[j * size : (j + 1) * size], axis=0, keepdims=True) for j in range(hp)], axis=0
                )

            psum[at, 0:hp] = narrow(yf * v_f)
            psum[at, hp : 2 * hp] = narrow(xf * u_f)
            psum[at, 2 * hp : 3 * hp] = narrow(y * mixed)
            psum[at, 3 * hp : 4 * hp] = narrow(x * grad_x)

        @pl.loop(0, blocks // 2)
        def _(i):
            for j in range(2):
                finish(2 * i + j)
            for j in range(2):
                tick(began + 2 * i + j, PER * c + PER, False)

    def gathered(make):
        out = []
        for k in range(blocks):
            for c in range(parts):
                out.append(make(k, c))
        return jnp.concatenate(out, axis=0)

    def sums(first_row):
        return gathered(lambda k, c: psum[k * parts + c, first_row : first_row + hp])

    row_low = stacked(lambda k: rsum[k].T[0:heads])
    col_low = gathered(lambda k, c: csum[k * parts + c, 0:hp])
    both = gathered(lambda k, c: csum[k * parts + c, hp : 2 * hp])
    center = stacked(
        lambda k: jnp.broadcast_to(
            jnp.sum(jnp.where(diag, gmat[k], 0.0), axis=0, keepdims=True), (heads, SPAN)
        )
    )
    ends_f, ends_r, gains = [], [], []
    for c in range(parts):
        for flow, comp, opp_flow, opp_comp, into in ((0, 0, 1, 0, ends_f), (1, 1, 0, 1, ends_r)):
            own = side(zone, flow, c, comp, 0, SPAN)
            faded = side(zone, flow, c, comp, SPAN, wide_rows)[:1] * side(ent, flow, c, comp, 0, SPAN)
            held = exact(pick, (own + faded) * side(ent, opp_flow, c, opp_comp, 0, SPAN), NT)
            into.append(jnp.sum(held, axis=1, keepdims=True)[0:hp])
        total = side(ent, 0, c, 0, SPAN, wide_rows) + (
            side(zone, 0, c, 0, SPAN, wide_rows) + side(ent, 1, c, 0, SPAN, wide_rows)
        )
        row = total[1:2] + (total[2:3] + total[3:4])
        spots = (iota((CHUNK, heads), 1) == c * hp + iota((CHUNK, heads), 0) // size).astype(F32)
        gains.append(exact(jnp.broadcast_to(row, (8, CHUNK)), spots))
    gain_sum = sum(gains)
    gg_ref[...] = ((gain_sum + exact(gain_sum, anti)) * (1.0 / math.sqrt(rows * count * size)))[:1]

    gain_all = jnp.concatenate([gain_col] * blocks, axis=0)
    own_terms = (gain_all + (sf + sr) * center) * both
    row_f = row_low + sums(0 * hp)
    col_f = col_low + sums(hp)
    row_r = sums(2 * hp) - own_terms - row_f
    col_r = sums(3 * hp) - own_terms - col_f
    mid = center * both
    diff_f, diff_r = col_f - row_f, col_r - row_r
    tail_f = exact(diff_f, behind_sum)
    head_r = exact(diff_r, ahead_sum)
    later, earlier = [None] * blocks, [None] * blocks
    run = -jnp.concatenate(ends_f, axis=0)
    for k in range(blocks - 1, -1, -1):
        at = slice(k * heads, (k + 1) * heads)
        later[k] = run
        run = run + tail_f[at, :1]
    run = -jnp.concatenate(ends_r, axis=0)
    for k in range(blocks):
        at = slice(k * heads, (k + 1) * heads)
        earlier[k] = run
        run = run + head_r[at, SPAN - 1 :]
    drop_f = tail_f + jnp.concatenate(later, axis=0)
    drop_r = head_r + jnp.concatenate(earlier, axis=0)
    d_f = col_f / sf + mid + rates_f * drop_f
    d_r = col_r / sr + mid + rates_r * drop_r
    grad_s = d_f * slope_f + d_r * slope_r
    for k in range(blocks):
        here = slice(k * SPAN, (k + 1) * SPAN)
        gs_ref[:, here] = grad_s[k * heads : (k + 1) * heads]
        d_h, d_l = pieces(dmat[k])
        gc_ref[here, :] = (gca[k] + mm(jnp.concatenate([d_h, d_l], axis=1), jnp.concatenate([b_ref[here, :]] * 2, axis=0))).astype(BF16)
        gb_ref[here, :] = (gba[k] + mm(jnp.concatenate([d_h, d_l], axis=0), jnp.concatenate([c_ref[here, :]] * 2, axis=0), TN)).astype(BF16)

    @pl.loop(0, messages)
    def _(m):
        zone_copy(m).wait_send()

        @pl.when(second)
        def _():
            give(m).wait_send()

            @pl.when(jnp.logical_not(first))
            def _():
                mate_copy(m).wait_send()

            @pl.when(jnp.logical_not(last))
            def _():
                chain_copy(m).wait_send()

        @pl.when(jnp.logical_not(second))
        def _():
            pair_copy(m).wait_send()

            @pl.when(jnp.logical_not(first))
            def _():
                pass_on(m).wait_send()


def write_out(*refs):
    sems = refs[-1]
    copies = [pltpu.make_async_copy(refs[i], refs[6 + i], sems.at[i]) for i in range(6)]
    for copy in copies:
        copy.start()
    for copy in copies:
        copy.wait()


def heads_per(dims):
    return dims[0] // dims[3]


def grid_bits(dims):
    limit = 120 * dims[2] * SPAN * dims[1]
    return 23 - math.ceil(math.log2(limit))


def per_device(
    features, write_map, read_map, step_raw, tokens, base_shift, decay_rate, skip_gain, cotangent
):
    rows, width = features.shape
    state = write_map.shape[1]
    heads = decay_rate.shape[0]
    count = lax.axis_size("ctx")
    blocks, parts = rows // SPAN, width // CHUNK
    messages = PER * parts
    dims = (heads, count, blocks, parts, messages)
    hp = heads // parts
    cells = blocks * parts
    wide_rows = SPAN + EXTRA
    vmem = pl.BlockSpec(memory_space=pltpu.VMEM)
    results = (
        ((rows, width), BF16),
        ((rows, width), BF16),
        ((rows, state), BF16),
        ((rows, state), BF16),
        ((heads, rows), F32),
        ((1, heads), F32),
    )
    outs = pl.pallas_call(
        functools.partial(kernel, dims),
        out_shape=tuple(pltpu.VMEM(dims_of, kind) for dims_of, kind in results),
        in_specs=[vmem] * 9,
        out_specs=(vmem,) * 6,
        scratch_shapes=[
            pltpu.VMEM((cells, 4 * hp, SPAN), F32),
            pltpu.VMEM((cells, SPAN, SPAN), F32),
            pltpu.VMEM((blocks, SPAN, SPAN), BF16),
            pltpu.VMEM((parts, SPAN, 4 * CHUNK), BF16),
            pltpu.VMEM((blocks, SPAN, 2 * SPAN), BF16),
            pltpu.VMEM((blocks, SPAN, 2 * SPAN), BF16),
            pltpu.VMEM((blocks, SPAN, 2 * SPAN), BF16),
            pltpu.VMEM((blocks, SPAN, 2 * SPAN), BF16),
            pltpu.VMEM((blocks, SPAN, SPAN), F32),
            pltpu.VMEM((blocks, SPAN, SPAN), F32),
            pltpu.VMEM((parts, 8, CHUNK), F32),
            pltpu.VMEM((parts, 2, blocks, CHUNK), F32),
            pltpu.VMEM((parts, 4, blocks, CHUNK), F32),
            pltpu.VMEM((parts, 2, EXTRA, CHUNK), F32),
            pltpu.VMEM((cells, CHUNK, SPAN), BF16),
            pltpu.VMEM((4, blocks + 1, SPAN, width), F32),
            pltpu.VMEM((cells, SPAN, CHUNK), F32),
            pltpu.VMEM((cells, CHUNK, SPAN), F32),
            pltpu.VMEM((blocks, SPAN, SPAN), F32),
            pltpu.VMEM((blocks, SPAN, SPAN), F32),
            pltpu.VMEM((cells, 2 * hp, SPAN), F32),
            pltpu.VMEM((blocks, SPAN, SPAN), F32),
            pltpu.VMEM((cells, 4 * hp, SPAN), F32),
            pltpu.VMEM((2, messages, wide_rows, PIECE), F32),
            pltpu.VMEM((messages, wide_rows, PIECE), F32),
            pltpu.VMEM((messages, wide_rows, PIECE), F32),
            pltpu.VMEM((messages, wide_rows, PIECE), F32),
            pltpu.VMEM((2, messages, wide_rows, PIECE), F32),
            pltpu.VMEM((messages, wide_rows, PIECE), F32),
            pltpu.VMEM((messages, wide_rows, PIECE), F32),
        ]
        + [pltpu.SemaphoreType.DMA((messages,))] * 9,
        compiler_params=pltpu.CompilerParams(
            collective_id=0, has_side_effects=True, vmem_limit_bytes=58 * 1024 * 1024
        ),
    )(
        features, cotangent, write_map, read_map, step_raw.T, tokens.reshape(blocks, SPAN),
        base_shift, decay_rate.reshape(1, heads), skip_gain.reshape(1, heads),
    )
    anywhere = pl.BlockSpec(memory_space=pl.ANY)
    mixed, grad_x, grad_b, grad_c, grad_s, gains = pl.pallas_call(
        write_out,
        out_shape=tuple(jax.ShapeDtypeStruct(dims_of, kind) for dims_of, kind in results),
        in_specs=[anywhere] * 6,
        out_specs=(anywhere,) * 6,
        scratch_shapes=[pltpu.SemaphoreType.DMA((6,))],
        compiler_params=pltpu.CompilerParams(vmem_limit_bytes=1024 * 1024),
    )(*outs)
    return mixed, grad_x, grad_b, grad_c, grad_s.T, gains.reshape(heads)


def solution(mesh):
    split = P(("groups", "ctx"), None)
    return jax.shard_map(
        per_device,
        mesh=mesh,
        in_specs=(split, split, split, split, P(("groups", "ctx")), P(), P(), P(), split),
        out_specs=(split, split, split, split, split, P("groups")),
        check_vma=False,
    )
```

```python
import functools
import math

import jax
import jax.numpy as jnp
from jax import lax
from jax.experimental import pallas as pl
from jax.experimental.pallas import tpu as pltpu
from jax.sharding import PartitionSpec as P

F32 = jnp.float32
BF16 = jnp.bfloat16
EXACT = lax.Precision.HIGHEST
SPAN = 128
CHUNK = 256
EXTRA = 8
PIECE = 128
PER = 2 * CHUNK // PIECE
LOG2E = 1.4426950408889634
MESH = pl.DeviceIdType.MESH

NN = (((1,), (0,)), ((), ()))
NT = (((1,), (1,)), ((), ()))
TN = (((0,), (0,)), ((), ()))


def mm(a, b, dims=NN):
    return lax.dot_general(a, b, dims, preferred_element_type=F32)


def exact(a, b, dims=NN):
    return lax.dot_general(a, b, dims, precision=EXACT, preferred_element_type=F32)


def pieces(v):
    high = v.astype(BF16)
    return high, (v - high.astype(F32)).astype(BF16)


def iota(shape, dim):
    return lax.broadcasted_iota(jnp.int32, shape, dim)


def log1p_unit(z):
    s = z / (z + 2.0)
    q = s * s
    acc = jnp.full_like(q, 1.0 / 19.0)
    for k in range(8, -1, -1):
        acc = acc * q + 1.0 / (2 * k + 1)
    return 2.0 * s * acc


def kernel(
    dims,
    x_hbm, y_hbm, b_hbm, c_hbm, raw_ref, tok_ref, base_ref, rate_ref, gain_ref,
    out_ref, gx_ref, gb_ref, gc_ref, gs_ref, gg_ref,
    rowp, cols, wcol, spread, bt2, ct2, bb2, cc2, gmat, dmat, gwide, fades, wts, whole, turn,
    loc, iy, ix, gca, gba, csum, rsum, psum,
    zone, zsib, ein, eout, ent, zpair, esib, x_ref, y_ref, b_ref, c_ref, in_sems,
    zs_send, zs_recv, ch_send, ch_recv, ot_send, ot_recv, zp_send, zp_recv, mt_send,
):
    heads, count, blocks, parts, messages = dims
    size = CHUNK // heads_per(dims)
    hp = heads_per(dims)
    rows = blocks * SPAN
    width = parts * CHUNK
    wide_rows = SPAN + EXTRA

    group = lax.axis_index("groups")
    me = lax.axis_index("ctx")
    core = lax.rem(me, 2)
    chip = me // 2
    chips = count // 2
    mine = 1 - core
    step = 2 * core - 1
    odd = lax.rem(chip, 2)
    second = odd == core
    pairs = chips // 2
    place = jnp.where(core == 1, chip // 2, pairs - 1 - chip // 2)
    first, last = place == 0, place == pairs - 1
    sibling = me + 1 - 2 * core
    mate = me + 2 - 4 * odd
    after = jnp.clip(me + 4 * step, 0, count - 1)
    before = jnp.clip(me - 4 * step, 0, count - 1)
    has_after = second & jnp.logical_not(last)
    has_before = second & jnp.logical_not(first)
    alone = second & last

    inputs = [
        pltpu.make_async_copy(source, target, in_sems.at[i])
        for i, (source, target) in enumerate(
            ((b_hbm, b_ref), (c_hbm, c_ref), (x_hbm, x_ref), (y_hbm, y_ref))
        )
    ]
    for copy in inputs:
        copy.start()

    barrier = pltpu.get_barrier_semaphore()
    pl.semaphore_signal(barrier, inc=1, device_id=(group, sibling), device_id_type=MESH)
    pl.semaphore_signal(barrier, inc=1, device_id=(group, mate), device_id_type=MESH)

    @pl.when(has_after)
    def _():
        pl.semaphore_signal(barrier, inc=1, device_id=(group, after), device_id_type=MESH)

    @pl.when(has_before)
    def _():
        pl.semaphore_signal(barrier, inc=1, device_id=(group, before), device_id_type=MESH)

    pl.semaphore_wait(barrier, 2 + has_after.astype(jnp.int32) + has_before.astype(jnp.int32))

    eye = (iota((heads, heads), 0) == iota((heads, heads), 1)).astype(F32)
    anti = (iota((heads, heads), 0) + iota((heads, heads), 1) == heads - 1).astype(F32)
    raw_t = raw_ref[...]
    base_f = exact(eye, base_ref[...], NT)
    base_r = exact(anti, base_ref[...], NT)
    rate_f = exact(eye, jnp.broadcast_to(rate_ref[...], (8, heads)), NT)[:, :1]
    rate_r = exact(anti, jnp.broadcast_to(rate_ref[...], (8, heads)), NT)[:, :1]
    gain_row = gain_ref[...] + exact(jnp.broadcast_to(gain_ref[...], (8, heads)), anti)[:1]
    gain_col = exact(eye, jnp.broadcast_to(gain_row, (8, heads)), NT)[:, :1]

    def stacked(make):
        return jnp.concatenate([make(k) for k in range(blocks)], axis=0)

    def logits(k, base, pair):
        tok = tok_ref[k : k + 1, :]
        value = raw_t[:, k * SPAN : (k + 1) * SPAN]
        for code in range(5):
            col = pair[code]
            value = value + jnp.where(tok == code, base[:, col : col + 1], 0.0)
        return value

    vf = stacked(lambda k: logits(k, base_f, (0, 1, 2, 3, 4)))
    vr = stacked(lambda k: logits(k, base_r, (3, 2, 1, 0, 4)))

    def steps_of(v):
        z = jnp.exp(-jnp.abs(v))
        s = jnp.maximum(v, 0.0) + log1p_unit(z)
        inv = 1.0 / (1.0 + z)
        return s, jnp.where(v >= 0.0, inv, z * inv)

    sf, slope_f = steps_of(vf)
    sr, slope_r = steps_of(vr)
    rates_f = jnp.concatenate([rate_f] * blocks, axis=0)
    rates_r = jnp.concatenate([rate_r] * blocks, axis=0)
    t_pos = iota((SPAN, SPAN), 0)
    s_pos = iota((SPAN, SPAN), 1)
    ahead_sum = (t_pos <= s_pos).astype(F32)
    behind_sum = (t_pos >= s_pos).astype(F32)
    nf = exact(sf * (rates_f * -LOG2E), ahead_sum)
    nr = exact(sr * (rates_r * -LOG2E), behind_sum)
    end_f, end_r = nf[:, SPAN - 1 :], nr[:, :1]
    ef, er = jnp.exp2(nf), jnp.exp2(nr)
    wf, wr = jnp.exp2(end_f - nf) * sf, jnp.exp2(end_r - nr) * sr
    mf, mr = nf - jnp.log2(sf), nr - jnp.log2(sr)
    both_log = jnp.log2(sf + sr)

    lane = iota((SPAN, SPAN), 1)
    ends_at_last, ends_at_first = [], []
    inputs[0].wait()
    inputs[1].wait()
    for k in range(blocks):
        at = slice(k * heads, (k + 1) * heads)
        four = jnp.concatenate([ef[at], wr[at], er[at], wf[at]] * 2, axis=0)
        turned = four.T
        high, low = pieces(turned)
        joint = jnp.where(lane < 4 * heads, high.astype(F32), low.astype(F32))
        wcol[k] = joint.astype(BF16)
        ends_at_last.append(joint[SPAN - 1 :])
        ends_at_first.append(joint[:1])
        order = []
        for c in range(parts):
            sub = slice(k * heads + c * hp, k * heads + (c + 1) * hp)
            order += [nf[sub], nr[sub]]
            rowp[k * parts + c] = jnp.concatenate([mf[sub], mr[sub], both_log[sub], both_log[sub]], axis=0)
        pad = [jnp.zeros((SPAN - 2 * heads, SPAN), F32)]
        turned = jnp.concatenate(order + pad, axis=0).T
        for c in range(parts):
            cols[k * parts + c, :, 0 : 2 * hp] = turned[:, 2 * hp * c : 2 * hp * (c + 1)]
        here = slice(k * SPAN, (k + 1) * SPAN)
        bk, ck = b_ref[here, :], c_ref[here, :]
        bkt, ckt = bk.T, ck.T
        bt2[k] = jnp.concatenate([bkt, bkt], axis=1)
        ct2[k] = jnp.concatenate([ckt, ckt], axis=1)
        bb2[k] = jnp.concatenate([bk, bk], axis=1)
        cc2[k] = jnp.concatenate([ck, ck], axis=1)
        gmat[k] = mm(ck, bk, NT)
        dmat[k] = jnp.zeros((SPAN, SPAN), F32)
        gca[k] = jnp.zeros((SPAN, SPAN), F32)
        gba[k] = jnp.zeros((SPAN, SPAN), F32)
        rsum[k] = jnp.zeros((SPAN, SPAN), F32)

    for c in range(parts):
        r = iota((SPAN, 4 * CHUNK), 0)
        j = iota((SPAN, 4 * CHUNK), 1)
        rr = lax.rem(r, 4 * heads)
        hit = (rr // heads == j // CHUNK) & (lax.rem(rr, heads) == c * hp + lax.rem(j, CHUNK) // size)
        spread[c] = hit.astype(F32).astype(BF16)
        hw = iota((heads, CHUNK), 0) == c * hp + iota((heads, CHUNK), 1) // size
        gwide[c] = exact(jnp.broadcast_to(gain_row, (8, heads)), hw.astype(F32))
        fade_f = mm(jnp.concatenate(ends_at_last, axis=0).astype(BF16), spread[c, :, :CHUNK])
        fade_r = mm(jnp.concatenate(ends_at_first, axis=0).astype(BF16), spread[c, :, 2 * CHUNK : 3 * CHUNK])
        fades[c, 0], fades[c, 1] = fade_f, fade_r
        for row, fade in ((0, fade_f), (1, fade_r)):
            run = jnp.ones((1, CHUNK), F32)
            for k in range(blocks):
                wts[c, row, k : k + 1, :] = run
                run = run * fade[k : k + 1]
            whole[c, row] = jnp.broadcast_to(run, (EXTRA, CHUNK))
            run = jnp.ones((1, CHUNK), F32)
            for k in range(blocks - 1, -1, -1):
                wts[c, row + 2, k : k + 1, :] = run
                run = run * fade[k : k + 1]

    def zone_copy(m):
        return pltpu.make_async_remote_copy(
            src_ref=zone.at[1 - mine, m], dst_ref=zsib.at[m],
            send_sem=zs_send.at[m], recv_sem=zs_recv.at[m],
            device_id=(group, sibling), device_id_type=MESH,
        )

    def chain_copy(m):
        return pltpu.make_async_remote_copy(
            src_ref=eout.at[m], dst_ref=ein.at[m],
            send_sem=ch_send.at[m], recv_sem=ch_recv.at[m],
            device_id=(group, after), device_id_type=MESH,
        )

    def remote(source, target, m, send, recv, device):
        return pltpu.make_async_remote_copy(
            src_ref=source, dst_ref=target, send_sem=send.at[m], recv_sem=recv.at[m],
            device_id=(group, device), device_id_type=MESH,
        )

    def pass_on(m):
        return remote(ein.at[m], ent.at[mine, m], m, ot_send, ot_recv, sibling)

    def give(m):
        return remote(esib.at[m], ent.at[mine, m], m, ot_send, ot_recv, sibling)

    def pair_copy(m):
        return remote(eout.at[m], zpair.at[m], m, zp_send, zp_recv, mate)

    def mate_copy(m):
        return remote(ein.at[m], ein.at[m], m, mt_send, ch_recv, mate)

    top, fine = 2.0 ** grid_bits(dims), 2.0 ** (grid_bits(dims) + 21)
    finest = 2.0 ** (grid_bits(dims) + 42)
    one_row = iota((EXTRA, CHUNK), 0)

    is_state = iota((wide_rows, PIECE), 0) < SPAN

    def over(near, value):
        return near + jnp.where(is_state, near[SPAN : SPAN + 1], 1.0) * value

    def join_step(m):
        zone_copy(m).wait_recv()
        near, own = zsib[m], zone[mine, m]
        eout[m] = over(own, near)
        eout[m, SPAN : SPAN + 1, :] = own[SPAN : SPAN + 1] * near[SPAN : SPAN + 1]
        pair_copy(m).start()

    def chain_step(m):
        @pl.when(first)
        def _():
            ein[m] = jnp.zeros((wide_rows, PIECE), F32)

        @pl.when(jnp.logical_not(first))
        def _():
            chain_copy(m).wait_recv()

        @pl.when(jnp.logical_not(second))
        def _():
            @pl.when(jnp.logical_not(first))
            def _():
                pass_on(m).start()

            ent[mine, m] = over(zsib[m], ein[m])

        @pl.when(second)
        def _():
            @pl.when(jnp.logical_not(first))
            def _():
                mate_copy(m).start()

            zone_copy(m).wait_recv()
            pair_copy(m).wait_recv()
            theirs = over(zpair[m], ein[m])
            esib[m] = theirs
            give(m).start()
            entry = over(zsib[m], theirs)
            ent[mine, m] = entry

            @pl.when(jnp.logical_not(last))
            def _():
                eout[m] = over(zone[mine, m], entry)
                chain_copy(m).start()

    zone_ticks, join_tick, cells = 8, 5, blocks * parts
    chain_tick = 14 + 12 * place + jnp.where(second, 0, 12)

    def due(m):
        return zone_ticks * (m // PER) + chain_tick + lax.rem(m, PER)

    def tick(t, least, joins):
        def run(late, allowed, do):
            m = PER * (late // zone_ticks) + lax.rem(late, zone_ticks)

            @pl.when(allowed & (late >= 0) & (lax.rem(late, zone_ticks) < PER) & (m >= least) & (m < messages))
            def _():
                do(m)

        if joins:
            run(t - join_tick, jnp.logical_not(second), join_step)
        run(t - chain_tick, True, chain_step)

    inputs[2].wait()
    inputs[3].wait()

    @pl.loop(0, parts)
    def _(c):
        at_w = pl.ds(pl.multiple_of(c * CHUNK, CHUNK), CHUNK)

        zero = jnp.zeros((SPAN, CHUNK), F32)
        loc[0, 0, :, at_w] = zero
        loc[1, 0, :, at_w] = zero
        loc[2, blocks, :, at_w] = zero
        loc[3, blocks, :, at_w] = zero

        def products(k, dot_xy):
            n = blocks - 1 - k
            at_k = pl.ds(pl.multiple_of(k * SPAN, SPAN), SPAN)
            at_n = pl.ds(pl.multiple_of(n * SPAN, SPAN), SPAN)
            x = x_ref[at_k, at_w].astype(F32)
            y = y_ref[at_k, at_w].astype(F32)
            turn[k * parts + c] = y.T.astype(BF16)
            wides = mm(wcol[k], spread[c, :, 2 * CHUNK :])
            xf = jnp.concatenate(pieces(wides[:, CHUNK:] * x), axis=0)
            yr = jnp.concatenate(pieces(wides[:, :CHUNK] * y), axis=0)
            fade_f = fades[c, 0, pl.ds(k, 1), :]
            fade_r = fades[c, 1, pl.ds(k, 1), :]
            loc[0, k + 1, :, at_w] = fade_f * loc[0, k, :, at_w] + mm(bt2[k], xf)
            loc[1, k + 1, :, at_w] = fade_r * loc[1, k, :, at_w] + mm(ct2[k], yr)
            wides = mm(wcol[n], spread[c, :, : 2 * CHUNK])
            yf = jnp.concatenate(pieces(wides[:, :CHUNK] * y_ref[at_n, at_w].astype(F32)), axis=0)
            xr = jnp.concatenate(pieces(wides[:, CHUNK:] * x_ref[at_n, at_w].astype(F32)), axis=0)
            fade_f = fades[c, 0, pl.ds(n, 1), :]
            fade_r = fades[c, 1, pl.ds(n, 1), :]
            loc[2, n, :, at_w] = fade_f * loc[2, n + 1, :, at_w] + mm(ct2[n], yf)
            loc[3, n, :, at_w] = fade_r * loc[3, n + 1, :, at_w] + mm(bt2[n], xr)
            return dot_xy + jnp.sum((x * y).reshape(SPAN // 8, 8, CHUNK), axis=0)

        dot_xy = lax.fori_loop(0, blocks, products, jnp.zeros((8, CHUNK), F32), unroll=8)

        dot_row = jnp.sum(dot_xy, axis=0, keepdims=True)
        coarse = jnp.round(dot_row * top) * (1.0 / top)
        rest = dot_row - coarse
        middle = jnp.round(rest * fine) * (1.0 / fine)
        small = jnp.round((rest - middle) * finest) * (1.0 / finest)

        def put(flow, comp, value, g):
            tail = jnp.where(
                one_row == 0, g,
                jnp.where(one_row == 1, coarse, jnp.where(one_row == 2, middle, jnp.where(one_row == 3, small, 0.0))),
            )
            for j in range(CHUNK // PIECE):
                m = c * PER + comp * (CHUNK // PIECE) + j
                zone[flow, m, 0:SPAN, :] = value[:, j * PIECE : (j + 1) * PIECE]
                zone[flow, m, SPAN:, :] = tail[:, j * PIECE : (j + 1) * PIECE]

        put(0, 0, loc[0, blocks, :, at_w], whole[c, 0])
        put(0, 1, loc[1, blocks, :, at_w], whole[c, 1])
        put(1, 0, loc[2, 0, :, at_w], whole[c, 0])
        put(1, 1, loc[3, 0, :, at_w], whole[c, 1])
        for j in range(PER):
            zone_copy(PER * c + j).start()

        @pl.loop(0, zone_ticks)
        def _(t):
            tick(zone_ticks * c + t, 0, True)

    low = t_pos > s_pos
    diag = t_pos == s_pos
    half = iota((SPAN, SPAN), 1) < size

    def inner(i):
        c, k = i // blocks, lax.rem(i, blocks)
        at_r = pl.ds(pl.multiple_of(k * SPAN, SPAN), SPAN)
        g = gmat[k]
        col = cols[k * parts + c]
        row = rowp[k * parts + c]
        d_sum = jnp.zeros((SPAN, SPAN), F32)
        left = jnp.zeros((SPAN, SPAN), F32)
        lows, diags = [], []
        for p in range(CHUNK // SPAN):
            at_w = pl.ds(pl.multiple_of(c * CHUNK + p * SPAN, SPAN), SPAN)
            x, y = x_ref[at_r, at_w], y_ref[at_r, at_w]
            tall, wide = [], []
            firsts = jnp.where(half, y.astype(F32), 0.0).astype(BF16)
            seconds = jnp.where(half, 0.0, y.astype(F32)).astype(BF16)
            crossed = mm(jnp.concatenate([firsts, seconds], axis=0), x, NT)
            for q in range(SPAN // size):
                h = p * (SPAN // size) + q
                fall = col[:, h : h + 1] - row[h : h + 1]
                rise = col[:, hp + h : hp + h + 1] - row[hp + h : hp + h + 1]
                mid = row[2 * hp + h : 2 * hp + h + 1]
                w = jnp.exp2(jnp.where(low, fall, jnp.where(diag, mid, rise)))
                cross = crossed[q * SPAN : (q + 1) * SPAN]
                wg = w * g
                d_sum = d_sum + cross * w
                pull = jnp.where(low, cross * wg, 0.0)
                lows.append(jnp.sum(pull, axis=0, keepdims=True))
                left = jnp.where(lane == c * hp + h, jnp.sum(pull, axis=1, keepdims=True), left)
                diags.append(jnp.sum(jnp.where(diag, cross, 0.0), axis=0, keepdims=True))
                w_h, w_l = pieces(wg)
                tall.append(jnp.concatenate([w_h, w_l], axis=1))
                y_t = turn[k * parts + c, h * size : (h + 1) * size, :]
                ix[k * parts + c, h * size : (h + 1) * size, :] = mm(
                    jnp.concatenate([y_t, y_t], axis=1), jnp.concatenate([w_h, w_l], axis=0)
                )
            both_y = mm(jnp.concatenate(tall, axis=0), jnp.concatenate([x, x], axis=0))
            iy[k * parts + c, :, p * SPAN : (p + 1) * SPAN] = jnp.where(half, both_y[:SPAN], both_y[SPAN:])
        dmat[k] += d_sum
        csum[k * parts + c] = jnp.concatenate(lows + diags, axis=0)
        rsum[k] += left

    first_tick = zone_ticks * parts

    @pl.loop(0, cells // 2)
    def _(i):
        for j in range(2):
            inner(2 * i + j)
        for j in range(2):
            tick(first_tick + 2 * i + j, 0, True)

    def side(array, flow, c, comp, low_row, high_row):
        m = PER * c + comp * (CHUNK // PIECE)
        return jnp.concatenate([array[flow, m + j, low_row:high_row, :] for j in range(CHUNK // PIECE)], axis=1)

    head_row = iota((8, CHUNK), 0) == iota((8, CHUNK), 1) // size
    pick = head_row.astype(F32)

    @pl.loop(0, parts)
    def _(c):
        at_w = pl.ds(pl.multiple_of(c * CHUNK, CHUNK), CHUNK)
        began = first_tick + cells + blocks * c
        for j in range(PER):
            m = PER * c + j

            @pl.when(due(m) >= began)
            def _():
                chain_step(m)

        for j in range(PER):
            m = PER * c + j

            @pl.when(alone)
            def _():
                ent[1 - mine, m] = jnp.zeros((wide_rows, PIECE), F32)

            @pl.when(jnp.logical_not(alone))
            def _():
                give(m).wait_recv()

        def finish(k):
            at_r = pl.ds(pl.multiple_of(k * SPAN, SPAN), SPAN)
            at = k * parts + c
            x = x_ref[at_r, at_w].astype(F32)
            y = y_ref[at_r, at_w].astype(F32)
            wides = mm(wcol[k], spread[c])
            ef_w, wr_w = wides[:, :CHUNK], wides[:, CHUNK : 2 * CHUNK]
            er_w, wf_w = wides[:, 2 * CHUNK : 3 * CHUNK], wides[:, 3 * CHUNK :]

            def entered(slot, row, flow, comp):
                return pieces(
                    loc[slot, k + flow, :, at_w] + wts[c, row, pl.ds(k, 1), :] * side(ent, flow, c, comp, 0, SPAN)
                )

            sf_h, sf_l = entered(0, 0, 0, 0)
            ar_h, ar_l = entered(1, 1, 0, 1)
            af_h, af_l = entered(2, 2, 1, 0)
            sr_h, sr_l = entered(3, 3, 1, 1)
            cat = lambda *v: jnp.concatenate(v, axis=0)
            v_f = mm(cc2[k], cat(sf_h, sf_l))
            v_r = mm(cc2[k], cat(sr_h, sr_l))
            u_f = mm(bb2[k], cat(af_h, af_l))
            u_r = mm(bb2[k], cat(ar_h, ar_l))
            gain = gwide[c, 0:1]
            yf, yr, xf, xr = ef_w * y, er_w * y, wf_w * x, wr_w * x
            mixed = iy[at] + ef_w * v_f + er_w * v_r + gain * x
            grad_x = ix[at].T + wf_w * u_f + wr_w * u_r + gain * y
            out_ref[at_r, at_w] = mixed.astype(BF16)
            gx_ref[at_r, at_w] = grad_x.astype(BF16)

            def joined(a, ah_al, b, bh_bl):
                a_h, a_l = pieces(a)
                b_h, b_l = pieces(b)
                left = jnp.concatenate([a_h, a_h, a_l, b_h, b_h, b_l], axis=1)
                right = jnp.concatenate(
                    [ah_al[0], ah_al[1], ah_al[0], bh_bl[0], bh_bl[1], bh_bl[0]], axis=1
                )
                return mm(left, right, NT)

            gca[k] += joined(yf, (sf_h, sf_l), yr, (sr_h, sr_l))
            gba[k] += joined(xf, (af_h, af_l), xr, (ar_h, ar_l))

            def narrow(v):
                turned = v.T
                return jnp.concatenate(
                    [jnp.sum(turned[j * size : (j + 1) * size], axis=0, keepdims=True) for j in range(hp)], axis=0
                )

            psum[at, 0:hp] = narrow(yf * v_f)
            psum[at, hp : 2 * hp] = narrow(xf * u_f)
            psum[at, 2 * hp : 3 * hp] = narrow(y * mixed)
            psum[at, 3 * hp : 4 * hp] = narrow(x * grad_x)

        @pl.loop(0, blocks // 4)
        def _(i):
            for j in range(4):
                finish(4 * i + j)
            for j in range(4):
                tick(began + 4 * i + j, PER * c + PER, False)

    def gathered(make):
        out = []
        for k in range(blocks):
            for c in range(parts):
                out.append(make(k, c))
        return jnp.concatenate(out, axis=0)

    def sums(first_row):
        return gathered(lambda k, c: psum[k * parts + c, first_row : first_row + hp])

    row_low = stacked(lambda k: rsum[k].T[0:heads])
    col_low = gathered(lambda k, c: csum[k * parts + c, 0:hp])
    both = gathered(lambda k, c: csum[k * parts + c, hp : 2 * hp])
    center = stacked(
        lambda k: jnp.broadcast_to(
            jnp.sum(jnp.where(diag, gmat[k], 0.0), axis=0, keepdims=True), (heads, SPAN)
        )
    )
    ends_f, ends_r, gains = [], [], []
    for c in range(parts):
        for flow, comp, opp_flow, opp_comp, into in ((0, 0, 1, 0, ends_f), (1, 1, 0, 1, ends_r)):
            own = side(zone, flow, c, comp, 0, SPAN)
            faded = side(zone, flow, c, comp, SPAN, wide_rows)[:1] * side(ent, flow, c, comp, 0, SPAN)
            held = exact(pick, (own + faded) * side(ent, opp_flow, c, opp_comp, 0, SPAN), NT)
            into.append(jnp.sum(held, axis=1, keepdims=True)[0:hp])
        total = side(ent, 0, c, 0, SPAN, wide_rows) + (
            side(zone, 0, c, 0, SPAN, wide_rows) + side(ent, 1, c, 0, SPAN, wide_rows)
        )
        row = total[1:2] + (total[2:3] + total[3:4])
        spots = (iota((CHUNK, heads), 1) == c * hp + iota((CHUNK, heads), 0) // size).astype(F32)
        gains.append(exact(jnp.broadcast_to(row, (8, CHUNK)), spots))
    gain_sum = sum(gains)
    gg_ref[...] = ((gain_sum + exact(gain_sum, anti)) * (1.0 / math.sqrt(rows * count * size)))[:1]

    gain_all = jnp.concatenate([gain_col] * blocks, axis=0)
    own_terms = (gain_all + (sf + sr) * center) * both
    row_f = row_low + sums(0 * hp)
    col_f = col_low + sums(hp)
    row_r = sums(2 * hp) - own_terms - row_f
    col_r = sums(3 * hp) - own_terms - col_f
    mid = center * both
    diff_f, diff_r = col_f - row_f, col_r - row_r
    tail_f = exact(diff_f, behind_sum)
    head_r = exact(diff_r, ahead_sum)
    later, earlier = [None] * blocks, [None] * blocks
    run = -jnp.concatenate(ends_f, axis=0)
    for k in range(blocks - 1, -1, -1):
        at = slice(k * heads, (k + 1) * heads)
        later[k] = run
        run = run + tail_f[at, :1]
    run = -jnp.concatenate(ends_r, axis=0)
    for k in range(blocks):
        at = slice(k * heads, (k + 1) * heads)
        earlier[k] = run
        run = run + head_r[at, SPAN - 1 :]
    drop_f = tail_f + jnp.concatenate(later, axis=0)
    drop_r = head_r + jnp.concatenate(earlier, axis=0)
    d_f = col_f / sf + mid + rates_f * drop_f
    d_r = col_r / sr + mid + rates_r * drop_r
    grad_s = d_f * slope_f + d_r * slope_r
    for k in range(blocks):
        here = slice(k * SPAN, (k + 1) * SPAN)
        gs_ref[:, here] = grad_s[k * heads : (k + 1) * heads]
        d_h, d_l = pieces(dmat[k])
        gc_ref[here, :] = (gca[k] + mm(jnp.concatenate([d_h, d_l], axis=1), jnp.concatenate([b_ref[here, :]] * 2, axis=0))).astype(BF16)
        gb_ref[here, :] = (gba[k] + mm(jnp.concatenate([d_h, d_l], axis=0), jnp.concatenate([c_ref[here, :]] * 2, axis=0), TN)).astype(BF16)

    @pl.loop(0, messages)
    def _(m):
        zone_copy(m).wait_send()

        @pl.when(second)
        def _():
            give(m).wait_send()

            @pl.when(jnp.logical_not(first))
            def _():
                mate_copy(m).wait_send()

            @pl.when(jnp.logical_not(last))
            def _():
                chain_copy(m).wait_send()

        @pl.when(jnp.logical_not(second))
        def _():
            pair_copy(m).wait_send()

            @pl.when(jnp.logical_not(first))
            def _():
                pass_on(m).wait_send()


def write_out(*refs):
    sems = refs[-1]
    copies = [pltpu.make_async_copy(refs[i], refs[6 + i], sems.at[i]) for i in range(6)]
    for copy in copies:
        copy.start()
    for copy in copies:
        copy.wait()


def heads_per(dims):
    return dims[0] // dims[3]


def grid_bits(dims):
    limit = 120 * dims[2] * SPAN * dims[1]
    return 23 - math.ceil(math.log2(limit))


def per_device(
    features, write_map, read_map, step_raw, tokens, base_shift, decay_rate, skip_gain, cotangent
):
    rows, width = features.shape
    state = write_map.shape[1]
    heads = decay_rate.shape[0]
    count = lax.axis_size("ctx")
    blocks, parts = rows // SPAN, width // CHUNK
    messages = PER * parts
    dims = (heads, count, blocks, parts, messages)
    hp = heads // parts
    cells = blocks * parts
    wide_rows = SPAN + EXTRA
    vmem = pl.BlockSpec(memory_space=pltpu.VMEM)
    results = (
        ((rows, width), BF16),
        ((rows, width), BF16),
        ((rows, state), BF16),
        ((rows, state), BF16),
        ((heads, rows), F32),
        ((1, heads), F32),
    )
    outs = pl.pallas_call(
        functools.partial(kernel, dims),
        out_shape=tuple(pltpu.VMEM(dims_of, kind) for dims_of, kind in results),
        in_specs=[pl.BlockSpec(memory_space=pl.ANY)] * 4 + [vmem] * 5,
        out_specs=(vmem,) * 6,
        scratch_shapes=[
            pltpu.VMEM((cells, 4 * hp, SPAN), F32),
            pltpu.VMEM((cells, SPAN, SPAN), F32),
            pltpu.VMEM((blocks, SPAN, SPAN), BF16),
            pltpu.VMEM((parts, SPAN, 4 * CHUNK), BF16),
            pltpu.VMEM((blocks, SPAN, 2 * SPAN), BF16),
            pltpu.VMEM((blocks, SPAN, 2 * SPAN), BF16),
            pltpu.VMEM((blocks, SPAN, 2 * SPAN), BF16),
            pltpu.VMEM((blocks, SPAN, 2 * SPAN), BF16),
            pltpu.VMEM((blocks, SPAN, SPAN), F32),
            pltpu.VMEM((blocks, SPAN, SPAN), F32),
            pltpu.VMEM((parts, 8, CHUNK), F32),
            pltpu.VMEM((parts, 2, blocks, CHUNK), F32),
            pltpu.VMEM((parts, 4, blocks, CHUNK), F32),
            pltpu.VMEM((parts, 2, EXTRA, CHUNK), F32),
            pltpu.VMEM((cells, CHUNK, SPAN), BF16),
            pltpu.VMEM((4, blocks + 1, SPAN, width), F32),
            pltpu.VMEM((cells, SPAN, CHUNK), F32),
            pltpu.VMEM((cells, CHUNK, SPAN), F32),
            pltpu.VMEM((blocks, SPAN, SPAN), F32),
            pltpu.VMEM((blocks, SPAN, SPAN), F32),
            pltpu.VMEM((cells, 2 * hp, SPAN), F32),
            pltpu.VMEM((blocks, SPAN, SPAN), F32),
            pltpu.VMEM((cells, 4 * hp, SPAN), F32),
            pltpu.VMEM((2, messages, wide_rows, PIECE), F32),
            pltpu.VMEM((messages, wide_rows, PIECE), F32),
            pltpu.VMEM((messages, wide_rows, PIECE), F32),
            pltpu.VMEM((messages, wide_rows, PIECE), F32),
            pltpu.VMEM((2, messages, wide_rows, PIECE), F32),
            pltpu.VMEM((messages, wide_rows, PIECE), F32),
            pltpu.VMEM((messages, wide_rows, PIECE), F32),
            pltpu.VMEM((rows, width), BF16),
            pltpu.VMEM((rows, width), BF16),
            pltpu.VMEM((rows, state), BF16),
            pltpu.VMEM((rows, state), BF16),
            pltpu.SemaphoreType.DMA((4,)),
        ]
        + [pltpu.SemaphoreType.DMA((messages,))] * 9,
        compiler_params=pltpu.CompilerParams(
            collective_id=0, has_side_effects=True, vmem_limit_bytes=58 * 1024 * 1024
        ),
    )(
        features, cotangent, write_map, read_map, step_raw.T, tokens.reshape(blocks, SPAN),
        base_shift, decay_rate.reshape(1, heads), skip_gain.reshape(1, heads),
    )
    anywhere = pl.BlockSpec(memory_space=pl.ANY)
    mixed, grad_x, grad_b, grad_c, grad_s, gains = pl.pallas_call(
        write_out,
        out_shape=tuple(jax.ShapeDtypeStruct(dims_of, kind) for dims_of, kind in results),
        in_specs=[anywhere] * 6,
        out_specs=(anywhere,) * 6,
        scratch_shapes=[pltpu.SemaphoreType.DMA((6,))],
        compiler_params=pltpu.CompilerParams(vmem_limit_bytes=1024 * 1024),
    )(*outs)
    return mixed, grad_x, grad_b, grad_c, grad_s.T, gains.reshape(heads)


def solution(mesh):
    split = P(("groups", "ctx"), None)
    return jax.shard_map(
        per_device,
        mesh=mesh,
        in_specs=(split, split, split, split, P(("groups", "ctx")), P(), P(), P(), split),
        out_specs=(split, split, split, split, split, P("groups")),
        check_vma=False,
    )
```

```python
import functools
import math

import jax
import jax.numpy as jnp
from jax import lax
from jax.experimental import pallas as pl
from jax.experimental.pallas import tpu as pltpu
from jax.sharding import PartitionSpec as P

F32 = jnp.float32
BF16 = jnp.bfloat16
EXACT = lax.Precision.HIGHEST
SPAN = 128
CHUNK = 256
EXTRA = 8
PIECE = 128
PER = 2 * CHUNK // PIECE
LOG2E = 1.4426950408889634
MESH = pl.DeviceIdType.MESH

NN = (((1,), (0,)), ((), ()))
NT = (((1,), (1,)), ((), ()))
TN = (((0,), (0,)), ((), ()))


def mm(a, b, dims=NN):
    return lax.dot_general(a, b, dims, preferred_element_type=F32)


def exact(a, b, dims=NN):
    return lax.dot_general(a, b, dims, precision=EXACT, preferred_element_type=F32)


def pieces(v):
    high = v.astype(BF16)
    return high, (v - high.astype(F32)).astype(BF16)


def iota(shape, dim):
    return lax.broadcasted_iota(jnp.int32, shape, dim)


def log1p_unit(z):
    s = z / (z + 2.0)
    q = s * s
    acc = jnp.full_like(q, 1.0 / 19.0)
    for k in range(8, -1, -1):
        acc = acc * q + 1.0 / (2 * k + 1)
    return 2.0 * s * acc


def kernel(
    dims,
    x_hbm, y_hbm, b_hbm, c_hbm, raw_ref, tok_ref, base_ref, rate_ref, gain_ref,
    out_ref, gx_ref, gb_ref, gc_ref, gs_ref, gg_ref,
    rowp, cols, wcol, spread, bt2, ct2, bb2, cc2, gmat, dmat, gwide, fades, wts, whole, turn,
    loc, iy, ix, gca, gba, csum, rsum, psum,
    zone, zsib, ein, eout, ent, zpair, esib, x_ref, y_ref, b_ref, c_ref, in_sems,
    zs_send, zs_recv, ch_send, ch_recv, ot_send, ot_recv, zp_send, zp_recv, mt_send,
):
    heads, count, blocks, parts, messages = dims
    size = CHUNK // heads_per(dims)
    hp = heads_per(dims)
    rows = blocks * SPAN
    width = parts * CHUNK
    wide_rows = SPAN + EXTRA

    group = lax.axis_index("groups")
    me = lax.axis_index("ctx")
    core = lax.rem(me, 2)
    chip = me // 2
    chips = count // 2
    mine = 1 - core
    step = 2 * core - 1
    odd = lax.rem(chip, 2)
    second = odd == core
    pairs = chips // 2
    place = jnp.where(core == 1, chip // 2, pairs - 1 - chip // 2)
    first, last = place == 0, place == pairs - 1
    sibling = me + 1 - 2 * core
    mate = me + 2 - 4 * odd
    after = jnp.clip(me + 4 * step, 0, count - 1)
    before = jnp.clip(me - 4 * step, 0, count - 1)
    has_after = second & jnp.logical_not(last)
    has_before = second & jnp.logical_not(first)
    alone = second & last

    inputs = [
        pltpu.make_async_copy(source, target, in_sems.at[i])
        for i, (source, target) in enumerate(
            ((b_hbm, b_ref), (c_hbm, c_ref), (x_hbm, x_ref), (y_hbm, y_ref))
        )
    ]
    for copy in inputs:
        copy.start()

    barrier = pltpu.get_barrier_semaphore()
    pl.semaphore_signal(barrier, inc=1, device_id=(group, sibling), device_id_type=MESH)
    pl.semaphore_signal(barrier, inc=1, device_id=(group, mate), device_id_type=MESH)

    @pl.when(has_after)
    def _():
        pl.semaphore_signal(barrier, inc=1, device_id=(group, after), device_id_type=MESH)

    @pl.when(has_before)
    def _():
        pl.semaphore_signal(barrier, inc=1, device_id=(group, before), device_id_type=MESH)

    pl.semaphore_wait(barrier, 2 + has_after.astype(jnp.int32) + has_before.astype(jnp.int32))

    eye = (iota((heads, heads), 0) == iota((heads, heads), 1)).astype(F32)
    anti = (iota((heads, heads), 0) + iota((heads, heads), 1) == heads - 1).astype(F32)
    raw_t = raw_ref[...]
    base_f = exact(eye, base_ref[...], NT)
    base_r = exact(anti, base_ref[...], NT)
    rate_f = exact(eye, jnp.broadcast_to(rate_ref[...], (8, heads)), NT)[:, :1]
    rate_r = exact(anti, jnp.broadcast_to(rate_ref[...], (8, heads)), NT)[:, :1]
    gain_row = gain_ref[...] + exact(jnp.broadcast_to(gain_ref[...], (8, heads)), anti)[:1]
    gain_col = exact(eye, jnp.broadcast_to(gain_row, (8, heads)), NT)[:, :1]

    def stacked(make):
        return jnp.concatenate([make(k) for k in range(blocks)], axis=0)

    def logits(k, base, pair):
        tok = tok_ref[k : k + 1, :]
        value = raw_t[:, k * SPAN : (k + 1) * SPAN]
        for code in range(5):
            col = pair[code]
            value = value + jnp.where(tok == code, base[:, col : col + 1], 0.0)
        return value

    vf = stacked(lambda k: logits(k, base_f, (0, 1, 2, 3, 4)))
    vr = stacked(lambda k: logits(k, base_r, (3, 2, 1, 0, 4)))

    def steps_of(v):
        z = jnp.exp(-jnp.abs(v))
        s = jnp.maximum(v, 0.0) + log1p_unit(z)
        inv = 1.0 / (1.0 + z)
        return s, jnp.where(v >= 0.0, inv, z * inv)

    sf, slope_f = steps_of(vf)
    sr, slope_r = steps_of(vr)
    rates_f = jnp.concatenate([rate_f] * blocks, axis=0)
    rates_r = jnp.concatenate([rate_r] * blocks, axis=0)
    t_pos = iota((SPAN, SPAN), 0)
    s_pos = iota((SPAN, SPAN), 1)
    ahead_sum = (t_pos <= s_pos).astype(F32)
    behind_sum = (t_pos >= s_pos).astype(F32)
    nf = exact(sf * (rates_f * -LOG2E), ahead_sum)
    nr = exact(sr * (rates_r * -LOG2E), behind_sum)
    end_f, end_r = nf[:, SPAN - 1 :], nr[:, :1]
    ef, er = jnp.exp2(nf), jnp.exp2(nr)
    wf, wr = jnp.exp2(end_f - nf) * sf, jnp.exp2(end_r - nr) * sr
    mf, mr = nf - jnp.log2(sf), nr - jnp.log2(sr)
    both_log = jnp.log2(sf + sr)

    lane = iota((SPAN, SPAN), 1)
    ends_at_last, ends_at_first = [], []
    inputs[0].wait()
    inputs[1].wait()
    for k in range(blocks):
        at = slice(k * heads, (k + 1) * heads)
        four = jnp.concatenate([ef[at], wr[at], er[at], wf[at]] * 2, axis=0)
        turned = four.T
        high, low = pieces(turned)
        joint = jnp.where(lane < 4 * heads, high.astype(F32), low.astype(F32))
        wcol[k] = joint.astype(BF16)
        ends_at_last.append(joint[SPAN - 1 :])
        ends_at_first.append(joint[:1])
        order = []
        for c in range(parts):
            sub = slice(k * heads + c * hp, k * heads + (c + 1) * hp)
            order += [nf[sub], nr[sub]]
            rowp[k * parts + c] = jnp.concatenate([mf[sub], mr[sub], both_log[sub], both_log[sub]], axis=0)
        pad = [jnp.zeros((SPAN - 2 * heads, SPAN), F32)]
        turned = jnp.concatenate(order + pad, axis=0).T
        for c in range(parts):
            cols[k * parts + c, :, 0 : 2 * hp] = turned[:, 2 * hp * c : 2 * hp * (c + 1)]
        here = slice(k * SPAN, (k + 1) * SPAN)
        bk, ck = b_ref[here, :], c_ref[here, :]
        bkt, ckt = bk.T, ck.T
        bt2[k] = jnp.concatenate([bkt, bkt], axis=1)
        ct2[k] = jnp.concatenate([ckt, ckt], axis=1)
        bb2[k] = jnp.concatenate([bk, bk], axis=1)
        cc2[k] = jnp.concatenate([ck, ck], axis=1)
        gmat[k] = mm(ck, bk, NT)
        dmat[k] = jnp.zeros((SPAN, SPAN), F32)
        gca[k] = jnp.zeros((SPAN, SPAN), F32)
        gba[k] = jnp.zeros((SPAN, SPAN), F32)
        rsum[k] = jnp.zeros((SPAN, SPAN), F32)

    for c in range(parts):
        r = iota((SPAN, 4 * CHUNK), 0)
        j = iota((SPAN, 4 * CHUNK), 1)
        rr = lax.rem(r, 4 * heads)
        hit = (rr // heads == j // CHUNK) & (lax.rem(rr, heads) == c * hp + lax.rem(j, CHUNK) // size)
        spread[c] = hit.astype(F32).astype(BF16)
        hw = iota((heads, CHUNK), 0) == c * hp + iota((heads, CHUNK), 1) // size
        gwide[c] = exact(jnp.broadcast_to(gain_row, (8, heads)), hw.astype(F32))
        fade_f = mm(jnp.concatenate(ends_at_last, axis=0).astype(BF16), spread[c, :, :CHUNK])
        fade_r = mm(jnp.concatenate(ends_at_first, axis=0).astype(BF16), spread[c, :, 2 * CHUNK : 3 * CHUNK])
        fades[c, 0], fades[c, 1] = fade_f, fade_r
        for row, fade in ((0, fade_f), (1, fade_r)):
            run = jnp.ones((1, CHUNK), F32)
            for k in range(blocks):
                wts[c, row, k : k + 1, :] = run
                run = run * fade[k : k + 1]
            whole[c, row] = jnp.broadcast_to(run, (EXTRA, CHUNK))
            run = jnp.ones((1, CHUNK), F32)
            for k in range(blocks - 1, -1, -1):
                wts[c, row + 2, k : k + 1, :] = run
                run = run * fade[k : k + 1]

    def zone_copy(m):
        return pltpu.make_async_remote_copy(
            src_ref=zone.at[1 - mine, m], dst_ref=zsib.at[m],
            send_sem=zs_send.at[m], recv_sem=zs_recv.at[m],
            device_id=(group, sibling), device_id_type=MESH,
        )

    def chain_copy(m):
        return pltpu.make_async_remote_copy(
            src_ref=eout.at[m], dst_ref=ein.at[m],
            send_sem=ch_send.at[m], recv_sem=ch_recv.at[m],
            device_id=(group, after), device_id_type=MESH,
        )

    def remote(source, target, m, send, recv, device):
        return pltpu.make_async_remote_copy(
            src_ref=source, dst_ref=target, send_sem=send.at[m], recv_sem=recv.at[m],
            device_id=(group, device), device_id_type=MESH,
        )

    def pass_on(m):
        return remote(ein.at[m], ent.at[mine, m], m, ot_send, ot_recv, sibling)

    def give(m):
        return remote(esib.at[m], ent.at[mine, m], m, ot_send, ot_recv, sibling)

    def pair_copy(m):
        return remote(eout.at[m], zpair.at[m], m, zp_send, zp_recv, mate)

    def mate_copy(m):
        return remote(ein.at[m], ein.at[m], m, mt_send, ch_recv, mate)

    top, fine = 2.0 ** grid_bits(dims), 2.0 ** (grid_bits(dims) + 21)
    finest = 2.0 ** (grid_bits(dims) + 42)
    one_row = iota((EXTRA, CHUNK), 0)

    is_state = iota((wide_rows, PIECE), 0) < SPAN

    def over(near, value):
        return near + jnp.where(is_state, near[SPAN : SPAN + 1], 1.0) * value

    def join_step(m):
        zone_copy(m).wait_recv()
        near, own = zsib[m], zone[mine, m]
        eout[m] = over(own, near)
        eout[m, SPAN : SPAN + 1, :] = own[SPAN : SPAN + 1] * near[SPAN : SPAN + 1]
        pair_copy(m).start()

    def chain_step(m):
        @pl.when(first)
        def _():
            ein[m] = jnp.zeros((wide_rows, PIECE), F32)

        @pl.when(jnp.logical_not(first))
        def _():
            chain_copy(m).wait_recv()

        @pl.when(jnp.logical_not(second))
        def _():
            @pl.when(jnp.logical_not(first))
            def _():
                pass_on(m).start()

            ent[mine, m] = over(zsib[m], ein[m])

        @pl.when(second)
        def _():
            @pl.when(jnp.logical_not(first))
            def _():
                mate_copy(m).start()

            zone_copy(m).wait_recv()
            pair_copy(m).wait_recv()
            theirs = over(zpair[m], ein[m])
            esib[m] = theirs
            give(m).start()
            entry = over(zsib[m], theirs)
            ent[mine, m] = entry

            @pl.when(jnp.logical_not(last))
            def _():
                eout[m] = over(zone[mine, m], entry)
                chain_copy(m).start()

    zone_ticks, join_tick, cells = 8, 5, blocks * parts
    chain_tick = 14 + 12 * place + jnp.where(second, 0, 12)

    def due(m):
        return zone_ticks * (m // PER) + chain_tick + lax.rem(m, PER)

    def tick(t, least, joins):
        def run(late, allowed, do):
            m = PER * (late // zone_ticks) + lax.rem(late, zone_ticks)

            @pl.when(allowed & (late >= 0) & (lax.rem(late, zone_ticks) < PER) & (m >= least) & (m < messages))
            def _():
                do(m)

        if joins:
            run(t - join_tick, jnp.logical_not(second), join_step)
        run(t - chain_tick, True, chain_step)

    inputs[2].wait()
    inputs[3].wait()

    @pl.loop(0, parts)
    def _(c):
        at_w = pl.ds(pl.multiple_of(c * CHUNK, CHUNK), CHUNK)

        zero = jnp.zeros((SPAN, CHUNK), F32)
        loc[0, 0, :, at_w] = zero
        loc[1, 0, :, at_w] = zero
        loc[2, blocks, :, at_w] = zero
        loc[3, blocks, :, at_w] = zero

        def products(k, dot_xy):
            n = blocks - 1 - k
            at_k = pl.ds(pl.multiple_of(k * SPAN, SPAN), SPAN)
            at_n = pl.ds(pl.multiple_of(n * SPAN, SPAN), SPAN)
            x = x_ref[at_k, at_w].astype(F32)
            y = y_ref[at_k, at_w].astype(F32)
            turn[k * parts + c] = y.T.astype(BF16)
            wides = mm(wcol[k], spread[c, :, 2 * CHUNK :])
            xf = jnp.concatenate(pieces(wides[:, CHUNK:] * x), axis=0)
            yr = jnp.concatenate(pieces(wides[:, :CHUNK] * y), axis=0)
            fade_f = fades[c, 0, pl.ds(k, 1), :]
            fade_r = fades[c, 1, pl.ds(k, 1), :]
            loc[0, k + 1, :, at_w] = fade_f * loc[0, k, :, at_w] + mm(bt2[k], xf)
            loc[1, k + 1, :, at_w] = fade_r * loc[1, k, :, at_w] + mm(ct2[k], yr)
            wides = mm(wcol[n], spread[c, :, : 2 * CHUNK])
            yf = jnp.concatenate(pieces(wides[:, :CHUNK] * y_ref[at_n, at_w].astype(F32)), axis=0)
            xr = jnp.concatenate(pieces(wides[:, CHUNK:] * x_ref[at_n, at_w].astype(F32)), axis=0)
            fade_f = fades[c, 0, pl.ds(n, 1), :]
            fade_r = fades[c, 1, pl.ds(n, 1), :]
            loc[2, n, :, at_w] = fade_f * loc[2, n + 1, :, at_w] + mm(ct2[n], yf)
            loc[3, n, :, at_w] = fade_r * loc[3, n + 1, :, at_w] + mm(bt2[n], xr)
            return dot_xy + jnp.sum((x * y).reshape(SPAN // 8, 8, CHUNK), axis=0)

        dot_xy = lax.fori_loop(0, blocks, products, jnp.zeros((8, CHUNK), F32), unroll=8)

        dot_row = jnp.sum(dot_xy, axis=0, keepdims=True)
        coarse = jnp.round(dot_row * top) * (1.0 / top)
        rest = dot_row - coarse
        middle = jnp.round(rest * fine) * (1.0 / fine)
        small = jnp.round((rest - middle) * finest) * (1.0 / finest)

        def put(flow, comp, value, g):
            tail = jnp.where(
                one_row == 0, g,
                jnp.where(one_row == 1, coarse, jnp.where(one_row == 2, middle, jnp.where(one_row == 3, small, 0.0))),
            )
            for j in range(CHUNK // PIECE):
                m = c * PER + comp * (CHUNK // PIECE) + j
                zone[flow, m, 0:SPAN, :] = value[:, j * PIECE : (j + 1) * PIECE]
                zone[flow, m, SPAN:, :] = tail[:, j * PIECE : (j + 1) * PIECE]

        put(0, 0, loc[0, blocks, :, at_w], whole[c, 0])
        put(0, 1, loc[1, blocks, :, at_w], whole[c, 1])
        put(1, 0, loc[2, 0, :, at_w], whole[c, 0])
        put(1, 1, loc[3, 0, :, at_w], whole[c, 1])
        for j in range(PER):
            zone_copy(PER * c + j).start()

        @pl.loop(0, zone_ticks)
        def _(t):
            tick(zone_ticks * c + t, 0, True)

    low = t_pos > s_pos
    diag = t_pos == s_pos
    half = iota((SPAN, SPAN), 1) < size

    def inner(i):
        c, k = i // blocks, lax.rem(i, blocks)
        at_r = pl.ds(pl.multiple_of(k * SPAN, SPAN), SPAN)
        g = gmat[k]
        col = cols[k * parts + c]
        row = rowp[k * parts + c]
        d_sum = jnp.zeros((SPAN, SPAN), F32)
        left = jnp.zeros((SPAN, SPAN), F32)
        lows, diags = [], []
        for p in range(CHUNK // SPAN):
            at_w = pl.ds(pl.multiple_of(c * CHUNK + p * SPAN, SPAN), SPAN)
            x, y = x_ref[at_r, at_w], y_ref[at_r, at_w]
            tall, wide = [], []
            firsts = jnp.where(half, y.astype(F32), 0.0).astype(BF16)
            seconds = jnp.where(half, 0.0, y.astype(F32)).astype(BF16)
            crossed = mm(jnp.concatenate([firsts, seconds], axis=0), x, NT)
            for q in range(SPAN // size):
                h = p * (SPAN // size) + q
                fall = col[:, h : h + 1] - row[h : h + 1]
                rise = col[:, hp + h : hp + h + 1] - row[hp + h : hp + h + 1]
                mid = row[2 * hp + h : 2 * hp + h + 1]
                w = jnp.exp2(jnp.where(low, fall, jnp.where(diag, mid, rise)))
                cross = crossed[q * SPAN : (q + 1) * SPAN]
                wg = w * g
                d_sum = d_sum + cross * w
                pull = jnp.where(low, cross * wg, 0.0)
                lows.append(jnp.sum(pull, axis=0, keepdims=True))
                left = jnp.where(lane == c * hp + h, jnp.sum(pull, axis=1, keepdims=True), left)
                diags.append(jnp.sum(jnp.where(diag, cross, 0.0), axis=0, keepdims=True))
                w_h, w_l = pieces(wg)
                tall.append(jnp.concatenate([w_h, w_l], axis=1))
                y_t = turn[k * parts + c, h * size : (h + 1) * size, :]
                ix[k * parts + c, h * size : (h + 1) * size, :] = mm(
                    jnp.concatenate([y_t, y_t], axis=1), jnp.concatenate([w_h, w_l], axis=0)
                )
            both_y = mm(jnp.concatenate(tall, axis=0), jnp.concatenate([x, x], axis=0))
            iy[k * parts + c, :, p * SPAN : (p + 1) * SPAN] = jnp.where(half, both_y[:SPAN], both_y[SPAN:])
        dmat[k] += d_sum
        csum[k * parts + c] = jnp.concatenate(lows + diags, axis=0)
        rsum[k] += left

    first_tick = zone_ticks * parts

    @pl.loop(0, cells // 2)
    def _(i):
        for j in range(2):
            inner(2 * i + j)
        for j in range(2):
            tick(first_tick + 2 * i + j, 0, True)

    def side(array, flow, c, comp, low_row, high_row):
        m = PER * c + comp * (CHUNK // PIECE)
        return jnp.concatenate([array[flow, m + j, low_row:high_row, :] for j in range(CHUNK // PIECE)], axis=1)

    head_row = iota((8, CHUNK), 0) == iota((8, CHUNK), 1) // size
    pick = head_row.astype(F32)

    @pl.loop(0, parts)
    def _(c):
        at_w = pl.ds(pl.multiple_of(c * CHUNK, CHUNK), CHUNK)
        began = first_tick + cells + blocks * c
        for j in range(PER):
            m = PER * c + j

            @pl.when(due(m) >= began)
            def _():
                chain_step(m)

        for j in range(PER):
            m = PER * c + j

            @pl.when(alone)
            def _():
                ent[1 - mine, m] = jnp.zeros((wide_rows, PIECE), F32)

            @pl.when(jnp.logical_not(alone))
            def _():
                give(m).wait_recv()

        def finish(k):
            at_r = pl.ds(pl.multiple_of(k * SPAN, SPAN), SPAN)
            at = k * parts + c
            x = x_ref[at_r, at_w].astype(F32)
            y = y_ref[at_r, at_w].astype(F32)
            wides = mm(wcol[k], spread[c])
            ef_w, wr_w = wides[:, :CHUNK], wides[:, CHUNK : 2 * CHUNK]
            er_w, wf_w = wides[:, 2 * CHUNK : 3 * CHUNK], wides[:, 3 * CHUNK :]

            def entered(slot, row, flow, comp):
                return pieces(
                    loc[slot, k + flow, :, at_w] + wts[c, row, pl.ds(k, 1), :] * side(ent, flow, c, comp, 0, SPAN)
                )

            sf_h, sf_l = entered(0, 0, 0, 0)
            ar_h, ar_l = entered(1, 1, 0, 1)
            af_h, af_l = entered(2, 2, 1, 0)
            sr_h, sr_l = entered(3, 3, 1, 1)
            cat = lambda *v: jnp.concatenate(v, axis=0)
            v_f = mm(cc2[k], cat(sf_h, sf_l))
            v_r = mm(cc2[k], cat(sr_h, sr_l))
            u_f = mm(bb2[k], cat(af_h, af_l))
            u_r = mm(bb2[k], cat(ar_h, ar_l))
            gain = gwide[c, 0:1]
            yf, yr, xf, xr = ef_w * y, er_w * y, wf_w * x, wr_w * x
            mixed = iy[at] + ef_w * v_f + er_w * v_r + gain * x
            grad_x = ix[at].T + wf_w * u_f + wr_w * u_r + gain * y
            out_ref[at_r, at_w] = mixed.astype(BF16)
            gx_ref[at_r, at_w] = grad_x.astype(BF16)

            def joined(a, ah_al, b, bh_bl):
                a_h, a_l = pieces(a)
                b_h, b_l = pieces(b)
                left = jnp.concatenate([a_h, a_h, a_l, b_h, b_h, b_l], axis=1)
                right = jnp.concatenate(
                    [ah_al[0], ah_al[1], ah_al[0], bh_bl[0], bh_bl[1], bh_bl[0]], axis=1
                )
                return mm(left, right, NT)

            gca[k] += joined(yf, (sf_h, sf_l), yr, (sr_h, sr_l))
            gba[k] += joined(xf, (af_h, af_l), xr, (ar_h, ar_l))

            def narrow(v):
                turned = v.T
                return jnp.concatenate(
                    [jnp.sum(turned[j * size : (j + 1) * size], axis=0, keepdims=True) for j in range(hp)], axis=0
                )

            psum[at, 0:hp] = narrow(yf * v_f)
            psum[at, hp : 2 * hp] = narrow(xf * u_f)
            psum[at, 2 * hp : 3 * hp] = narrow(y * mixed)
            psum[at, 3 * hp : 4 * hp] = narrow(x * grad_x)

        @pl.loop(0, blocks // 8)
        def _(i):
            for j in range(8):
                finish(8 * i + j)
            for j in range(8):
                tick(began + 8 * i + j, PER * c + PER, False)

    def gathered(make):
        out = []
        for k in range(blocks):
            for c in range(parts):
                out.append(make(k, c))
        return jnp.concatenate(out, axis=0)

    def sums(first_row):
        return gathered(lambda k, c: psum[k * parts + c, first_row : first_row + hp])

    row_low = stacked(lambda k: rsum[k].T[0:heads])
    col_low = gathered(lambda k, c: csum[k * parts + c, 0:hp])
    both = gathered(lambda k, c: csum[k * parts + c, hp : 2 * hp])
    center = stacked(
        lambda k: jnp.broadcast_to(
            jnp.sum(jnp.where(diag, gmat[k], 0.0), axis=0, keepdims=True), (heads, SPAN)
        )
    )
    ends_f, ends_r, gains = [], [], []
    for c in range(parts):
        for flow, comp, opp_flow, opp_comp, into in ((0, 0, 1, 0, ends_f), (1, 1, 0, 1, ends_r)):
            own = side(zone, flow, c, comp, 0, SPAN)
            faded = side(zone, flow, c, comp, SPAN, wide_rows)[:1] * side(ent, flow, c, comp, 0, SPAN)
            row = jnp.sum((own + faded) * side(ent, opp_flow, c, opp_comp, 0, SPAN), axis=0, keepdims=True)
            held = exact(pick, jnp.broadcast_to(row, (8, CHUNK)), NT)
            into.append(held[0:hp, :1])
        total = side(ent, 0, c, 0, SPAN, wide_rows) + (
            side(zone, 0, c, 0, SPAN, wide_rows) + side(ent, 1, c, 0, SPAN, wide_rows)
        )
        row = total[1:2] + (total[2:3] + total[3:4])
        spots = (iota((CHUNK, heads), 1) == c * hp + iota((CHUNK, heads), 0) // size).astype(F32)
        gains.append(exact(jnp.broadcast_to(row, (8, CHUNK)), spots))
    gain_sum = sum(gains)
    gg_ref[...] = ((gain_sum + exact(gain_sum, anti)) * (1.0 / math.sqrt(rows * count * size)))[:1]

    gain_all = jnp.concatenate([gain_col] * blocks, axis=0)
    own_terms = (gain_all + (sf + sr) * center) * both
    row_f = row_low + sums(0 * hp)
    col_f = col_low + sums(hp)
    row_r = sums(2 * hp) - own_terms - row_f
    col_r = sums(3 * hp) - own_terms - col_f
    mid = center * both
    diff_f, diff_r = col_f - row_f, col_r - row_r
    tail_f = exact(diff_f, behind_sum)
    head_r = exact(diff_r, ahead_sum)
    later, earlier = [None] * blocks, [None] * blocks
    run = -jnp.concatenate(ends_f, axis=0)
    for k in range(blocks - 1, -1, -1):
        at = slice(k * heads, (k + 1) * heads)
        later[k] = run
        run = run + tail_f[at, :1]
    run = -jnp.concatenate(ends_r, axis=0)
    for k in range(blocks):
        at = slice(k * heads, (k + 1) * heads)
        earlier[k] = run
        run = run + head_r[at, SPAN - 1 :]
    drop_f = tail_f + jnp.concatenate(later, axis=0)
    drop_r = head_r + jnp.concatenate(earlier, axis=0)
    d_f = col_f / sf + mid + rates_f * drop_f
    d_r = col_r / sr + mid + rates_r * drop_r
    grad_s = d_f * slope_f + d_r * slope_r
    for k in range(blocks):
        here = slice(k * SPAN, (k + 1) * SPAN)
        gs_ref[:, here] = grad_s[k * heads : (k + 1) * heads]
        d_h, d_l = pieces(dmat[k])
        gc_ref[here, :] = (gca[k] + mm(jnp.concatenate([d_h, d_l], axis=1), jnp.concatenate([b_ref[here, :]] * 2, axis=0))).astype(BF16)
        gb_ref[here, :] = (gba[k] + mm(jnp.concatenate([d_h, d_l], axis=0), jnp.concatenate([c_ref[here, :]] * 2, axis=0), TN)).astype(BF16)

    @pl.loop(0, messages)
    def _(m):
        zone_copy(m).wait_send()

        @pl.when(second)
        def _():
            give(m).wait_send()

            @pl.when(jnp.logical_not(first))
            def _():
                mate_copy(m).wait_send()

            @pl.when(jnp.logical_not(last))
            def _():
                chain_copy(m).wait_send()

        @pl.when(jnp.logical_not(second))
        def _():
            pair_copy(m).wait_send()

            @pl.when(jnp.logical_not(first))
            def _():
                pass_on(m).wait_send()


def write_out(*refs):
    sems = refs[-1]
    copies = [pltpu.make_async_copy(refs[i], refs[6 + i], sems.at[i]) for i in range(6)]
    for copy in copies:
        copy.start()
    for copy in copies:
        copy.wait()


def heads_per(dims):
    return dims[0] // dims[3]


def grid_bits(dims):
    limit = 120 * dims[2] * SPAN * dims[1]
    return 23 - math.ceil(math.log2(limit))


def per_device(
    features, write_map, read_map, step_raw, tokens, base_shift, decay_rate, skip_gain, cotangent
):
    rows, width = features.shape
    state = write_map.shape[1]
    heads = decay_rate.shape[0]
    count = lax.axis_size("ctx")
    blocks, parts = rows // SPAN, width // CHUNK
    messages = PER * parts
    dims = (heads, count, blocks, parts, messages)
    hp = heads // parts
    cells = blocks * parts
    wide_rows = SPAN + EXTRA
    vmem = pl.BlockSpec(memory_space=pltpu.VMEM)
    results = (
        ((rows, width), BF16),
        ((rows, width), BF16),
        ((rows, state), BF16),
        ((rows, state), BF16),
        ((heads, rows), F32),
        ((1, heads), F32),
    )
    outs = pl.pallas_call(
        functools.partial(kernel, dims),
        out_shape=tuple(pltpu.VMEM(dims_of, kind) for dims_of, kind in results),
        in_specs=[pl.BlockSpec(memory_space=pl.ANY)] * 4 + [vmem] * 5,
        out_specs=(vmem,) * 6,
        scratch_shapes=[
            pltpu.VMEM((cells, 4 * hp, SPAN), F32),
            pltpu.VMEM((cells, SPAN, SPAN), F32),
            pltpu.VMEM((blocks, SPAN, SPAN), BF16),
            pltpu.VMEM((parts, SPAN, 4 * CHUNK), BF16),
            pltpu.VMEM((blocks, SPAN, 2 * SPAN), BF16),
            pltpu.VMEM((blocks, SPAN, 2 * SPAN), BF16),
            pltpu.VMEM((blocks, SPAN, 2 * SPAN), BF16),
            pltpu.VMEM((blocks, SPAN, 2 * SPAN), BF16),
            pltpu.VMEM((blocks, SPAN, SPAN), F32),
            pltpu.VMEM((blocks, SPAN, SPAN), F32),
            pltpu.VMEM((parts, 8, CHUNK), F32),
            pltpu.VMEM((parts, 2, blocks, CHUNK), F32),
            pltpu.VMEM((parts, 4, blocks, CHUNK), F32),
            pltpu.VMEM((parts, 2, EXTRA, CHUNK), F32),
            pltpu.VMEM((cells, CHUNK, SPAN), BF16),
            pltpu.VMEM((4, blocks + 1, SPAN, width), F32),
            pltpu.VMEM((cells, SPAN, CHUNK), F32),
            pltpu.VMEM((cells, CHUNK, SPAN), F32),
            pltpu.VMEM((blocks, SPAN, SPAN), F32),
            pltpu.VMEM((blocks, SPAN, SPAN), F32),
            pltpu.VMEM((cells, 2 * hp, SPAN), F32),
            pltpu.VMEM((blocks, SPAN, SPAN), F32),
            pltpu.VMEM((cells, 4 * hp, SPAN), F32),
            pltpu.VMEM((2, messages, wide_rows, PIECE), F32),
            pltpu.VMEM((messages, wide_rows, PIECE), F32),
            pltpu.VMEM((messages, wide_rows, PIECE), F32),
            pltpu.VMEM((messages, wide_rows, PIECE), F32),
            pltpu.VMEM((2, messages, wide_rows, PIECE), F32),
            pltpu.VMEM((messages, wide_rows, PIECE), F32),
            pltpu.VMEM((messages, wide_rows, PIECE), F32),
            pltpu.VMEM((rows, width), BF16),
            pltpu.VMEM((rows, width), BF16),
            pltpu.VMEM((rows, state), BF16),
            pltpu.VMEM((rows, state), BF16),
            pltpu.SemaphoreType.DMA((4,)),
        ]
        + [pltpu.SemaphoreType.DMA((messages,))] * 9,
        compiler_params=pltpu.CompilerParams(
            collective_id=0, has_side_effects=True, vmem_limit_bytes=58 * 1024 * 1024
        ),
    )(
        features, cotangent, write_map, read_map, step_raw.T, tokens.reshape(blocks, SPAN),
        base_shift, decay_rate.reshape(1, heads), skip_gain.reshape(1, heads),
    )
    anywhere = pl.BlockSpec(memory_space=pl.ANY)
    mixed, grad_x, grad_b, grad_c, grad_s, gains = pl.pallas_call(
        write_out,
        out_shape=tuple(jax.ShapeDtypeStruct(dims_of, kind) for dims_of, kind in results),
        in_specs=[anywhere] * 6,
        out_specs=(anywhere,) * 6,
        scratch_shapes=[pltpu.SemaphoreType.DMA((6,))],
        compiler_params=pltpu.CompilerParams(vmem_limit_bytes=1024 * 1024),
    )(*outs)
    return mixed, grad_x, grad_b, grad_c, grad_s.T, gains.reshape(heads)


def solution(mesh):
    split = P(("groups", "ctx"), None)
    return jax.shard_map(
        per_device,
        mesh=mesh,
        in_specs=(split, split, split, split, P(("groups", "ctx")), P(), P(), P(), split),
        out_specs=(split, split, split, split, split, P("groups")),
        check_vma=False,
    )
```
